32 devices in a mesh: dp: 4 (over z), seq: 8 (over y, x, core).
Axes of the slice: x: 2, y: 2, z: 4, core: 2. Of those that a mesh axis runs over, the one named last changes fastest.
Arguments:
- stream: bfloat16 [8192, 768], P(('dp', 'seq')), may hold values from -6 to 6
- w_mix: bfloat16 [2, 768, 1920], P(None, ('dp', 'seq')), may hold values from -0.21875 to 0.21875
- w_out: bfloat16 [2, 768, 768], P(None, ('dp', 'seq')), may hold values from -0.21875 to 0.21875
- w_up: bfloat16 [2, 768, 3072], P(None, ('dp', 'seq')), may hold values from -0.21875 to 0.21875
- w_down: bfloat16 [2, 1536, 768], P(None, ('dp', 'seq')), may hold values from -0.15625 to 0.15625
- gains: bfloat16 [2, 3, 768], P(None, None, ('dp', 'seq')), may hold values from 0.5 to 1.5
- chan_params: bfloat16 [2, 768], P(None, ('dp', 'seq')), may hold values from -3.2 to 12, as said below
- lengths: int32 [4, 3], P('dp'), may hold values from 1 to 2045, as said below
- cotangent: bfloat16 [8192, 768], P(('dp', 'seq')), may hold values from -6 to 6
Outputs:
- mixed: bfloat16 [8192, 768], P(('dp', 'seq'))
- grad_stream: float32 [8192, 768], P(('dp', 'seq'))
- grad_w_mix: float32 [2, 768, 1920], P(None, ('dp', 'seq'))
- grad_w_out: float32 [2, 768, 768], P(None, ('dp', 'seq'))
- grad_w_up: float32 [2, 768, 3072], P(None, ('dp', 'seq'))
- grad_w_down: float32 [2, 1536, 768], P(None, ('dp', 'seq'))
- grad_gains: float32 [2, 3, 768], P(None, None, ('dp', 'seq'))
- grad_chan_params: float32 [2, 768], P(None, ('dp', 'seq'))
The draws below stay inside these ranges and needn't reach their ends.
Inputs may be any that keep to these rules, and one draw needn't show every extreme that they name: Each row's lengths fill its stream of 2048 slots but for 1 to 85 padding slots at its end; one sequence of each row is longer than 1792, each other one has at most (255) // 3 tokens. `chan_params`: per layer, the first 384 entries are forget-gate biases, the last 384 angles in radians.
All inputs are finite; a program needn't handle non-finite values.
Results may differ from the reference program's by a relative error of at most 0.017.
Values may be sent and summed in bfloat16 or wider, within the bound.
No kernel may reach another device: no remote copies, remote signals or barrier semaphores. Data moves between devices by JAX's collectives and lax.ppermute only.
A program may use at most 256 MiB of HBM per device.

```python
import math
import jax
import jax.numpy as jnp
from jax import lax

D = 768
CH = 384
FF = 1536
GN_WIDTH = 128
LAYERS = 2
SEQS = 3
TOK_DEV = 256
STREAMS = 4
GROUP_TOK = 2048
TOKENS = 8192
N_SEQ = 8


def draw_lengths(key, part):
    key_short, key_pad, key_which = jax.random.split(key, 3)
    limit = (TOK_DEV - 1) // 3
    first_row = jnp.arange(STREAMS) == 0
    shorts = jax.random.randint(key_short, (STREAMS, SEQS), 1, limit + 1)
    shorts = jnp.where(first_row[:, None], 1, shorts)
    padding = jax.random.randint(key_pad, (STREAMS,), 1, limit + 1)
    padding = jnp.where(first_row, 1, padding)
    which = jax.random.randint(key_which, (STREAMS,), 0, SEQS)
    is_long = jnp.arange(SEQS)[None, :] == which[:, None]
    others = jnp.sum(jnp.where(is_long, 0, shorts), axis=1)
    longest = GROUP_TOK - others - padding
    return jnp.where(is_long, longest[:, None], shorts).astype(jnp.int32)


def draw_chan_params(key, part):
    key_pick, key_slow, key_fast, key_angle = jax.random.split(key, 4)
    share = 0.5
    slow = jax.random.uniform(key_pick, (LAYERS, CH)) < share
    slow_low = math.log(GROUP_TOK) + 0.5
    slow_bias = slow_low + (12.0 - slow_low) * jax.random.uniform(key_slow, (LAYERS, CH), jnp.float32, 0.0, 1.0)
    slow_bias = slow_bias.at[0, 0].set(12.0)
    fast_bias = jax.random.uniform(key_fast, (LAYERS, CH), jnp.float32, 1.0, 3.2)
    bias = jnp.where(slow, slow_bias, fast_bias)
    bias = bias.at[0, 0].set(12.0)
    angle = jax.random.uniform(key_angle, (LAYERS, CH), jnp.float32, -math.pi, math.pi)
    return jnp.concatenate([bias, angle], axis=1).astype(jnp.bfloat16)


def level_of(own_key, dims, cuts, low, largest):
    factor_of, own = 1.0, jax.random.fold_in(own_key, 6)
    for axis_at, parts in cuts:
        draws = jnp.exp(jax.random.uniform(jax.random.fold_in(own, axis_at), (parts,), jnp.float32, low / len(cuts), largest / len(cuts)))
        factor_of = factor_of * jnp.repeat(draws, dims[axis_at] // parts).reshape([-1 if axis == axis_at else 1 for axis in range(len(dims))])
    return factor_of


def scatter_about(rng, extent, width, most, cuts=(), held_as=jnp.bfloat16):
    entries = width * jax.random.normal(rng, extent, jnp.float32)
    if cuts:
        entries = entries * level_of(rng, extent, cuts, -0.22, 0.18)
    return jnp.clip(entries, -most, most).astype(held_as)


def setup_inputs(seed: int = 0) -> dict:
    arg_keys = jax.random.split(jax.random.key(seed), 10)
    stream = scatter_about(arg_keys[0], (TOKENS, D), 1.0, 6.0, ((0, 32),))
    w_mix = scatter_about(arg_keys[1], (LAYERS, D, 2 * D + CH), D ** -0.5, 0.21875, ((1, 32),))
    w_out = scatter_about(arg_keys[2], (LAYERS, D, D), D ** -0.5, 0.21875, ((1, 32),))
    w_up = scatter_about(arg_keys[3], (LAYERS, D, 2 * FF), D ** -0.5, 0.21875, ((1, 32),))
    w_down = scatter_about(arg_keys[4], (LAYERS, FF, D), FF ** -0.5, 0.15625, ((1, 32),))
    gains = jnp.clip(1.0 + 0.1 * jax.random.normal(arg_keys[5], (LAYERS, 3, D), jnp.float32), 0.5, 1.5).astype(jnp.bfloat16)
    chan_params = draw_chan_params(jax.random.fold_in(arg_keys[9], 71), 0)
    lengths = draw_lengths(jax.random.fold_in(arg_keys[9], 71), 0)
    cotangent = scatter_about(arg_keys[8], (TOKENS, D), 1.0, 6.0, ((0, 32),))
    return {"stream": stream, "w_mix": w_mix, "w_out": w_out, "w_up": w_up, "w_down": w_down, "gains": gains, "chan_params": chan_params, "lengths": lengths, "cotangent": cotangent}


EPS = 1e-06

@jax.custom_vjp
def low(v):
    return lax.optimization_barrier(v.astype(jnp.bfloat16)).astype(jnp.float32)

@jax.custom_vjp
def low_back(v):
    return v

def low_keep(v):
    return (low(v), None)

def low_pass(kept, grad):
    return (grad,)

def back_keep(v):
    return (v, None)

def back_low(kept, grad):
    return (low(grad),)
low.defvjp(low_keep, low_pass)
low_back.defvjp(back_keep, back_low)

def matmul(left, right):
    return jnp.dot(left, right, precision=lax.Precision.HIGHEST)

def rms_norm(values, gain):
    return values * lax.rsqrt(lax.optimization_barrier(jnp.mean(values * values, axis=-1, keepdims=True)) + EPS) * gain

def group_norm(values, gain):
    shaped = values.reshape(values.shape[0], D // GN_WIDTH, GN_WIDTH)
    centre = shaped - lax.optimization_barrier(jnp.mean(shaped, axis=-1, keepdims=True))
    scaled = centre * lax.rsqrt(lax.optimization_barrier(jnp.mean(centre * centre, axis=-1, keepdims=True)) + EPS)
    return scaled.reshape(values.shape) * gain

def stream_masks(length_row):
    ends = jnp.cumsum(length_row)
    starts = ends - length_row
    places = jnp.arange(GROUP_TOK, dtype=jnp.int32)
    restart = jnp.any(places[:, None] == starts[None, :], axis=1).astype(jnp.float32)
    keep = (places < ends[SEQS - 1]).astype(jnp.float32)
    return (restart, keep)

def recurrence(rate, part_re, part_im, restart, angle):
    cos_t = jnp.cos(angle)
    sin_t = jnp.sin(angle)

    def block(state, pieces):

        def advance(carry, item):
            rate_now, feed_re, feed_im, fresh = item
            kept = (1.0 - fresh) * rate_now
            new_re = kept * (cos_t * carry[0] - sin_t * carry[1]) + (1.0 - rate_now) * feed_re
            new_im = kept * (sin_t * carry[0] + cos_t * carry[1]) + (1.0 - rate_now) * feed_im
            return ((new_re, new_im), jnp.concatenate([new_re, new_im]))
        return lax.scan(advance, state, pieces)
    pieces = (rate.reshape(N_SEQ, TOK_DEV, CH), part_re.reshape(N_SEQ, TOK_DEV, CH), part_im.reshape(N_SEQ, TOK_DEV, CH), restart.reshape(N_SEQ, TOK_DEV))
    start = (jnp.zeros((CH,), jnp.float32), jnp.zeros((CH,), jnp.float32))
    final, states = lax.scan(jax.checkpoint(block), start, pieces)
    return states.reshape(GROUP_TOK, D)

def layer(values, restart, weight_set, index):
    w_mix, w_out, w_up, w_down, gains, chan = weight_set
    normed = low(rms_norm(values, gains[index, 0]))
    mixin = low_back(matmul(normed, w_mix[index]))
    candidate = jax.nn.silu(mixin[:, :D])
    gate = jax.nn.sigmoid(mixin[:, D:2 * D])
    rate = jax.nn.sigmoid(mixin[:, 2 * D:] + chan[index, :CH])
    states = recurrence(rate, candidate[:, :CH], candidate[:, CH:], restart, chan[index, CH:])
    gated = low(group_norm(gate * states, gains[index, 1]))
    after = values + low_back(matmul(gated, w_out[index]))
    lifted = low(rms_norm(after, gains[index, 2]))
    both = low_back(matmul(lifted, w_up[index]))
    hidden = low(jax.nn.silu(both[:, :FF]) * both[:, FF:])
    return after + low_back(matmul(hidden, w_down[index]))

def reference(stream, w_mix, w_out, w_up, w_down, gains, chan_params, lengths, cotangent):
    weight_set = tuple((array.astype(jnp.float32) for array in (w_mix, w_out, w_up, w_down, gains, chan_params)))

    def forward(values, *weights):

        def one_group(item):
            rows_now, length_row = item
            restart, keep = stream_masks(length_row)
            for index in range(LAYERS):
                rows_now = layer(rows_now, restart, weights, index)
            return rows_now
        grouped = values.reshape(STREAMS, GROUP_TOK, D)
        return lax.map(jax.checkpoint(one_group), (grouped, lengths)).reshape(TOKENS, D)
    result, pullback = jax.vjp(forward, stream.astype(jnp.float32), *weight_set)
    keeps = jax.vmap(lambda length_row: stream_masks(length_row)[1])(lengths).reshape(TOKENS, 1)
    gradients = pullback(cotangent.astype(jnp.float32) * keeps)
    return (result.astype(jnp.bfloat16), gradients[0], gradients[1], gradients[2], gradients[3], gradients[4], gradients[5], gradients[6])
```

```python
import functools

import jax
import jax.numpy as jnp
from jax import lax
from jax.experimental import pallas as pl
from jax.experimental.pallas import tpu as pltpu
from jax.sharding import PartitionSpec as P

GROUP = 128
EPS = 1e-06
SUB = 8
UNIT = 48
HALVES = {"mix": 1024, "out": 384, "up": 1536}
ROWS = 32
F32 = jnp.float32
BF16 = jnp.bfloat16
ALL = ("dp", "seq")
VMEM = pl.BlockSpec(memory_space=pltpu.VMEM)
SMEM = pl.BlockSpec(memory_space=pltpu.SMEM)
ANY = pl.BlockSpec(memory_space=pl.ANY)


def sds(shape, dtype=F32):
    return jax.ShapeDtypeStruct(shape, dtype)


def over_rows(total, body):
    def step(i, _):
        body(pl.ds(pl.multiple_of(i * ROWS, ROWS), ROWS))
        return 0

    lax.fori_loop(0, total // ROWS, step, 0)


def dot(left, right):
    return jnp.dot(left, right, preferred_element_type=F32)


def dot_t(left, right):
    return lax.dot_general(left, right, (((1,), (1,)), ((), ())), preferred_element_type=F32)


def cmul(ar, ai, br, bi):
    return ar * br - ai * bi, ar * bi + ai * br


def power(cos, sin, times):
    while times > 1:
        cos, sin = cos * cos - sin * sin, 2.0 * cos * sin
        times //= 2
    return cos, sin


def turns(p_ref, half):
    cos, sin = p_ref[3:4, half:], p_ref[4:5, :half]
    return tuple(
        [jnp.broadcast_to(part[:, t * GROUP : (t + 1) * GROUP], (SUB, GROUP)) for t in range(half // GROUP)]
        for part in (cos, sin)
    )


def parts(ref, k, tiles):
    return [ref[k, :, t * GROUP : (t + 1) * GROUP] for t in range(tiles)]


def mix_width(plan, width):
    return 2 * width + width // 2 if plan is None else 2 * HALVES["mix"]


def load_start(pairs, sem):
    for source, target in pairs:
        pltpu.make_async_copy(source, target, sem).start()


def load_wait(pairs, sem):
    for source, target in pairs:
        pltpu.make_async_copy(source, target, sem).wait()


def pairs_of(plan, sources, me_ref, name, target):
    if plan is None:
        return [(sources[{"mix": 0, "out": 1, "up": 2, "down": 3}[name]], target)]
    chip, core = me_ref[1], me_ref[2]
    pairs = []
    for source, others, other_core, column, columns, begin in plan[name]:
        half = core ^ other_core
        for b, other in enumerate(others):
            block = chip ^ other
            if name == "down":
                row, left = block * (2 * UNIT) + half * UNIT, 0
            else:
                row, left = block * UNIT, half * HALVES[name] + begin
            to = target.at[pl.ds(pl.multiple_of(row, UNIT), UNIT), pl.ds(pl.multiple_of(left, GROUP), columns)]
            pairs.append((sources[source].at[b, :, pl.ds(column, columns)], to))
    return pairs


def front_kernel(
    plan, count, me_ref, place_ref, x_ref, p_ref, *refs
):
    w_hbm, refs = refs[:count], refs[count:]
    (
    normed_ref, cpre_ref, gate_ref, rate_ref, kept_ref, feed_ref, sub_ref, total_ref,
    w_ref, sem,
    ) = refs
    rows, width = x_ref.shape
    half = width // 2
    block = rows // SUB
    pairs = pairs_of(plan, w_hbm, me_ref, "mix", w_ref)
    load_start(pairs, sem)

    def norm(r):
        x = x_ref[r, :]
        scale = lax.rsqrt(jnp.mean(x * x, axis=1, keepdims=True) + EPS)
        normed_ref[r, :] = (x * scale * p_ref[0:1, :]).astype(BF16)

    over_rows(rows, norm)
    load_wait(pairs, sem)
    normed = normed_ref[...]
    rate = jax.nn.sigmoid(dot(normed, w_ref[:, 2 * width : 2 * width + half]) + p_ref[3:4, :half])
    rate_ref[...] = rate
    at = lax.broadcasted_iota(jnp.int32, (rows, GROUP), 0)
    fresh = at == place_ref[0]
    for j in range(1, place_ref.shape[0]):
        fresh = jnp.logical_or(fresh, at == place_ref[j])
    tiles = half // GROUP
    for t in range(tiles):
        kept_ref[t] = jnp.where(fresh, 0.0, rate[:, t * GROUP : (t + 1) * GROUP])
    for k in range(2):
        cols = slice(k * half, (k + 1) * half)
        pre = dot(normed, w_ref[:, cols])
        cpre_ref[:, cols] = pre
        feed = (1.0 - rate_ref[...]) * (pre * jax.nn.sigmoid(pre))
        for t in range(tiles):
            feed_ref[k * tiles + t] = feed[:, t * GROUP : (t + 1) * GROUP]
    cos, sin = turns(p_ref, half)

    mag = [jnp.ones((SUB, GROUP), F32)] * tiles
    br = [jnp.zeros((SUB, GROUP), F32)] * tiles
    bi = [jnp.zeros((SUB, GROUP), F32)] * tiles
    for j in range(block):
        at = pl.ds(j, SUB, stride=block)
        for t in range(tiles):
            kept = kept_ref[t, at, :]
            tr, ti = cmul(cos[t], sin[t], br[t], bi[t])
            br[t] = kept * tr + feed_ref[t, at, :]
            bi[t] = kept * ti + feed_ref[tiles + t, at, :]
            mag[t] = mag[t] * kept
    mag, br, bi = (jnp.concatenate(part, axis=1) for part in (mag, br, bi))
    far_cos, far_sin = power(jnp.concatenate(cos, axis=1), jnp.concatenate(sin, axis=1), block)
    ar, ai = mag * far_cos, mag * far_sin
    sub_ref[0] = ar
    sub_ref[1] = ai
    sub_ref[2] = br
    sub_ref[3] = bi
    one_r, one_i, sum_r, sum_i = (part[0:1] for part in (ar, ai, br, bi))
    for k in range(1, SUB):
        kr, ki = ar[k : k + 1], ai[k : k + 1]
        one_r, one_i = cmul(kr, ki, one_r, one_i)
        sum_r, sum_i = cmul(kr, ki, sum_r, sum_i)
        sum_r = sum_r + br[k : k + 1]
        sum_i = sum_i + bi[k : k + 1]
    total_ref[0:1, :] = one_r
    total_ref[1:2, :] = one_i
    total_ref[2:3, :] = sum_r
    total_ref[3:4, :] = sum_i
    for k in range(2):
        cols = slice(width + k * half, width + (k + 1) * half)
        gate_ref[:, k * half : (k + 1) * half] = jax.nn.sigmoid(dot(normed, w_ref[:, cols]))


def front(plan, me, place, x, params, weights):
    rows, width = x.shape
    half = width // 2
    return pl.pallas_call(
        functools.partial(front_kernel, plan, len(weights)),
        out_shape=(
            sds((rows, width), BF16),
            sds((rows, width)),
            sds((rows, width)),
            sds((rows, half)),
            sds((half // GROUP, rows, GROUP)),
            sds((width // GROUP, rows, GROUP)),
            sds((4, SUB, half)),
            sds((4, half)),
        ),
        in_specs=[SMEM, SMEM, VMEM, VMEM] + [ANY] * len(weights),
        out_specs=(VMEM,) * 8,
        scratch_shapes=[pltpu.VMEM((width, mix_width(plan, width)), BF16), pltpu.SemaphoreType.DMA],
        compiler_params=pltpu.CompilerParams(vmem_limit_bytes=56 << 20),
        cost_estimate=pl.CostEstimate(flops=2 * rows * width * 5 * half, bytes_accessed=8 << 20, transcendentals=0),
        name="front",
    )(me, place, x, params, *weights)


def rest_kernel(plan, count, me_ref, x_ref, p_ref, gate_ref, kept_ref, feed_ref, sub_ref, every_ref, *refs):
    w_hbm, refs = refs[:count], refs[count:]
    (
    states_ref, first_ref, gn_ref, rg_ref, gated_ref, after_ref, lifted_ref, both_ref, hidden_ref, next_ref,
    out_ref, up_ref, down_ref, sems,
    ) = refs
    rows, width = x_ref.shape
    half = width // 2
    block = rows // SUB
    inner = hidden_ref.shape[1]
    out_pairs, up_pairs, down_pairs = (
        pairs_of(plan, w_hbm, me_ref, name, ref)
        for name, ref in (("out", out_ref), ("up", up_ref), ("down", down_ref))
    )
    load_start(out_pairs, sems.at[0])
    load_start(up_pairs, sems.at[1])
    load_start(down_pairs, sems.at[2])

    sr = jnp.zeros((1, half), F32)
    si = jnp.zeros((1, half), F32)
    for k in range(every_ref.shape[0]):
        nr, ni = cmul(every_ref[k, 0:1, :], every_ref[k, 1:2, :], sr, si)
        earlier = k < me_ref[0]
        sr = jnp.where(earlier, nr + every_ref[k, 2:3, :], sr)
        si = jnp.where(earlier, ni + every_ref[k, 3:4, :], si)
    for k in range(SUB):
        first_ref[0, k : k + 1, :] = sr
        first_ref[1, k : k + 1, :] = si
        nr, ni = cmul(sub_ref[0, k : k + 1, :], sub_ref[1, k : k + 1, :], sr, si)
        sr = nr + sub_ref[2, k : k + 1, :]
        si = ni + sub_ref[3, k : k + 1, :]
    cos, sin = turns(p_ref, half)
    tiles = half // GROUP
    sr = parts(first_ref, 0, tiles)
    si = parts(first_ref, 1, tiles)
    for j in range(block):
        at = pl.ds(j, SUB, stride=block)
        for t in range(tiles):
            kept = kept_ref[t, at, :]
            tr, ti = cmul(cos[t], sin[t], sr[t], si[t])
            sr[t] = kept * tr + feed_ref[t, at, :]
            si[t] = kept * ti + feed_ref[tiles + t, at, :]
            states_ref[t, at, :] = sr[t]
            states_ref[tiles + t, at, :] = si[t]

    lane = lax.broadcasted_iota(jnp.int32, (ROWS, GROUP), 1)

    def group_norm(r):
        held = jnp.zeros((ROWS, GROUP), F32)
        for g in range(width // GROUP):
            cols = slice(g * GROUP, (g + 1) * GROUP)
            v = gate_ref[r, cols] * states_ref[g, r, :]
            centre = v - jnp.mean(v, axis=1, keepdims=True)
            scale = lax.rsqrt(jnp.mean(centre * centre, axis=1, keepdims=True) + EPS)
            gn = centre * scale
            gn_ref[r, cols] = gn
            gated_ref[r, cols] = (gn * p_ref[1:2, cols]).astype(BF16)
            held = jnp.where(lane == g, scale, held)
        rg_ref[r, :] = held

    over_rows(rows, group_norm)
    load_wait(out_pairs, sems.at[0])
    after_ref[...] = x_ref[...] + dot(gated_ref[...], out_ref[...])

    def norm(r):
        after = after_ref[r, :]
        scale = lax.rsqrt(jnp.mean(after * after, axis=1, keepdims=True) + EPS)
        lifted_ref[r, :] = (after * scale * p_ref[2:3, :]).astype(BF16)

    over_rows(rows, norm)
    load_wait(up_pairs, sems.at[1])
    lifted = lifted_ref[...]
    step = half
    for k in range(inner // step):
        cols = slice(k * step, (k + 1) * step)
        more = slice(inner + k * step, inner + (k + 1) * step)
        a = dot(lifted, up_ref[:, cols])
        b = dot(lifted, up_ref[:, more])
        both_ref[:, cols] = a
        both_ref[:, more] = b
        hidden_ref[:, cols] = (a * jax.nn.sigmoid(a) * b).astype(BF16)
    load_wait(down_pairs, sems.at[2])
    next_ref[...] = after_ref[...] + dot(hidden_ref[...], down_ref[...])


def rest(plan, me, x, params, gate, kept, feed, sub, every, weights):
    rows, width = x.shape
    half = width // 2
    inner = 2 * width
    return pl.pallas_call(
        functools.partial(rest_kernel, plan, len(weights)),
        out_shape=(
            sds((width // GROUP, rows, GROUP)),
            sds((2, SUB, half)),
            sds((rows, width)),
            sds((rows, GROUP)),
            sds((rows, width), BF16),
            sds((rows, width)),
            sds((rows, width), BF16),
            sds((rows, 2 * inner)),
            sds((rows, inner), BF16),
            sds((rows, width)),
        ),
        in_specs=[SMEM] + [VMEM] * 7 + [ANY] * len(weights),
        out_specs=(VMEM,) * 10,
        scratch_shapes=[
            pltpu.VMEM((width, width), BF16),
            pltpu.VMEM((width, 2 * inner), BF16),
            pltpu.VMEM((inner, width), BF16),
            pltpu.SemaphoreType.DMA((3,)),
        ],
        compiler_params=pltpu.CompilerParams(vmem_limit_bytes=56 << 20),
        cost_estimate=pl.CostEstimate(flops=2 * rows * width * 7 * width, bytes_accessed=20 << 20, transcendentals=0),
        name="rest",
    )(me, x, params, gate, kept, feed, sub, every, *weights)


def back_one_kernel(
    plan, count, me_ref, dx_ref, p_ref, both_ref, after_ref, gn_ref, rg_ref, gate_ref, states_ref, kept_ref, sub_ref, *refs
):
    w_hbm, refs = refs[:count], refs[count:]
    (
    dlow_ref, dboth_ref, dafter_ref, dmid_ref, dgpre_ref, dstates_ref, gains_ref, rsub_ref, rtotal_ref,
    work_ref, out_ref, up_ref, down_ref, sems,
    ) = refs
    rows, width = dx_ref.shape
    half = width // 2
    block = rows // SUB
    inner = down_ref.shape[0]
    out_pairs, up_pairs, down_pairs = (
        pairs_of(plan, w_hbm, me_ref, name, ref)
        for name, ref in (("out", out_ref), ("up", up_ref), ("down", down_ref))
    )
    load_start(down_pairs, sems.at[2])
    load_start(up_pairs, sems.at[1])
    load_start(out_pairs, sems.at[0])
    dlow = dx_ref[...].astype(BF16)
    dlow_ref[...] = dlow
    load_wait(down_pairs, sems.at[2])
    step = half
    for k in range(inner // step):
        cols = slice(k * step, (k + 1) * step)
        more = slice(inner + k * step, inner + (k + 1) * step)
        dh = dot_t(dlow, down_ref[cols, :])
        a = both_ref[:, cols]
        sig = jax.nn.sigmoid(a)
        dboth_ref[:, cols] = (dh * both_ref[:, more] * (sig * (1.0 + a * (1.0 - sig)))).astype(BF16)
        dboth_ref[:, more] = (dh * (a * sig)).astype(BF16)
    load_wait(up_pairs, sems.at[1])
    work_ref[...] = dot_t(dboth_ref[...], up_ref[...])

    def norm_back(r):
        after = after_ref[r, :]
        scale = lax.rsqrt(jnp.mean(after * after, axis=1, keepdims=True) + EPS)
        normal = after * scale
        lift = work_ref[r, :]
        e = lift * p_ref[2:3, :]
        d = dx_ref[r, :] + scale * (e - normal * jnp.mean(e * normal, axis=1, keepdims=True))
        dafter_ref[r, :] = d
        dmid_ref[r, :] = d.astype(BF16)
        work_ref[r, :] = lift * normal

    over_rows(rows, norm_back)
    gains_ref[0:1, :] = jnp.sum(work_ref[...], axis=0, keepdims=True)
    load_wait(out_pairs, sems.at[0])
    work_ref[...] = dot_t(dmid_ref[...], out_ref[...])

    def group_back(r):
        held = rg_ref[r, :]
        for g in range(width // GROUP):
            cols = slice(g * GROUP, (g + 1) * GROUP)
            gn = gn_ref[r, cols]
            dg = work_ref[r, cols]
            e = dg * p_ref[1:2, cols]
            dv = held[:, g : g + 1] * (
                e - jnp.mean(e, axis=1, keepdims=True) - gn * jnp.mean(e * gn, axis=1, keepdims=True)
            )
            gate = gate_ref[r, cols]
            dgpre_ref[r, cols] = (dv * states_ref[g, r, :] * gate * (1.0 - gate)).astype(BF16)
            dstates_ref[g, r, :] = dv * gate
            work_ref[r, cols] = dg * gn

    over_rows(rows, group_back)
    gains_ref[1:2, :] = jnp.sum(work_ref[...], axis=0, keepdims=True)

    cos, sin = turns(p_ref, half)
    tiles = half // GROUP
    zr = [jnp.zeros((SUB, GROUP), F32)] * tiles
    zi = [jnp.zeros((SUB, GROUP), F32)] * tiles
    for j in reversed(range(block)):
        at = pl.ds(j, SUB, stride=block)
        for t in range(tiles):
            kept = kept_ref[t, at, :]
            qr = dstates_ref[t, at, :] + zr[t]
            qi = dstates_ref[tiles + t, at, :] + zi[t]
            zr[t] = kept * (cos[t] * qr + sin[t] * qi)
            zi[t] = kept * (cos[t] * qi - sin[t] * qr)
    zr, zi = jnp.concatenate(zr, axis=1), jnp.concatenate(zi, axis=1)
    rsub_ref[0] = zr
    rsub_ref[1] = zi
    tr = jnp.zeros((1, half), F32)
    ti = jnp.zeros((1, half), F32)
    for k in reversed(range(SUB)):
        ar, ai = sub_ref[0, k : k + 1, :], sub_ref[1, k : k + 1, :]
        tr, ti = ar * tr + ai * ti + zr[k : k + 1], ar * ti - ai * tr + zi[k : k + 1]
    rtotal_ref[0:1, :] = tr
    rtotal_ref[1:2, :] = ti


def back_one(plan, me, dx, params, kept_values, weights):
    both, after, gn, rg, gate, states, kept, sub = kept_values
    rows, width = dx.shape
    half = width // 2
    inner = 2 * width
    return pl.pallas_call(
        functools.partial(back_one_kernel, plan, len(weights)),
        out_shape=(
            sds((rows, width), BF16),
            sds((rows, 2 * inner), BF16),
            sds((rows, width)),
            sds((rows, width), BF16),
            sds((rows, width), BF16),
            sds((width // GROUP, rows, GROUP)),
            sds((2, width)),
            sds((2, SUB, half)),
            sds((2, half)),
        ),
        in_specs=[SMEM] + [VMEM] * 10 + [ANY] * len(weights),
        out_specs=(VMEM,) * 9,
        scratch_shapes=[
            pltpu.VMEM((rows, width), F32),
            pltpu.VMEM((width, width), BF16),
            pltpu.VMEM((width, 2 * inner), BF16),
            pltpu.VMEM((inner, width), BF16),
            pltpu.SemaphoreType.DMA((3,)),
        ],
        compiler_params=pltpu.CompilerParams(vmem_limit_bytes=56 << 20),
        cost_estimate=pl.CostEstimate(flops=2 * rows * width * 7 * width, bytes_accessed=20 << 20, transcendentals=0),
        name="back_one",
    )(me, dx, params, both, after, gn, rg, gate, states, kept, sub, *weights)


def back_two_kernel(
    plan, count, me_ref, x_ref, p_ref, dafter_ref, dgpre_ref, dstates_ref, states_ref, kept_ref, rate_ref, cpre_ref,
    first_ref, sub_ref, rsub_ref, every_ref, revery_ref, *refs
):
    w_hbm, refs = refs[:count], refs[count:]
    (
    dmixin_ref, dx_ref, gains_ref,
    work_ref, q_ref, turn_ref, start_ref, w_ref, sem,
    ) = refs
    rows, width = x_ref.shape
    half = width // 2
    block = rows // SUB
    pairs = pairs_of(plan, w_hbm, me_ref, "mix", w_ref)
    load_start(pairs, sem)
    zr = jnp.zeros((1, half), F32)
    zi = jnp.zeros((1, half), F32)
    for k in reversed(range(every_ref.shape[0])):
        ar, ai = every_ref[k, 0:1, :], every_ref[k, 1:2, :]
        later = k > me_ref[0]
        nr = ar * zr + ai * zi + revery_ref[k, 0:1, :]
        ni = ar * zi - ai * zr + revery_ref[k, 1:2, :]
        zr = jnp.where(later, nr, zr)
        zi = jnp.where(later, ni, zi)
    for k in reversed(range(SUB)):
        start_ref[0, k : k + 1, :] = zr
        start_ref[1, k : k + 1, :] = zi
        ar, ai = sub_ref[0, k : k + 1, :], sub_ref[1, k : k + 1, :]
        zr, zi = (
            ar * zr + ai * zi + rsub_ref[0, k : k + 1, :],
            ar * zi - ai * zr + rsub_ref[1, k : k + 1, :],
        )
    cos, sin = turns(p_ref, half)
    tiles = half // GROUP
    zr = parts(start_ref, 0, tiles)
    zi = parts(start_ref, 1, tiles)
    angle = [jnp.zeros((SUB, GROUP), F32)] * tiles
    for j in reversed(range(block)):
        at = pl.ds(j, SUB, stride=block)
        before = pl.ds(max(j - 1, 0), SUB, stride=block)
        for t in range(tiles):
            kept = kept_ref[t, at, :]
            qr = dstates_ref[t, at, :] + zr[t]
            qi = dstates_ref[tiles + t, at, :] + zi[t]
            q_ref[t, at, :] = qr
            q_ref[tiles + t, at, :] = qi
            zr[t] = kept * (cos[t] * qr + sin[t] * qi)
            zi[t] = kept * (cos[t] * qi - sin[t] * qr)
            if j:
                sr, si = states_ref[t, before, :], states_ref[tiles + t, before, :]
            else:
                sr, si = (first_ref[k, :, t * GROUP : (t + 1) * GROUP] for k in range(2))
            turn_ref[t, at, :] = zr[t] * sr + zi[t] * si
            angle[t] = angle[t] + (zi[t] * sr - zr[t] * si)
    gains_ref[1:2, half:] = jnp.sum(jnp.concatenate(angle, axis=1), axis=0, keepdims=True)

    def activations(r):
        for t in range(tiles):
            rate = rate_ref[r, t * GROUP : (t + 1) * GROUP]
            left = 1.0 - rate
            meet = jnp.zeros_like(rate)
            for k in range(2):
                cols = slice((k * tiles + t) * GROUP, (k * tiles + t + 1) * GROUP)
                pre = cpre_ref[r, cols]
                sig = jax.nn.sigmoid(pre)
                q = q_ref[k * tiles + t, r, :]
                meet = meet + q * (pre * sig)
                dmixin_ref[r, cols] = (left * q * (sig * (1.0 + pre * (1.0 - sig)))).astype(BF16)
            dfpre = left * (turn_ref[t, r, :] - rate * meet)
            dmixin_ref[r, 2 * width + t * GROUP : 2 * width + (t + 1) * GROUP] = dfpre.astype(BF16)
            turn_ref[t, r, :] = dfpre
        dmixin_ref[r, width : 2 * width] = dgpre_ref[r, :]

    over_rows(rows, activations)
    for t in range(tiles):
        gains_ref[1:2, t * GROUP : (t + 1) * GROUP] = jnp.sum(turn_ref[t], axis=0, keepdims=True)
    load_wait(pairs, sem)
    work_ref[...] = dot_t(dmixin_ref[...], w_ref[:, : dmixin_ref.shape[1]])

    def norm_back(r):
        x = x_ref[r, :]
        scale = lax.rsqrt(jnp.mean(x * x, axis=1, keepdims=True) + EPS)
        normal = x * scale
        dn = work_ref[r, :]
        e = dn * p_ref[0:1, :]
        dx_ref[r, :] = dafter_ref[r, :] + scale * (e - normal * jnp.mean(e * normal, axis=1, keepdims=True))
        work_ref[r, :] = dn * normal

    over_rows(rows, norm_back)
    gains_ref[0:1, :] = jnp.sum(work_ref[...], axis=0, keepdims=True)


def back_two(plan, me, x, params, dafter, dgpre, dstates, states, kept, rate, cpre, first, sub, rsub, every, revery, weights):
    rows, width = x.shape
    half = width // 2
    return pl.pallas_call(
        functools.partial(back_two_kernel, plan, len(weights)),
        out_shape=(
            sds((rows, 2 * width + half), BF16),
            sds((rows, width)),
            sds((2, width)),
        ),
        in_specs=[SMEM] + [VMEM] * 14 + [ANY] * len(weights),
        out_specs=(VMEM,) * 3,
        scratch_shapes=[
            pltpu.VMEM((rows, width), F32),
            pltpu.VMEM((width // GROUP, rows, GROUP), F32),
            pltpu.VMEM((half // GROUP, rows, GROUP), F32),
            pltpu.VMEM((2, SUB, half), F32),
            pltpu.VMEM((width, mix_width(plan, width)), BF16),
            pltpu.SemaphoreType.DMA,
        ],
        compiler_params=pltpu.CompilerParams(vmem_limit_bytes=56 << 20),
        cost_estimate=pl.CostEstimate(flops=2 * rows * width * 5 * half, bytes_accessed=10 << 20, transcendentals=0),
        name="back_two",
    )(me, x, params, dafter, dgpre, dstates, states, kept, rate, cpre, first, sub, rsub, every, revery, *weights)


def row_product(left, right):
    return lax.dot_general(left, right, (((0,), (0,)), ((), ())), preferred_element_type=F32)


def grad_rest_kernel(
    me_ref, gated_ref, dmid_ref, lifted_ref, dboth_ref, hidden_ref, dlow_ref, keep_ref, send_ref,
    down_ref, up_ref, out_ref, sem,
):
    chip, core = me_ref[1], me_ref[2]
    chips = keep_ref.shape[0]
    width = dlow_ref.shape[1]
    pairs = []

    def export(name, grad, column, columns):
        for half, target in ((core, keep_ref), (1 - core, send_ref)):
            for b in range(chips):
                block = chip ^ b
                if name == "down":
                    row, left = block * (2 * UNIT) + half * UNIT, 0
                else:
                    row, left = block * UNIT, half * HALVES[name]
                pair = (
                    grad.at[pl.ds(pl.multiple_of(row, UNIT), UNIT), pl.ds(pl.multiple_of(left, GROUP), columns)],
                    target.at[b, :, pl.ds(column, columns)],
                )
                load_start([pair], sem)
                pairs.append(pair)

    step = HALVES["out"]
    hidden, dlow = hidden_ref[...], dlow_ref[...]
    for k in range(width // step):
        cols = slice(k * step, (k + 1) * step)
        down_ref[:, cols] = row_product(hidden, dlow[:, cols]).astype(BF16)
    export("down", down_ref, HALVES["out"] + HALVES["up"], width)
    lifted = lifted_ref[...]
    for k in range(up_ref.shape[1] // step):
        cols = slice(k * step, (k + 1) * step)
        up_ref[:, cols] = row_product(lifted, dboth_ref[:, cols]).astype(BF16)
    export("up", up_ref, HALVES["out"], HALVES["up"])
    gated = gated_ref[...]
    for k in range(width // step):
        cols = slice(k * step, (k + 1) * step)
        out_ref[:, cols] = row_product(gated, dmid_ref[:, cols]).astype(BF16)
    export("out", out_ref, 0, HALVES["out"])
    load_wait(pairs, sem)


def grad_rest(me, chips, gated, dmid, lifted, dboth, hidden, dlow):
    rows, width = dlow.shape
    inner = hidden.shape[1]
    shape = sds((chips, UNIT, HALVES["out"] + HALVES["up"] + width), BF16)
    return pl.pallas_call(
        grad_rest_kernel,
        out_shape=(shape, shape),
        in_specs=[SMEM] + [VMEM] * 6,
        out_specs=(ANY, ANY),
        scratch_shapes=[
            pltpu.VMEM((inner, width), BF16),
            pltpu.VMEM((width, 2 * inner), BF16),
            pltpu.VMEM((width, width), BF16),
            pltpu.SemaphoreType.DMA,
        ],
        compiler_params=pltpu.CompilerParams(vmem_limit_bytes=56 << 20),
        cost_estimate=pl.CostEstimate(flops=2 * rows * width * 7 * width, bytes_accessed=12 << 20, transcendentals=0),
        name="grad_rest",
    )(me, gated, dmid, lifted, dboth, hidden, dlow)


def grad_mix_kernel(me_ref, normed_ref, dmixin_ref, extra_ref, keep_ref, send_ref, grad_ref, sem):
    chip, core = me_ref[1], me_ref[2]
    step = HALVES["out"]
    normed = normed_ref[...]
    size = dmixin_ref.shape[1]
    for k in range(size // step):
        cols = slice(k * step, (k + 1) * step)
        grad_ref[:, cols] = row_product(normed, dmixin_ref[:, cols]).astype(BF16)
    grad_ref[:, size:] = jnp.transpose(extra_ref[...]).astype(BF16)
    pairs = []
    for half, target in ((core, keep_ref), (1 - core, send_ref)):
        for b in range(keep_ref.shape[0]):
            row, left = (chip ^ b) * UNIT, half * HALVES["mix"]
            pairs.append(
                (
                    grad_ref.at[
                        pl.ds(pl.multiple_of(row, UNIT), UNIT), pl.ds(pl.multiple_of(left, GROUP), HALVES["mix"])
                    ],
                    target.at[b],
                )
            )
    load_start(pairs, sem)
    load_wait(pairs, sem)


def grad_mix(me, chips, normed, dmixin, extra):
    rows, width = normed.shape
    shape = sds((chips, UNIT, HALVES["mix"]), BF16)
    return pl.pallas_call(
        grad_mix_kernel,
        out_shape=(shape, shape),
        in_specs=[SMEM] + [VMEM] * 3,
        out_specs=(ANY, ANY),
        scratch_shapes=[pltpu.VMEM((width, 2 * HALVES["mix"]), BF16), pltpu.SemaphoreType.DMA],
        compiler_params=pltpu.CompilerParams(vmem_limit_bytes=56 << 20),
        cost_estimate=pl.CostEstimate(flops=5 * rows * width * width, bytes_accessed=4 << 20, transcendentals=0),
        name="grad_mix",
    )(me, normed, dmixin, extra)


def table_kernel(plan, count, me_ref, *refs):
    sources, (table_ref, held_ref, sem) = refs[:count], refs[count:]
    chip, core = me_ref[1], me_ref[2]
    pairs = []
    for source, others, other_core, column in plan["small"]:
        left = pl.multiple_of((core ^ other_core) * GROUP, GROUP)
        for b, other in enumerate(others):
            row = pl.multiple_of((chip ^ other) * UNIT, UNIT)
            pairs.append(
                (sources[source].at[b, :, pl.ds(column, GROUP)], held_ref.at[pl.ds(row, UNIT), pl.ds(left, GROUP)])
            )
    load_start(pairs, sem)
    load_wait(pairs, sem)
    table_ref[...] = jnp.transpose(held_ref[:, GROUP:].astype(F32))[: table_ref.shape[0]]


def table_of(plan, me, weights, rows, width):
    return pl.pallas_call(
        functools.partial(table_kernel, plan, len(weights)),
        out_shape=sds((rows, width)),
        in_specs=[SMEM] + [ANY] * len(weights),
        out_specs=VMEM,
        scratch_shapes=[pltpu.VMEM((width, 2 * GROUP), BF16), pltpu.SemaphoreType.DMA],
        compiler_params=pltpu.CompilerParams(vmem_limit_bytes=16 << 20),
        cost_estimate=pl.CostEstimate(flops=1 << 20, bytes_accessed=1 << 20, transcendentals=0),
        name="table",
    )(me, *weights)


def swap_seq(x, bit):
    return lax.ppermute(x, "seq", [(i, i ^ bit) for i in range(lax.axis_size("seq"))])


def swap_dp(x, bit):
    return lax.ppermute(x, "dp", [(i, i ^ bit) for i in range(lax.axis_size("dp"))])


def spread(unit, cut):
    n_dp = lax.axis_size("dp")
    far = jnp.stack([unit] + [swap_dp(unit, k) for k in range(1, n_dp)])
    deep = tuple(4 * k for k in range(n_dp))
    arrays = []
    for cols, one, two in ((slice(0, cut), 1, 2), (slice(cut, None), 2, 1)):
        own = far[:, :, cols]
        near = jnp.concatenate([own, swap_seq(own, 2 * one)], axis=0)
        near_at = deep + tuple(k ^ one for k in deep)
        last = swap_seq(near, 2 * two)
        last_at = tuple(k ^ two for k in near_at)
        for array, at in ((near, near_at), (last, last_at)):
            arrays.append((array, at, 0, cols.start))
            arrays.append((swap_seq(array, 1), at, 1, cols.start))
    return arrays


def gather_up(keep, send, cut):
    n_dp = lax.axis_size("dp")
    both = (keep.astype(F32) + swap_seq(send, 1).astype(F32)).astype(BF16)
    both = both.reshape(n_dp, 2, 2, *both.shape[1:])
    pieces = []
    for cols, first in ((slice(0, cut), 2), (slice(cut, None), 1)):
        part = both[..., cols]
        if first == 1:
            part = jnp.swapaxes(part, 1, 2)
        got = swap_seq(part[:, 1], 2 * first)
        part = (part[:, 0].astype(F32) + got.astype(F32)).astype(BF16)
        got = swap_seq(part[:, 1], 2 * (3 - first))
        pieces.append((part[:, 0].astype(F32) + got.astype(F32)).astype(BF16))
    total = jnp.concatenate(pieces, axis=2)
    result = total[0].astype(F32)
    for k in range(1, n_dp):
        result = result + swap_dp(total[k], k).astype(F32)
    return result


def layer_params(gains, chan):
    half = chan.shape[0] // 2
    angle = chan[half:]
    rows = [
        gains[0],
        gains[1],
        gains[2],
        jnp.concatenate([chan[:half], jnp.cos(angle)]),
        jnp.concatenate([jnp.sin(angle), jnp.zeros((half,), F32)]),
    ]
    return jnp.concatenate([jnp.stack(rows), jnp.zeros((3, 2 * half), F32)], axis=0)


def body(stream, w_mix, w_out, w_up, w_down, gains, chan_params, lengths, cotangent):
    rows, width = stream.shape
    depth = w_mix.shape[0]
    share = w_mix.shape[1]
    where = lax.axis_index("seq")
    me = jnp.stack([where, (lax.axis_index("dp") * lax.axis_size("seq") + where) // 2, where % 2]).astype(jnp.int32)
    n_dp, n_seq = lax.axis_size("dp"), lax.axis_size("seq")
    shards = n_dp * n_seq
    base = where * rows
    ends = [lengths[0, 0]]
    for j in range(1, lengths.shape[1]):
        ends.append(ends[-1] + lengths[0, j])
    fresh = jnp.stack([end - lengths[0, j] for j, end in enumerate(ends)])
    place = (fresh - base).astype(jnp.int32)
    keep = ((base + lax.broadcasted_iota(jnp.int32, (rows, 1), 0)) < ends[-1]).astype(F32)

    small = jnp.concatenate(
        [gains.reshape(depth * 3, share).T, chan_params.T, jnp.zeros((share, 128 - 4 * depth), BF16)], axis=1
    )
    mix_cols, out_cols, up_cols = w_mix.shape[2], w_out.shape[2], w_up.shape[2]
    starts = [0, mix_cols, mix_cols + out_cols, mix_cols + out_cols + up_cols]
    full = starts[-1] + 2 * width
    weights = []
    fast = n_seq == 8 and n_dp & (n_dp - 1) == 0 and 2 * share == UNIT
    chips = shards // 2
    core = where % 2
    if fast:
        padding = jnp.zeros((share, 2 * HALVES["mix"] - mix_cols - 128), BF16)
        halves = ([], [])
        for l in range(depth):
            tail = small if l == 0 else jnp.zeros_like(small)
            mix = jnp.concatenate([w_mix[l], padding, tail], axis=1)
            for h in range(2):
                for w, size in ((mix, HALVES["mix"]), (w_out[l], HALVES["out"]), (w_up[l], HALVES["up"])):
                    halves[h].append(w[:, h * size : (h + 1) * size])
        halves = [jnp.concatenate(half, axis=1) for half in halves]
        mine = jnp.where(core == 0, halves[0], halves[1])
        other = swap_seq(jnp.where(core == 0, halves[1], halves[0]), 1)
        units = jnp.where(core == 0, jnp.concatenate([mine, other]), jnp.concatenate([other, mine]))
        size = sum(HALVES.values())
        plans = []
        for l in range(depth):
            unit = units[:, l * size : (l + 1) * size]
            mix_unit = unit[:, : HALVES["mix"]]
            rest_unit = jnp.concatenate([unit[:, HALVES["mix"] :], w_down[l]], axis=1)
            mix_arrays = spread(mix_unit, HALVES["mix"] // 2)
            rest_arrays = spread(rest_unit, HALVES["out"] + 2 * GROUP * 6)
            weights.append((tuple(a[0] for a in mix_arrays), tuple(a[0] for a in rest_arrays)))
            plan = {"mix": [], "out": [], "up": [], "down": [], "small": []}
            for source, (array, at, other_core, begin) in enumerate(mix_arrays):
                plan["mix"].append((source, at, other_core, 0, array.shape[2], begin))
                if begin:
                    plan["small"].append((source, at, other_core, array.shape[2] - 128))
            spans = {"out": (0, HALVES["out"]), "up": (HALVES["out"], HALVES["up"]), "down": (HALVES["out"] + HALVES["up"], width)}
            for source, (array, at, other_core, begin) in enumerate(rest_arrays):
                for name, (low, count) in spans.items():
                    a, b = max(low, begin), min(low + count, begin + array.shape[2])
                    if a < b:
                        plan[name].append((source, at, other_core, a - begin, b - a, a - low))
            plans.append(plan)
        table = table_of(plans[0], me, weights[0][0], 4 * depth, width)
    else:
        plans = [None] * depth
        table = lax.all_gather(small, ALL, axis=0, tiled=True)[:, : 4 * depth].T.astype(F32)
        for l in range(depth):
            got = tuple(lax.all_gather(w[l], ALL, axis=0, tiled=True) for w in (w_mix, w_out, w_up, w_down))
            weights.append((got, got))
    params = [layer_params(table[3 * l : 3 * l + 3], table[3 * depth + l]) for l in range(depth)]

    values = stream.astype(F32)
    saved = []
    for l in range(depth):
        normed, cpre, gate, rate, kept, feed, sub, total = front(plans[l], me, place, values, params[l], weights[l][0])
        every = lax.all_gather(total, "seq")
        states, first, gn, rg, gated, after, lifted, both, hidden, result = rest(
            plans[l], me, values, params[l], gate, kept, feed, sub, every, weights[l][1]
        )
        saved.append((values, normed, cpre, gate, rate, kept, sub, every, states, first, gn, rg, gated, after, lifted, both, hidden))
        values = result
    mixed = values.astype(BF16)
    dx = cotangent.astype(F32) * keep
    sums = [None] * depth
    smalls = [None] * depth
    for l in reversed(range(depth)):
        x, normed, cpre, gate, rate, kept, sub, every, states, first, gn, rg, gated, after, lifted, both, hidden = saved[l]
        dlow, dboth, dafter, dmid, dgpre, dstates, gains_a, rsub, rtotal = back_one(
            plans[l], me, dx, params[l], (both, after, gn, rg, gate, states, kept, sub), weights[l][1]
        )
        revery = lax.all_gather(rtotal, "seq")
        dmixin, dx, gains_b = back_two(
            plans[l], me, x, params[l], dafter, dgpre, dstates, states, kept, rate, cpre, first, sub, rsub, every, revery, weights[l][0]
        )
        smalls[l] = [gains_b[0], gains_a[1], gains_a[0], gains_b[1]]
        if fast:
            rest_sum = gather_up(
                *grad_rest(me, chips, gated, dmid, lifted, dboth, hidden, dlow), HALVES["out"] + 2 * GROUP * 6
            )
            extra = jnp.zeros((128, width), F32)
            if l == 0:
                extra = jnp.concatenate([jnp.stack(smalls[k]) for k in range(depth)] + [extra[: 128 - 4 * depth]])
            mix_sum = gather_up(*grad_mix(me, chips, normed, dmixin, extra), HALVES["mix"] // 2)
            sums[l] = (mix_sum, rest_sum)
        else:
            grads = [row_product(normed, dmixin), row_product(gated, dmid), row_product(lifted, dboth), row_product(hidden, dlow)]
            grads.append(jnp.stack(smalls[l], axis=1))
            sums[l] = [
                lax.psum_scatter(g.astype(BF16), ALL, scatter_dimension=0, tiled=True).astype(F32) for g in grads
            ]
    if fast:
        pieces = {"mix": [], "out": [], "up": [], "down": []}
        for l in range(depth):
            mix_sum, rest_sum = sums[l]
            joint = HALVES["out"] + HALVES["up"]
            line = jnp.concatenate([mix_sum, rest_sum[:, :joint]], axis=1)
            line = line.reshape(2, share, -1)
            mine = jnp.where(core == 0, line[0], line[1])
            other = swap_seq(jnp.where(core == 0, line[1], line[0]), 1)
            first = jnp.where(core == 0, mine, other)
            second = jnp.where(core == 0, other, mine)
            at = 0
            for name in ("mix", "out", "up"):
                cols = slice(at, at + HALVES[name])
                pieces[name].append(jnp.concatenate([first[:, cols], second[:, cols]], axis=1))
                at += HALVES[name]
            pieces["down"].append(rest_sum[:, joint:])
        g_mix, g_out, g_up, g_down = (jnp.stack(pieces[name]) for name in ("mix", "out", "up", "down"))
        tail = g_mix[0][:, 2 * HALVES["mix"] - 128 :][:, : 4 * depth].reshape(share, depth, 4)
        tail = jnp.swapaxes(tail, 0, 1)
        g_mix = g_mix[:, :, :mix_cols]
    else:
        g_mix, g_out, g_up, g_down, tail = (jnp.stack([sums[l][k] for l in range(depth)]) for k in range(5))
    return (mixed, dx, g_mix, g_out, g_up, g_down, jnp.swapaxes(tail[:, :, :3], 1, 2), tail[:, :, 3])


def solution(mesh):
    placed = (
        P(ALL, None),
        P(None, ALL, None),
        P(None, ALL, None),
        P(None, ALL, None),
        P(None, ALL, None),
        P(None, None, ALL),
        P(None, ALL),
        P("dp", None),
        P(ALL, None),
    )
    return jax.shard_map(
        body,
        mesh=mesh,
        in_specs=placed,
        out_specs=(
            P(ALL, None),
            P(ALL, None),
            P(None, ALL, None),
            P(None, ALL, None),
            P(None, ALL, None),
            P(None, ALL, None),
            P(None, None, ALL),
            P(None, ALL),
        ),
        check_vma=False,
    )
```

```python
import functools

import jax
import jax.numpy as jnp
from jax import lax
from jax.experimental import pallas as pl
from jax.experimental.pallas import tpu as pltpu
from jax.sharding import PartitionSpec as P

GROUP = 128
EPS = 1e-06
SUB = 8
UNIT = 48
HALVES = {"mix": 1024, "out": 384, "up": 1536}
ROWS = 32
F32 = jnp.float32
BF16 = jnp.bfloat16
ALL = ("dp", "seq")
VMEM = pl.BlockSpec(memory_space=pltpu.VMEM)
SMEM = pl.BlockSpec(memory_space=pltpu.SMEM)
ANY = pl.BlockSpec(memory_space=pl.ANY)


def sds(shape, dtype=F32):
    return jax.ShapeDtypeStruct(shape, dtype)


def over_rows(total, body):
    def step(i, _):
        body(pl.ds(pl.multiple_of(i * ROWS, ROWS), ROWS))
        return 0

    lax.fori_loop(0, total // ROWS, step, 0)


def dot(left, right):
    return jnp.dot(left, right, preferred_element_type=F32)


def dot_t(left, right):
    return lax.dot_general(left, right, (((1,), (1,)), ((), ())), preferred_element_type=F32)


def cmul(ar, ai, br, bi):
    return ar * br - ai * bi, ar * bi + ai * br


def power(cos, sin, times):
    while times > 1:
        cos, sin = cos * cos - sin * sin, 2.0 * cos * sin
        times //= 2
    return cos, sin


def turns(p_ref, half):
    cos, sin = p_ref[3:4, half:], p_ref[4:5, :half]
    return tuple(
        [jnp.broadcast_to(part[:, t * GROUP : (t + 1) * GROUP], (SUB, GROUP)) for t in range(half // GROUP)]
        for part in (cos, sin)
    )


def parts(ref, k, tiles):
    return [ref[k, :, t * GROUP : (t + 1) * GROUP] for t in range(tiles)]


def mix_width(plan, width):
    return 2 * width + width // 2 if plan is None else 2 * HALVES["mix"]


def load_start(pairs, sem):
    for source, target in pairs:
        pltpu.make_async_copy(source, target, sem).start()


def load_wait(pairs, sem):
    for source, target in pairs:
        pltpu.make_async_copy(source, target, sem).wait()


def pairs_of(plan, sources, me_ref, name, target):
    if plan is None:
        return [(sources[{"mix": 0, "out": 1, "up": 2, "down": 3}[name]], target)]
    chip, core = me_ref[1], me_ref[2]
    column, columns = plan[name]
    pairs = []
    for source, (other_core, rels) in enumerate(plan["sources"]):
        half = core ^ other_core
        for b, (zero, one) in enumerate(zip(*rels)):
            block = chip ^ (zero + half * (one - zero))
            if name == "down":
                row, left = block * (2 * UNIT) + half * UNIT, 0
            elif name == "small":
                row, left = block * UNIT, half * GROUP
            else:
                row, left = block * UNIT, half * HALVES[name]
            to = target.at[pl.ds(pl.multiple_of(row, UNIT), UNIT), pl.ds(pl.multiple_of(left, GROUP), columns)]
            pairs.append((sources[source].at[b, :, pl.ds(column, columns)], to))
    return pairs


def front_kernel(
    plan, count, me_ref, x_ref, p_ref, *refs
):
    w_hbm, refs = refs[:count], refs[count:]
    (
    normed_ref, cpre_ref, gate_ref, rate_ref, kept_ref, feed_ref, sub_ref, total_ref,
    w_ref, sem,
    ) = refs
    rows, width = x_ref.shape
    half = width // 2
    block = rows // SUB
    pairs = pairs_of(plan, w_hbm, me_ref, "mix", w_ref)
    load_start(pairs, sem)

    def norm(r):
        x = x_ref[r, :].astype(F32)
        scale = lax.rsqrt(jnp.mean(x * x, axis=1, keepdims=True) + EPS)
        normed_ref[r, :] = (x * scale * p_ref[0:1, :]).astype(BF16)

    over_rows(rows, norm)
    load_wait(pairs, sem)
    normed = normed_ref[...]
    rate = jax.nn.sigmoid(dot(normed, w_ref[:, 2 * width : 2 * width + half]) + p_ref[3:4, :half])
    rate_ref[...] = rate
    at = lax.broadcasted_iota(jnp.int32, (rows, GROUP), 0)
    fresh = at == me_ref[5]
    for j in range(6, me_ref.shape[0]):
        fresh = jnp.logical_or(fresh, at == me_ref[j])
    tiles = half // GROUP
    for t in range(tiles):
        kept_ref[t] = jnp.where(fresh, 0.0, rate[:, t * GROUP : (t + 1) * GROUP])
    for k in range(2):
        cols = slice(k * half, (k + 1) * half)
        pre = dot(normed, w_ref[:, cols])
        cpre_ref[:, cols] = pre
        feed = (1.0 - rate_ref[...]) * (pre * jax.nn.sigmoid(pre))
        for t in range(tiles):
            feed_ref[k * tiles + t] = feed[:, t * GROUP : (t + 1) * GROUP]
    cos, sin = turns(p_ref, half)

    mag = [jnp.ones((SUB, GROUP), F32)] * tiles
    br = [jnp.zeros((SUB, GROUP), F32)] * tiles
    bi = [jnp.zeros((SUB, GROUP), F32)] * tiles
    for j in range(block):
        at = pl.ds(j, SUB, stride=block)
        for t in range(tiles):
            kept = kept_ref[t, at, :]
            tr, ti = cmul(cos[t], sin[t], br[t], bi[t])
            br[t] = kept * tr + feed_ref[t, at, :]
            bi[t] = kept * ti + feed_ref[tiles + t, at, :]
            mag[t] = mag[t] * kept
    mag, br, bi = (jnp.concatenate(part, axis=1) for part in (mag, br, bi))
    far_cos, far_sin = power(jnp.concatenate(cos, axis=1), jnp.concatenate(sin, axis=1), block)
    ar, ai = mag * far_cos, mag * far_sin
    sub_ref[0] = ar
    sub_ref[1] = ai
    sub_ref[2] = br
    sub_ref[3] = bi
    one_r, one_i, sum_r, sum_i = (part[0:1] for part in (ar, ai, br, bi))
    for k in range(1, SUB):
        kr, ki = ar[k : k + 1], ai[k : k + 1]
        one_r, one_i = cmul(kr, ki, one_r, one_i)
        sum_r, sum_i = cmul(kr, ki, sum_r, sum_i)
        sum_r = sum_r + br[k : k + 1]
        sum_i = sum_i + bi[k : k + 1]
    total_ref[0:1, :] = one_r
    total_ref[1:2, :] = one_i
    total_ref[2:3, :] = sum_r
    total_ref[3:4, :] = sum_i
    for k in range(2):
        cols = slice(width + k * half, width + (k + 1) * half)
        gate_ref[:, k * half : (k + 1) * half] = jax.nn.sigmoid(dot(normed, w_ref[:, cols]))


def front(plan, me, x, params, weights):
    rows, width = x.shape
    half = width // 2
    return pl.pallas_call(
        functools.partial(front_kernel, plan, len(weights)),
        out_shape=(
            sds((rows, width), BF16),
            sds((rows, width)),
            sds((rows, width)),
            sds((rows, half)),
            sds((half // GROUP, rows, GROUP)),
            sds((width // GROUP, rows, GROUP)),
            sds((4, SUB, half)),
            sds((4, half)),
        ),
        in_specs=[SMEM, VMEM, VMEM] + [ANY] * len(weights),
        out_specs=(VMEM,) * 8,
        scratch_shapes=[pltpu.VMEM((width, mix_width(plan, width)), BF16), pltpu.SemaphoreType.DMA],
        compiler_params=pltpu.CompilerParams(vmem_limit_bytes=56 << 20),
        cost_estimate=pl.CostEstimate(flops=2 * rows * width * 5 * half, bytes_accessed=8 << 20, transcendentals=0),
        name="front",
    )(me, x, params, *weights)


def mid_kernel(plan, count, me_ref, x_ref, p_ref, gate_ref, kept_ref, feed_ref, sub_ref, every_ref, *refs):
    w_hbm, refs = refs[:count], refs[count:]
    states_ref, first_ref, gn_ref, rg_ref, gated_ref, after_ref, lifted_ref, out_ref, sem = refs
    rows, width = x_ref.shape
    half = width // 2
    block = rows // SUB
    pairs = pairs_of(plan, w_hbm, me_ref, "out", out_ref)
    load_start(pairs, sem)

    sr = jnp.zeros((1, half), F32)
    si = jnp.zeros((1, half), F32)
    for k in range(every_ref.shape[0]):
        at = k ^ me_ref[3]
        nr, ni = cmul(every_ref[at, 0:1, :], every_ref[at, 1:2, :], sr, si)
        earlier = k < me_ref[0]
        sr = jnp.where(earlier, nr + every_ref[at, 2:3, :], sr)
        si = jnp.where(earlier, ni + every_ref[at, 3:4, :], si)
    for k in range(SUB):
        first_ref[0, k : k + 1, :] = sr
        first_ref[1, k : k + 1, :] = si
        nr, ni = cmul(sub_ref[0, k : k + 1, :], sub_ref[1, k : k + 1, :], sr, si)
        sr = nr + sub_ref[2, k : k + 1, :]
        si = ni + sub_ref[3, k : k + 1, :]
    cos, sin = turns(p_ref, half)
    tiles = half // GROUP
    sr = parts(first_ref, 0, tiles)
    si = parts(first_ref, 1, tiles)
    for j in range(block):
        at = pl.ds(j, SUB, stride=block)
        for t in range(tiles):
            kept = kept_ref[t, at, :]
            tr, ti = cmul(cos[t], sin[t], sr[t], si[t])
            sr[t] = kept * tr + feed_ref[t, at, :]
            si[t] = kept * ti + feed_ref[tiles + t, at, :]
            states_ref[t, at, :] = sr[t]
            states_ref[tiles + t, at, :] = si[t]

    lane = lax.broadcasted_iota(jnp.int32, (ROWS, GROUP), 1)

    def group_norm(r):
        held = jnp.zeros((ROWS, GROUP), F32)
        for g in range(width // GROUP):
            cols = slice(g * GROUP, (g + 1) * GROUP)
            v = gate_ref[r, cols] * states_ref[g, r, :]
            centre = v - jnp.mean(v, axis=1, keepdims=True)
            scale = lax.rsqrt(jnp.mean(centre * centre, axis=1, keepdims=True) + EPS)
            gn = centre * scale
            gn_ref[r, cols] = gn
            gated_ref[r, cols] = (gn * p_ref[1:2, cols]).astype(BF16)
            held = jnp.where(lane == g, scale, held)
        rg_ref[r, :] = held

    over_rows(rows, group_norm)
    load_wait(pairs, sem)
    after_ref[...] = x_ref[...].astype(F32) + dot(gated_ref[...], out_ref[...])

    def norm(r):
        after = after_ref[r, :]
        scale = lax.rsqrt(jnp.mean(after * after, axis=1, keepdims=True) + EPS)
        lifted_ref[r, :] = (after * scale * p_ref[2:3, :]).astype(BF16)

    over_rows(rows, norm)


def mid(plan, me, x, params, gate, kept, feed, sub, every, weights):
    rows, width = x.shape
    half = width // 2
    return pl.pallas_call(
        functools.partial(mid_kernel, plan, len(weights)),
        out_shape=(
            sds((width // GROUP, rows, GROUP)),
            sds((2, SUB, half)),
            sds((rows, width)),
            sds((rows, GROUP)),
            sds((rows, width), BF16),
            sds((rows, width)),
            sds((rows, width), BF16),
        ),
        in_specs=[SMEM] + [VMEM] * 7 + [ANY] * len(weights),
        out_specs=(VMEM,) * 7,
        scratch_shapes=[pltpu.VMEM((width, width), BF16), pltpu.SemaphoreType.DMA],
        compiler_params=pltpu.CompilerParams(vmem_limit_bytes=56 << 20),
        cost_estimate=pl.CostEstimate(flops=2 * rows * width * width, bytes_accessed=8 << 20, transcendentals=0),
        name="mid",
    )(me, x, params, gate, kept, feed, sub, every, *weights)


def ffn_kernel(plan, count, me_ref, after_ref, lifted_ref, *refs):
    w_hbm, refs = refs[:count], refs[count:]
    both_ref, hidden_ref, next_ref, up_ref, down_ref, sems = refs
    inner = hidden_ref.shape[1]
    up_pairs = pairs_of(plan, w_hbm, me_ref, "up", up_ref)
    down_pairs = pairs_of(plan, w_hbm, me_ref, "down", down_ref)
    load_start(up_pairs, sems.at[0])
    load_start(down_pairs, sems.at[1])
    load_wait(up_pairs, sems.at[0])
    lifted = lifted_ref[...]
    step = after_ref.shape[1] // 2
    for k in range(inner // step):
        cols = slice(k * step, (k + 1) * step)
        more = slice(inner + k * step, inner + (k + 1) * step)
        a = dot(lifted, up_ref[:, cols])
        b = dot(lifted, up_ref[:, more])
        both_ref[:, cols] = a
        both_ref[:, more] = b
        hidden_ref[:, cols] = (a * jax.nn.sigmoid(a) * b).astype(BF16)
    load_wait(down_pairs, sems.at[1])
    next_ref[...] = (after_ref[...] + dot(hidden_ref[...], down_ref[...])).astype(next_ref.dtype)


def ffn(plan, me, after, lifted, weights, dtype):
    rows, width = after.shape
    inner = 2 * width
    return pl.pallas_call(
        functools.partial(ffn_kernel, plan, len(weights)),
        out_shape=(sds((rows, 2 * inner)), sds((rows, inner), BF16), sds((rows, width), dtype)),
        in_specs=[SMEM] + [VMEM] * 2 + [ANY] * len(weights),
        out_specs=(VMEM,) * 3,
        scratch_shapes=[
            pltpu.VMEM((width, 2 * inner), BF16),
            pltpu.VMEM((inner, width), BF16),
            pltpu.SemaphoreType.DMA((2,)),
        ],
        compiler_params=pltpu.CompilerParams(vmem_limit_bytes=56 << 20),
        cost_estimate=pl.CostEstimate(flops=2 * rows * width * 6 * width, bytes_accessed=14 << 20, transcendentals=0),
        name="ffn",
    )(me, after, lifted, *weights)


def back_ffn_kernel(plan, count, me_ref, dx_ref, p_ref, both_ref, after_ref, *refs):
    w_hbm, refs = refs[:count], refs[count:]
    dlow_ref, dboth_ref, dafter_ref, dmid_ref, gain_ref, work_ref, up_ref, down_ref, sems = refs
    rows, width = dx_ref.shape
    inner = down_ref.shape[0]
    up_pairs = pairs_of(plan, w_hbm, me_ref, "up", up_ref)
    down_pairs = pairs_of(plan, w_hbm, me_ref, "down", down_ref)
    load_start(down_pairs, sems.at[1])
    load_start(up_pairs, sems.at[0])
    if dx_ref.dtype == BF16:
        at = lax.broadcasted_iota(jnp.int32, (rows, GROUP), 0)
        live = at < me_ref[4]
        for t in range(width // GROUP):
            cols = slice(t * GROUP, (t + 1) * GROUP)
            dlow_ref[:, cols] = jnp.where(live, dx_ref[:, cols].astype(F32), 0.0).astype(BF16)
        grad_ref = dlow_ref
    else:
        dlow_ref[...] = dx_ref[...].astype(BF16)
        grad_ref = dx_ref
    dlow = dlow_ref[...]
    load_wait(down_pairs, sems.at[1])
    step = width // 2
    for k in range(inner // step):
        cols = slice(k * step, (k + 1) * step)
        more = slice(inner + k * step, inner + (k + 1) * step)
        dh = dot_t(dlow, down_ref[cols, :])
        a = both_ref[:, cols]
        sig = jax.nn.sigmoid(a)
        dboth_ref[:, cols] = (dh * both_ref[:, more] * (sig * (1.0 + a * (1.0 - sig)))).astype(BF16)
        dboth_ref[:, more] = (dh * (a * sig)).astype(BF16)
    load_wait(up_pairs, sems.at[0])
    work_ref[...] = dot_t(dboth_ref[...], up_ref[...])

    def norm_back(r):
        after = after_ref[r, :]
        scale = lax.rsqrt(jnp.mean(after * after, axis=1, keepdims=True) + EPS)
        normal = after * scale
        lift = work_ref[r, :]
        e = lift * p_ref[2:3, :]
        d = grad_ref[r, :].astype(F32) + scale * (e - normal * jnp.mean(e * normal, axis=1, keepdims=True))
        dafter_ref[r, :] = d
        dmid_ref[r, :] = d.astype(BF16)
        work_ref[r, :] = lift * normal

    over_rows(rows, norm_back)
    gain_ref[...] = jnp.sum(work_ref[...], axis=0, keepdims=True)


def back_ffn(plan, me, dx, params, both, after, weights):
    rows, width = dx.shape
    inner = 2 * width
    return pl.pallas_call(
        functools.partial(back_ffn_kernel, plan, len(weights)),
        out_shape=(
            sds((rows, width), BF16),
            sds((rows, 2 * inner), BF16),
            sds((rows, width)),
            sds((rows, width), BF16),
            sds((1, width)),
        ),
        in_specs=[SMEM] + [VMEM] * 4 + [ANY] * len(weights),
        out_specs=(VMEM,) * 5,
        scratch_shapes=[
            pltpu.VMEM((rows, width), F32),
            pltpu.VMEM((width, 2 * inner), BF16),
            pltpu.VMEM((inner, width), BF16),
            pltpu.SemaphoreType.DMA((2,)),
        ],
        compiler_params=pltpu.CompilerParams(vmem_limit_bytes=56 << 20),
        cost_estimate=pl.CostEstimate(flops=2 * rows * width * 6 * width, bytes_accessed=14 << 20, transcendentals=0),
        name="back_ffn",
    )(me, dx, params, both, after, *weights)


def back_mid_kernel(
    plan, count, me_ref, dmid_ref, p_ref, gn_ref, rg_ref, gate_ref, states_ref, kept_ref, sub_ref, *refs
):
    w_hbm, refs = refs[:count], refs[count:]
    dgpre_ref, dstates_ref, gain_ref, rsub_ref, rtotal_ref, work_ref, out_ref, sem = refs
    rows, width = dmid_ref.shape
    half = width // 2
    block = rows // SUB
    pairs = pairs_of(plan, w_hbm, me_ref, "out", out_ref)
    load_start(pairs, sem)
    load_wait(pairs, sem)
    work_ref[...] = dot_t(dmid_ref[...], out_ref[...])

    def group_back(r):
        held = rg_ref[r, :]
        for g in range(width // GROUP):
            cols = slice(g * GROUP, (g + 1) * GROUP)
            gn = gn_ref[r, cols]
            dg = work_ref[r, cols]
            e = dg * p_ref[1:2, cols]
            dv = held[:, g : g + 1] * (
                e - jnp.mean(e, axis=1, keepdims=True) - gn * jnp.mean(e * gn, axis=1, keepdims=True)
            )
            gate = gate_ref[r, cols]
            dgpre_ref[r, cols] = (dv * states_ref[g, r, :] * gate * (1.0 - gate)).astype(BF16)
            dstates_ref[g, r, :] = dv * gate
            work_ref[r, cols] = dg * gn

    over_rows(rows, group_back)
    gain_ref[...] = jnp.sum(work_ref[...], axis=0, keepdims=True)

    cos, sin = turns(p_ref, half)
    tiles = half // GROUP
    zr = [jnp.zeros((SUB, GROUP), F32)] * tiles
    zi = [jnp.zeros((SUB, GROUP), F32)] * tiles
    for j in reversed(range(block)):
        at = pl.ds(j, SUB, stride=block)
        for t in range(tiles):
            kept = kept_ref[t, at, :]
            qr = dstates_ref[t, at, :] + zr[t]
            qi = dstates_ref[tiles + t, at, :] + zi[t]
            zr[t] = kept * (cos[t] * qr + sin[t] * qi)
            zi[t] = kept * (cos[t] * qi - sin[t] * qr)
    zr, zi = jnp.concatenate(zr, axis=1), jnp.concatenate(zi, axis=1)
    rsub_ref[0] = zr
    rsub_ref[1] = zi
    tr = jnp.zeros((1, half), F32)
    ti = jnp.zeros((1, half), F32)
    for k in reversed(range(SUB)):
        ar, ai = sub_ref[0, k : k + 1, :], sub_ref[1, k : k + 1, :]
        tr, ti = ar * tr + ai * ti + zr[k : k + 1], ar * ti - ai * tr + zi[k : k + 1]
    rtotal_ref[0:1, :] = tr
    rtotal_ref[1:2, :] = ti


def back_mid(plan, me, dmid, params, gn, rg, gate, states, kept, sub, weights):
    rows, width = dmid.shape
    half = width // 2
    return pl.pallas_call(
        functools.partial(back_mid_kernel, plan, len(weights)),
        out_shape=(
            sds((rows, width), BF16),
            sds((width // GROUP, rows, GROUP)),
            sds((1, width)),
            sds((2, SUB, half)),
            sds((2, half)),
        ),
        in_specs=[SMEM] + [VMEM] * 8 + [ANY] * len(weights),
        out_specs=(VMEM,) * 5,
        scratch_shapes=[
            pltpu.VMEM((rows, width), F32),
            pltpu.VMEM((width, width), BF16),
            pltpu.SemaphoreType.DMA,
        ],
        compiler_params=pltpu.CompilerParams(vmem_limit_bytes=56 << 20),
        cost_estimate=pl.CostEstimate(flops=2 * rows * width * width, bytes_accessed=8 << 20, transcendentals=0),
        name="back_mid",
    )(me, dmid, params, gn, rg, gate, states, kept, sub, *weights)


def back_two_kernel(
    plan, count, me_ref, x_ref, p_ref, dafter_ref, dgpre_ref, dstates_ref, states_ref, kept_ref, rate_ref, cpre_ref,
    first_ref, sub_ref, rsub_ref, every_ref, revery_ref, *refs
):
    w_hbm, refs = refs[:count], refs[count:]
    (
    dmixin_ref, dx_ref, gains_ref,
    work_ref, q_ref, turn_ref, start_ref, w_ref, sem,
    ) = refs
    rows, width = x_ref.shape
    half = width // 2
    block = rows // SUB
    pairs = pairs_of(plan, w_hbm, me_ref, "mix", w_ref)
    load_start(pairs, sem)
    zr = jnp.zeros((1, half), F32)
    zi = jnp.zeros((1, half), F32)
    for k in reversed(range(every_ref.shape[0])):
        at = k ^ me_ref[3]
        ar, ai = every_ref[at, 0:1, :], every_ref[at, 1:2, :]
        later = k > me_ref[0]
        nr = ar * zr + ai * zi + revery_ref[at, 0:1, :]
        ni = ar * zi - ai * zr + revery_ref[at, 1:2, :]
        zr = jnp.where(later, nr, zr)
        zi = jnp.where(later, ni, zi)
    for k in reversed(range(SUB)):
        start_ref[0, k : k + 1, :] = zr
        start_ref[1, k : k + 1, :] = zi
        ar, ai = sub_ref[0, k : k + 1, :], sub_ref[1, k : k + 1, :]
        zr, zi = (
            ar * zr + ai * zi + rsub_ref[0, k : k + 1, :],
            ar * zi - ai * zr + rsub_ref[1, k : k + 1, :],
        )
    cos, sin = turns(p_ref, half)
    tiles = half // GROUP
    zr = parts(start_ref, 0, tiles)
    zi = parts(start_ref, 1, tiles)
    angle = [jnp.zeros((SUB, GROUP), F32)] * tiles
    for j in reversed(range(block)):
        at = pl.ds(j, SUB, stride=block)
        before = pl.ds(max(j - 1, 0), SUB, stride=block)
        for t in range(tiles):
            kept = kept_ref[t, at, :]
            qr = dstates_ref[t, at, :] + zr[t]
            qi = dstates_ref[tiles + t, at, :] + zi[t]
            q_ref[t, at, :] = qr
            q_ref[tiles + t, at, :] = qi
            zr[t] = kept * (cos[t] * qr + sin[t] * qi)
            zi[t] = kept * (cos[t] * qi - sin[t] * qr)
            if j:
                sr, si = states_ref[t, before, :], states_ref[tiles + t, before, :]
            else:
                sr, si = (first_ref[k, :, t * GROUP : (t + 1) * GROUP] for k in range(2))
            turn_ref[t, at, :] = zr[t] * sr + zi[t] * si
            angle[t] = angle[t] + (zi[t] * sr - zr[t] * si)
    gains_ref[1:2, half:] = jnp.sum(jnp.concatenate(angle, axis=1), axis=0, keepdims=True)

    def activations(r):
        for t in range(tiles):
            rate = rate_ref[r, t * GROUP : (t + 1) * GROUP]
            left = 1.0 - rate
            meet = jnp.zeros_like(rate)
            for k in range(2):
                cols = slice((k * tiles + t) * GROUP, (k * tiles + t + 1) * GROUP)
                pre = cpre_ref[r, cols]
                sig = jax.nn.sigmoid(pre)
                q = q_ref[k * tiles + t, r, :]
                meet = meet + q * (pre * sig)
                dmixin_ref[r, cols] = (left * q * (sig * (1.0 + pre * (1.0 - sig)))).astype(BF16)
            dfpre = left * (turn_ref[t, r, :] - rate * meet)
            dmixin_ref[r, 2 * width + t * GROUP : 2 * width + (t + 1) * GROUP] = dfpre.astype(BF16)
            turn_ref[t, r, :] = dfpre
        dmixin_ref[r, width : 2 * width] = dgpre_ref[r, :]

    over_rows(rows, activations)
    for t in range(tiles):
        gains_ref[1:2, t * GROUP : (t + 1) * GROUP] = jnp.sum(turn_ref[t], axis=0, keepdims=True)
    load_wait(pairs, sem)
    work_ref[...] = dot_t(dmixin_ref[...], w_ref[:, : dmixin_ref.shape[1]])

    def norm_back(r):
        x = x_ref[r, :].astype(F32)
        scale = lax.rsqrt(jnp.mean(x * x, axis=1, keepdims=True) + EPS)
        normal = x * scale
        dn = work_ref[r, :]
        e = dn * p_ref[0:1, :]
        dx_ref[r, :] = dafter_ref[r, :] + scale * (e - normal * jnp.mean(e * normal, axis=1, keepdims=True))
        work_ref[r, :] = dn * normal

    over_rows(rows, norm_back)
    gains_ref[0:1, :] = jnp.sum(work_ref[...], axis=0, keepdims=True)


def back_two(plan, me, x, params, dafter, dgpre, dstates, states, kept, rate, cpre, first, sub, rsub, every, revery, weights):
    rows, width = x.shape
    half = width // 2
    return pl.pallas_call(
        functools.partial(back_two_kernel, plan, len(weights)),
        out_shape=(
            sds((rows, 2 * width + half), BF16),
            sds((rows, width)),
            sds((2, width)),
        ),
        in_specs=[SMEM] + [VMEM] * 14 + [ANY] * len(weights),
        out_specs=(VMEM,) * 3,
        scratch_shapes=[
            pltpu.VMEM((rows, width), F32),
            pltpu.VMEM((width // GROUP, rows, GROUP), F32),
            pltpu.VMEM((half // GROUP, rows, GROUP), F32),
            pltpu.VMEM((2, SUB, half), F32),
            pltpu.VMEM((width, mix_width(plan, width)), BF16),
            pltpu.SemaphoreType.DMA,
        ],
        compiler_params=pltpu.CompilerParams(vmem_limit_bytes=56 << 20),
        cost_estimate=pl.CostEstimate(flops=2 * rows * width * 5 * half, bytes_accessed=10 << 20, transcendentals=0),
        name="back_two",
    )(me, x, params, dafter, dgpre, dstates, states, kept, rate, cpre, first, sub, rsub, every, revery, *weights)


def row_product(left, right):
    return lax.dot_general(left, right, (((0,), (0,)), ((), ())), preferred_element_type=F32)


def export(info_ref, rels, name, grad, column, columns, keep_ref, send_ref, sem):
    chip, core = info_ref[1], info_ref[2]
    pairs = []
    for half, target in ((1 - core, send_ref), (core, keep_ref)):
        for b, (zero, one) in enumerate(zip(*rels)):
            block = chip ^ (zero + half * (one - zero))
            if name == "down":
                row, left = block * (2 * UNIT) + half * UNIT, 0
            else:
                row, left = block * UNIT, half * HALVES[name]
            pairs.append(
                (
                    grad.at[pl.ds(pl.multiple_of(row, UNIT), UNIT), pl.ds(pl.multiple_of(left, GROUP), columns)],
                    target.at[b, :, pl.ds(column, columns)],
                )
            )
    load_start(pairs, sem)
    return pairs


def products(left, right_ref, grad_ref, size):
    step = HALVES["out"]
    for k in range(size // step):
        cols = slice(k * step, (k + 1) * step)
        grad_ref[:, cols] = row_product(left, right_ref[:, cols]).astype(BF16)


def grad_ud_kernel(
    rels, info_ref, lifted_ref, dboth_ref, hidden_ref, dlow_ref, keep_ref, send_ref, up_ref, down_ref, sem
):
    width = dlow_ref.shape[1]
    products(hidden_ref[...], dlow_ref, down_ref, width)
    pairs = export(info_ref, rels, "down", down_ref, HALVES["up"], width, keep_ref, send_ref, sem)
    products(lifted_ref[...], dboth_ref, up_ref, up_ref.shape[1])
    pairs += export(info_ref, rels, "up", up_ref, 0, HALVES["up"], keep_ref, send_ref, sem)
    load_wait(pairs, sem)


def grad_ud(rels, info, lifted, dboth, hidden, dlow):
    rows, width = dlow.shape
    inner = hidden.shape[1]
    shape = sds((len(rels[0]), UNIT, HALVES["up"] + width), BF16)
    return pl.pallas_call(
        functools.partial(grad_ud_kernel, rels),
        out_shape=(shape, shape),
        in_specs=[SMEM] + [VMEM] * 4,
        out_specs=(ANY, ANY),
        scratch_shapes=[
            pltpu.VMEM((width, 2 * inner), BF16),
            pltpu.VMEM((inner, width), BF16),
            pltpu.SemaphoreType.DMA,
        ],
        compiler_params=pltpu.CompilerParams(vmem_limit_bytes=56 << 20),
        cost_estimate=pl.CostEstimate(flops=2 * rows * width * 6 * width, bytes_accessed=12 << 20, transcendentals=0),
        name="grad_ud",
    )(info, lifted, dboth, hidden, dlow)


def grad_mo_kernel(rels, info_ref, gated_ref, dmid_ref, normed_ref, dmixin_ref, *refs):
    extra, (keep_ref, send_ref, out_ref, mix_ref, held_ref, sem) = refs[:-6], refs[-6:]
    width = dmid_ref.shape[1]
    products(gated_ref[...], dmid_ref, out_ref, width)
    pairs = export(info_ref, rels, "out", out_ref, HALVES["mix"], HALVES["out"], keep_ref, send_ref, sem)
    size = dmixin_ref.shape[1]
    held_ref[...] = jnp.zeros_like(held_ref)
    for k in range(len(extra) // 3):
        two, mid_gain, ffn_gain = extra[3 * k : 3 * k + 3]
        held_ref[4 * k : 4 * k + 1, :] = two[0:1, :]
        held_ref[4 * k + 1 : 4 * k + 2, :] = mid_gain[...]
        held_ref[4 * k + 2 : 4 * k + 3, :] = ffn_gain[...]
        held_ref[4 * k + 3 : 4 * k + 4, :] = two[1:2, :]
    mix_ref[:, size:] = jnp.transpose(held_ref[...]).astype(BF16)
    products(normed_ref[...], dmixin_ref, mix_ref, size)
    pairs += export(info_ref, rels, "mix", mix_ref, 0, HALVES["mix"], keep_ref, send_ref, sem)
    load_wait(pairs, sem)


def grad_mo(rels, info, gated, dmid, normed, dmixin, extra):
    rows, width = normed.shape
    shape = sds((len(rels[0]), UNIT, HALVES["mix"] + HALVES["out"]), BF16)
    return pl.pallas_call(
        functools.partial(grad_mo_kernel, rels),
        out_shape=(shape, shape),
        in_specs=[SMEM] + [VMEM] * (4 + len(extra)),
        out_specs=(ANY, ANY),
        scratch_shapes=[
            pltpu.VMEM((width, width), BF16),
            pltpu.VMEM((width, 2 * HALVES["mix"]), BF16),
            pltpu.VMEM((GROUP, width), F32),
            pltpu.SemaphoreType.DMA,
        ],
        compiler_params=pltpu.CompilerParams(vmem_limit_bytes=56 << 20),
        cost_estimate=pl.CostEstimate(flops=7 * rows * width * width, bytes_accessed=6 << 20, transcendentals=0),
        name="grad_mo",
    )(info, gated, dmid, normed, dmixin, *extra)


def table_kernel(plan, count, me_ref, *refs):
    sources, (table_ref, held_ref, sem) = refs[:count], refs[count:]
    pairs = pairs_of(plan, sources, me_ref, "small", held_ref)
    load_start(pairs, sem)
    load_wait(pairs, sem)
    depth = table_ref.shape[0]
    half = table_ref.shape[2] // 2
    table = jnp.transpose(held_ref[:, GROUP:].astype(F32))
    table_ref[...] = jnp.zeros_like(table_ref)
    for l in range(depth):
        chan = table[3 * depth + l : 3 * depth + l + 1]
        table_ref[l, 0:3, :] = table[3 * l : 3 * l + 3]
        table_ref[l, 3:4, :half] = chan[:, :half]
        table_ref[l, 3:4, half:] = jnp.cos(chan[:, half:])
        table_ref[l, 4:5, :half] = jnp.sin(chan[:, half:])


def table_of(plan, me, weights, depth, width):
    return pl.pallas_call(
        functools.partial(table_kernel, plan, len(weights)),
        out_shape=sds((depth, 8, width)),
        in_specs=[SMEM] + [ANY] * len(weights),
        out_specs=VMEM,
        scratch_shapes=[pltpu.VMEM((width, 2 * GROUP), BF16), pltpu.SemaphoreType.DMA],
        compiler_params=pltpu.CompilerParams(vmem_limit_bytes=16 << 20),
        cost_estimate=pl.CostEstimate(flops=1 << 20, bytes_accessed=1 << 20, transcendentals=0),
        name="table",
    )(me, *weights)


def swap(x, bits):
    count = lax.axis_size("dp") * lax.axis_size("seq")
    return lax.ppermute(x, ALL, [(i, i ^ bits[i % 2]) for i in range(count)])


def hold(values, *after):
    return lax.optimization_barrier(tuple(values) + after)[: len(values)]


def rels_of(stages):
    rels = ([0], [0])
    for bits in stages:
        for core in range(2):
            rels[core].extend([rel ^ bits[core] for rel in rels[core]])
    return rels


class Spread:
    def __init__(self, unit, stages):
        self.held, self.stages, self.at = unit[None], stages, 0
        self.got = None

    def join(self):
        if self.got is not None:
            self.held = jnp.concatenate([self.held, self.got])

    def next(self):
        self.join()
        one, two = self.stages[self.at]
        self.at += 1
        self.got = swap(self.held, (2 * one, 2 * two))

    def end(self):
        self.near, self.last = self.held, self.got
        self.last_core = swap(self.last, (1, 1))

    def near_core(self):
        self.held_core = swap(self.held, (1, 1))

    def arrays(self):
        return (self.near, self.held_core, self.last, self.last_core)

    def sources(self):
        rels = rels_of(self.stages)
        half = len(rels[0]) // 2
        low = tuple(tuple(rel[:half]) for rel in rels)
        high = tuple(tuple(rel[half:]) for rel in rels)
        return ((0, low), (1, low), (0, high), (1, high))


class Reduce:
    def __init__(self, keep, send, stages):
        self.held, self.stages = keep, list(stages)
        self.got = swap(send, (1, 1))

    def add(self):
        half = self.held.shape[0] // 2
        if not half:
            return self.held[0].astype(F32) + self.got[0].astype(F32)

        def joined(part):
            return (self.held[part].astype(F32) + self.got[part].astype(F32)).astype(BF16)

        self.low, self.high = joined(slice(0, half)), joined(slice(half, None))

    def next(self):
        self.add()
        one, two = self.stages.pop()
        self.got = swap(self.high, (2 * one, 2 * two))
        self.held = self.low


def exchange(x):
    pair = jnp.stack([x, swap(x, (1, 1))])
    got = [swap(pair, (k, k)) for k in range(2, lax.axis_size("seq"), 2)]
    return jnp.concatenate([pair] + got)


def finish_kernel(info_ref, *refs):
    depth = (len(refs) - 5) // 3
    mine, other, downs = refs[:depth], refs[depth : 2 * depth], refs[2 * depth : 3 * depth]
    mix_ref, out_ref, up_ref, down_ref, tail_ref = refs[3 * depth :]
    width = down_ref.shape[2]
    mix_cols = mix_ref.shape[2]
    size = HALVES["mix"]

    def place(first, second):
        for l in range(depth):
            mix_ref[l, :, :size] = first[l][:, :size]
            mix_ref[l, :, size:] = second[l][:, : mix_cols - size]
            at = size
            for name, ref in (("out", out_ref), ("up", up_ref)):
                step = HALVES[name]
                ref[l, :, :step] = first[l][:, at : at + step]
                ref[l, :, step:] = second[l][:, at : at + step]
                at += step
        tail_ref[...] = second[0][:, size - GROUP : size]

    @pl.when(info_ref[2] == 0)
    def _():
        place(mine, other)

    @pl.when(info_ref[2] == 1)
    def _():
        place(other, mine)

    for l in range(depth):
        down_ref[l] = downs[l][:, downs[l].shape[1] - width :]


def finish(info, mine, other, downs, shapes):
    share = mine[0].shape[0]
    return pl.pallas_call(
        finish_kernel,
        out_shape=tuple(sds(shape) for shape in shapes) + (sds((share, GROUP)),),
        in_specs=[SMEM] + [VMEM] * (3 * len(mine)),
        out_specs=(VMEM,) * 5,
        compiler_params=pltpu.CompilerParams(vmem_limit_bytes=32 << 20),
        cost_estimate=pl.CostEstimate(flops=1 << 20, bytes_accessed=6 << 20, transcendentals=0),
        name="finish",
    )(info, *mine, *other, *downs)


def layer_params(gains, chan):
    half = chan.shape[0] // 2
    angle = chan[half:]
    rows = [
        gains[0],
        gains[1],
        gains[2],
        jnp.concatenate([chan[:half], jnp.cos(angle)]),
        jnp.concatenate([jnp.sin(angle), jnp.zeros((half,), F32)]),
    ]
    return jnp.concatenate([jnp.stack(rows), jnp.zeros((3, 2 * half), F32)], axis=0)


STAGES = ((4, 8), (8, 4), (1, 2), (2, 1))


def small_of(gains, chan_params):
    depth, _, share = gains.shape
    return jnp.concatenate(
        [gains.reshape(depth * 3, share).T, chan_params.T, jnp.zeros((share, GROUP - 4 * depth), BF16)], axis=1
    )


def info_of(lengths, rows, turned):
    where = lax.axis_index("seq")
    base = where * rows
    ends = [lengths[0, 0]]
    for j in range(1, lengths.shape[1]):
        ends.append(ends[-1] + lengths[0, j])
    chip = (lax.axis_index("dp") * lax.axis_size("seq") + where) // 2
    values = [where, chip, where % 2, where if turned else jnp.zeros_like(where), ends[-1] - base]
    values += [end - lengths[0, j] - base for j, end in enumerate(ends)]
    return jnp.stack([value.astype(jnp.int32) for value in values])


def plain_body(stream, w_mix, w_out, w_up, w_down, gains, chan_params, lengths, cotangent):
    rows, width = stream.shape
    depth = w_mix.shape[0]
    info = info_of(lengths, rows, False)
    small = small_of(gains, chan_params)
    table = lax.all_gather(small, ALL, axis=0, tiled=True)[:, : 4 * depth].T.astype(F32)
    params = [layer_params(table[3 * l : 3 * l + 3], table[3 * depth + l]) for l in range(depth)]
    weights = [
        tuple(lax.all_gather(w[l], ALL, axis=0, tiled=True) for w in (w_mix, w_out, w_up, w_down))
        for l in range(depth)
    ]
    x = stream
    saved = []
    for l in range(depth):
        head = front(None, info, x, params[l], weights[l])
        every = lax.all_gather(head[-1], "seq")
        middle = mid(None, info, x, params[l], head[2], head[4], head[5], head[6], every, weights[l])
        tail = ffn(None, info, middle[5], middle[6], weights[l], F32)
        saved.append((x, every, head, middle, tail))
        x = tail[-1]
    mixed = x.astype(BF16)
    dx = cotangent
    sums = [None] * depth
    for l in reversed(range(depth)):
        x, every, (normed, cpre, gate, rate, kept, feed, sub, _), middle, (both, hidden, _) = saved[l]
        states, first, gn, rg, gated, after, lifted = middle
        dlow, dboth, dafter, dmid, ffn_gain = back_ffn(None, info, dx, params[l], both, after, weights[l])
        dgpre, dstates, mid_gain, rsub, rtotal = back_mid(
            None, info, dmid, params[l], gn, rg, gate, states, kept, sub, weights[l]
        )
        revery = lax.all_gather(rtotal, "seq")
        dmixin, dx, gains_b = back_two(
            None, info, x, params[l], dafter, dgpre, dstates, states, kept, rate, cpre, first, sub, rsub, every, revery,
            weights[l],
        )
        grads = [row_product(normed, dmixin), row_product(gated, dmid), row_product(lifted, dboth), row_product(hidden, dlow)]
        grads.append(jnp.stack([gains_b[0], mid_gain[0], ffn_gain[0], gains_b[1]], axis=1))
        sums[l] = [lax.psum_scatter(g.astype(BF16), ALL, scatter_dimension=0, tiled=True).astype(F32) for g in grads]
    outs = [jnp.stack([sums[l][k] for l in range(depth)]) for k in range(5)]
    tail = outs.pop()
    return (mixed, dx, *outs, jnp.swapaxes(tail[:, :, :3], 1, 2), tail[:, :, 3])


def fast_body(stream, w_mix, w_out, w_up, w_down, gains, chan_params, lengths, cotangent):
    rows, width = stream.shape
    depth, share, mix_cols = w_mix.shape
    info = info_of(lengths, rows, True)
    small = small_of(gains, chan_params)
    core = lax.axis_index("seq") % 2
    padding = jnp.zeros((share, 2 * HALVES["mix"] - mix_cols - GROUP), BF16)
    halves = ([], [])
    for l in range(depth):
        mix = jnp.concatenate([w_mix[l], padding, small if l == 0 else jnp.zeros_like(small)], axis=1)
        for h in range(2):
            for w, size in ((mix, HALVES["mix"]), (w_out[l], HALVES["out"]), (w_up[l], HALVES["up"])):
                halves[h].append(w[:, h * size : (h + 1) * size])
    halves = [jnp.concatenate(half, axis=1) for half in halves]
    mine = jnp.where(core == 0, halves[0], halves[1])
    other = swap(jnp.where(core == 0, halves[1], halves[0]), (1, 1))
    units = jnp.where(core == 0, jnp.concatenate([mine, other]), jnp.concatenate([other, mine]))
    joint = HALVES["mix"] + HALVES["out"]
    size = joint + HALVES["up"]
    mos, uds = [], []
    for l in range(depth):
        unit = units[:, l * size : (l + 1) * size]
        mos.append(Spread(unit[:, :joint], STAGES))
        uds.append(Spread(jnp.concatenate([unit[:, joint:], w_down[l]], axis=1), STAGES))
    rels = rels_of(STAGES)
    plan = {
        "sources": mos[0].sources(),
        "mix": (0, HALVES["mix"]),
        "out": (HALVES["mix"], HALVES["out"]),
        "small": (HALVES["mix"] - GROUP, GROUP),
        "up": (0, HALVES["up"]),
        "down": (HALVES["up"], width),
    }

    x = stream
    saved = []
    mo, ud = mos[0], uds[0]
    mo.next()
    mo.next()
    (ud.held,) = hold((ud.held,), mo.held)
    ud.next()
    mo.next()
    (ud.got,) = hold((ud.got,), mo.held)
    ud.next()
    mo.next()
    mo.near_core()
    mo.end()
    params = table_of(plan, info, mo.arrays(), depth, width)
    for l in range(depth):
        mo, ud = mos[l], uds[l]
        (ud.got,) = hold((ud.got,), mo.last)
        ud.next()
        if l + 1 < depth:
            (mos[l + 1].held,) = hold((mos[l + 1].held,), ud.held)
            mos[l + 1].next()
        head = front(plan, info, x, params[l], mo.arrays())
        every = exchange(head[-1])
        (ud.got,) = hold((ud.got,), every)
        ud.next()
        ud.near_core()
        if l + 1 < depth:
            (mos[l + 1].got,) = hold((mos[l + 1].got,), ud.held)
            mos[l + 1].next()
        middle = mid(plan, info, x, params[l], head[2], head[4], head[5], head[6], every, mo.arrays())
        (ud.got,) = hold((ud.got,), middle[-1])
        ud.end()
        if l + 1 < depth:
            (mos[l + 1].got,) = hold((mos[l + 1].got,), ud.last)
            mos[l + 1].next()
            (uds[l + 1].held,) = hold((uds[l + 1].held,), mos[l + 1].held)
            uds[l + 1].next()
        tail = ffn(plan, info, middle[5], middle[6], ud.arrays(), F32 if l + 1 < depth else BF16)
        saved.append((x, every, head, middle, tail))
        x = tail[-1]
        if l + 1 < depth:
            (mos[l + 1].got,) = hold((mos[l + 1].got,), x)
            mos[l + 1].next()
            mos[l + 1].near_core()
            (uds[l + 1].got,) = hold((uds[l + 1].got,), mos[l + 1].held)
            uds[l + 1].next()
            mos[l + 1].end()
    mixed = x
    dx = cotangent
    sums = [None] * depth
    extra = ()
    for l in reversed(range(depth)):
        x, every, (normed, cpre, gate, rate, kept, feed, sub, _), middle, (both, hidden, _) = saved[l]
        states, first, gn, rg, gated, after, lifted = middle
        dlow, dboth, dafter, dmid, ffn_gain = back_ffn(plan, info, dx, params[l], both, after, uds[l].arrays())
        above = sums[l + 1] if l + 1 < depth else None
        if above:
            above[0].got, above[1].got = hold((above[0].got, above[1].got), dlow)
            above[1].next()
            above[0].next()
            (lifted,) = hold((lifted,), above[1].high)
        ud = Reduce(*grad_ud(rels, info, lifted, dboth, hidden, dlow), STAGES)
        (dmid,) = hold((dmid,), ud.held)
        dgpre, dstates, mid_gain, rsub, rtotal = back_mid(
            plan, info, dmid, params[l], gn, rg, gate, states, kept, sub, mos[l].arrays()
        )
        revery = exchange(rtotal)
        (ud.got,) = hold((ud.got,), rtotal)
        if above:
            above[1].got, above[0].got = hold((above[1].got, above[0].got), rtotal)
            above[1].next()
            above[0].next()
        ud.next()
        (dstates,) = hold((dstates,), ud.high)
        dmixin, dx, gains_b = back_two(
            plan, info, x, params[l], dafter, dgpre, dstates, states, kept, rate, cpre, first, sub, rsub, every, revery,
            mos[l].arrays(),
        )
        extra = (gains_b, mid_gain, ffn_gain) + extra
        if above:
            above[1].got, above[0].got = hold((above[1].got, above[0].got), dmixin)
            above[0].next()
        mo = Reduce(*grad_mo(rels, info, gated, dmid, normed, dmixin, extra if l == 0 else ()), STAGES)
        (ud.got,) = hold((ud.got,), mo.held)
        ud.next()
        mo.next()
        if l:
            (dx,) = hold((dx,), mo.high, ud.high)
        sums[l] = (mo, ud)
    mo, ud = sums[0]
    mo.next()
    ud.next()
    mo.next()
    ud.next()
    mo.next()
    mine, other, downs = [], [], []
    for mo, ud in sums:
        ready = ud.add()
        line = jnp.concatenate([mo.add(), ready[:, : HALVES["up"]]], axis=1)
        first, second = line[:share], line[share:]
        mine.append(jnp.where(core == 0, first, second))
        other.append(swap(jnp.where(core == 0, second, first), (1, 1)))
        downs.append(ready)
    shapes = (w_mix.shape, w_out.shape, w_up.shape, w_down.shape)
    *grads, tail = finish(info, mine, other, downs, shapes)
    tail = tail[:, : 4 * depth].T.reshape(depth, 4, share)
    return (mixed, dx, *grads, tail[:, :3], tail[:, 3])


def body(stream, w_mix, *others):
    n_dp, n_seq = lax.axis_size("dp"), lax.axis_size("seq")
    fast = n_seq == 8 and n_dp & (n_dp - 1) == 0 and 2 * w_mix.shape[1] == UNIT
    return (fast_body if fast else plain_body)(stream, w_mix, *others)


def solution(mesh):
    placed = (
        P(ALL, None),
        P(None, ALL, None),
        P(None, ALL, None),
        P(None, ALL, None),
        P(None, ALL, None),
        P(None, None, ALL),
        P(None, ALL),
        P("dp", None),
        P(ALL, None),
    )
    return jax.shard_map(
        body,
        mesh=mesh,
        in_specs=placed,
        out_specs=(
            P(ALL, None),
            P(ALL, None),
            P(None, ALL, None),
            P(None, ALL, None),
            P(None, ALL, None),
            P(None, ALL, None),
            P(None, None, ALL),
            P(None, ALL),
        ),
        check_vma=False,
    )
```

```python
import functools

import jax
import jax.numpy as jnp
from jax import lax
from jax.experimental import pallas as pl
from jax.experimental.pallas import tpu as pltpu
from jax.sharding import PartitionSpec as P

GROUP = 128
EPS = 1e-06
SUB = 8
UNIT = 48
HALVES = {"mix": 1024, "out": 384, "up": 1536}
ROWS = 32
F32 = jnp.float32
BF16 = jnp.bfloat16
ALL = ("dp", "seq")
VMEM = pl.BlockSpec(memory_space=pltpu.VMEM)
SMEM = pl.BlockSpec(memory_space=pltpu.SMEM)
ANY = pl.BlockSpec(memory_space=pl.ANY)
COST = pl.CostEstimate(flops=1000, bytes_accessed=1000, transcendentals=0)


def sds(shape, dtype=F32):
    return jax.ShapeDtypeStruct(shape, dtype)


def over_rows(total, body):
    def step(i, _):
        body(pl.ds(pl.multiple_of(i * ROWS, ROWS), ROWS))
        return 0

    lax.fori_loop(0, total // ROWS, step, 0)


def dot(left, right):
    return jnp.dot(left, right, preferred_element_type=F32)


def dot_t(left, right):
    return lax.dot_general(left, right, (((1,), (1,)), ((), ())), preferred_element_type=F32)


def cmul(ar, ai, br, bi):
    return ar * br - ai * bi, ar * bi + ai * br


def power(cos, sin, times):
    while times > 1:
        cos, sin = cos * cos - sin * sin, 2.0 * cos * sin
        times //= 2
    return cos, sin


def turns(p_ref, half):
    cos, sin = p_ref[3:4, half:], p_ref[4:5, :half]
    return tuple(
        [jnp.broadcast_to(part[:, t * GROUP : (t + 1) * GROUP], (SUB, GROUP)) for t in range(half // GROUP)]
        for part in (cos, sin)
    )


def parts(ref, k, tiles):
    return [ref[k, :, t * GROUP : (t + 1) * GROUP] for t in range(tiles)]


def mix_width(plan, width):
    return 2 * width + width // 2 if plan is None else 2 * HALVES["mix"]


def load_start(pairs, sem):
    for source, target in pairs:
        pltpu.make_async_copy(source, target, sem).start()


def load_wait(pairs, sem):
    for source, target in pairs:
        pltpu.make_async_copy(source, target, sem).wait()


def pairs_of(plan, sources, me_ref, name, target):
    if plan is None:
        return [(sources[{"mix": 0, "out": 1, "up": 2, "down": 3}[name]], target)]
    chip, core = me_ref[1], me_ref[2]
    column, columns = plan[name]
    pairs = []
    for source, (other_core, rels) in enumerate(plan["sources"]):
        half = core ^ other_core
        for b, (zero, one) in enumerate(zip(*rels)):
            block = chip ^ (zero + half * (one - zero))
            if name == "down":
                row, left = block * (2 * UNIT) + half * UNIT, 0
            elif name == "small":
                row, left = block * UNIT, half * GROUP
            else:
                row, left = block * UNIT, half * HALVES[name]
            to = target.at[pl.ds(pl.multiple_of(row, UNIT), UNIT), pl.ds(pl.multiple_of(left, GROUP), columns)]
            pairs.append((sources[source].at[b, :, pl.ds(column, columns)], to))
    return pairs


def front_kernel(
    plan, count, me_ref, x_ref, p_ref, *refs
):
    w_hbm, refs = refs[:count], refs[count:]
    (
    normed_ref, cpre_ref, gate_ref, rate_ref, kept_ref, feed_ref, sub_ref, total_ref,
    w_ref, sem,
    ) = refs
    rows, width = x_ref.shape
    half = width // 2
    block = rows // SUB
    pairs = pairs_of(plan, w_hbm, me_ref, "mix", w_ref)
    load_start(pairs, sem)

    def norm(r):
        x = x_ref[r, :].astype(F32)
        scale = lax.rsqrt(jnp.mean(x * x, axis=1, keepdims=True) + EPS)
        normed_ref[r, :] = (x * scale * p_ref[0:1, :]).astype(BF16)

    over_rows(rows, norm)
    load_wait(pairs, sem)
    normed = normed_ref[...]
    rate = jax.nn.sigmoid(dot(normed, w_ref[:, 2 * width : 2 * width + half]) + p_ref[3:4, :half])
    rate_ref[...] = rate
    at = lax.broadcasted_iota(jnp.int32, (rows, GROUP), 0)
    fresh = at == me_ref[5]
    for j in range(6, me_ref.shape[0]):
        fresh = jnp.logical_or(fresh, at == me_ref[j])
    tiles = half // GROUP
    for t in range(tiles):
        kept_ref[t] = jnp.where(fresh, 0.0, rate[:, t * GROUP : (t + 1) * GROUP])
    for k in range(2):
        cols = slice(k * half, (k + 1) * half)
        pre = dot(normed, w_ref[:, cols])
        cpre_ref[:, cols] = pre
        feed = (1.0 - rate_ref[...]) * (pre * jax.nn.sigmoid(pre))
        for t in range(tiles):
            feed_ref[k * tiles + t] = feed[:, t * GROUP : (t + 1) * GROUP]
    cos, sin = turns(p_ref, half)

    mag = [jnp.ones((SUB, GROUP), F32)] * tiles
    br = [jnp.zeros((SUB, GROUP), F32)] * tiles
    bi = [jnp.zeros((SUB, GROUP), F32)] * tiles
    for j in range(block):
        at = pl.ds(j, SUB, stride=block)
        for t in range(tiles):
            kept = kept_ref[t, at, :]
            tr, ti = cmul(cos[t], sin[t], br[t], bi[t])
            br[t] = kept * tr + feed_ref[t, at, :]
            bi[t] = kept * ti + feed_ref[tiles + t, at, :]
            mag[t] = mag[t] * kept
    mag, br, bi = (jnp.concatenate(part, axis=1) for part in (mag, br, bi))
    far_cos, far_sin = power(jnp.concatenate(cos, axis=1), jnp.concatenate(sin, axis=1), block)
    ar, ai = mag * far_cos, mag * far_sin
    sub_ref[0] = ar
    sub_ref[1] = ai
    sub_ref[2] = br
    sub_ref[3] = bi
    one_r, one_i, sum_r, sum_i = (part[0:1] for part in (ar, ai, br, bi))
    for k in range(1, SUB):
        kr, ki = ar[k : k + 1], ai[k : k + 1]
        one_r, one_i = cmul(kr, ki, one_r, one_i)
        sum_r, sum_i = cmul(kr, ki, sum_r, sum_i)
        sum_r = sum_r + br[k : k + 1]
        sum_i = sum_i + bi[k : k + 1]
    total_ref[0:1, :] = one_r
    total_ref[1:2, :] = one_i
    total_ref[2:3, :] = sum_r
    total_ref[3:4, :] = sum_i
    for k in range(2):
        cols = slice(width + k * half, width + (k + 1) * half)
        gate_ref[:, k * half : (k + 1) * half] = jax.nn.sigmoid(dot(normed, w_ref[:, cols]))


def front(plan, me, x, params, weights):
    rows, width = x.shape
    half = width // 2
    return pl.pallas_call(
        functools.partial(front_kernel, plan, len(weights)),
        out_shape=(
            sds((rows, width), BF16),
            sds((rows, width)),
            sds((rows, width)),
            sds((rows, half)),
            sds((half // GROUP, rows, GROUP)),
            sds((width // GROUP, rows, GROUP)),
            sds((4, SUB, half)),
            sds((4, half)),
        ),
        in_specs=[SMEM, VMEM, VMEM] + [ANY] * len(weights),
        out_specs=(VMEM,) * 8,
        scratch_shapes=[pltpu.VMEM((width, mix_width(plan, width)), BF16), pltpu.SemaphoreType.DMA],
        compiler_params=pltpu.CompilerParams(vmem_limit_bytes=24 << 20),
        cost_estimate=COST,
        name="front",
    )(me, x, params, *weights)


def mid_kernel(plan, count, me_ref, x_ref, p_ref, gate_ref, kept_ref, feed_ref, sub_ref, every_ref, *refs):
    w_hbm, refs = refs[:count], refs[count:]
    states_ref, first_ref, gn_ref, rg_ref, gated_ref, after_ref, lifted_ref, out_ref, sem = refs
    rows, width = x_ref.shape
    half = width // 2
    block = rows // SUB
    pairs = pairs_of(plan, w_hbm, me_ref, "out", out_ref)
    load_start(pairs, sem)

    sr = jnp.zeros((1, half), F32)
    si = jnp.zeros((1, half), F32)
    for k in range(every_ref.shape[0]):
        at = k ^ me_ref[3]
        nr, ni = cmul(every_ref[at, 0:1, :], every_ref[at, 1:2, :], sr, si)
        earlier = k < me_ref[0]
        sr = jnp.where(earlier, nr + every_ref[at, 2:3, :], sr)
        si = jnp.where(earlier, ni + every_ref[at, 3:4, :], si)
    for k in range(SUB):
        first_ref[0, k : k + 1, :] = sr
        first_ref[1, k : k + 1, :] = si
        nr, ni = cmul(sub_ref[0, k : k + 1, :], sub_ref[1, k : k + 1, :], sr, si)
        sr = nr + sub_ref[2, k : k + 1, :]
        si = ni + sub_ref[3, k : k + 1, :]
    cos, sin = turns(p_ref, half)
    tiles = half // GROUP
    sr = parts(first_ref, 0, tiles)
    si = parts(first_ref, 1, tiles)
    for j in range(block):
        at = pl.ds(j, SUB, stride=block)
        for t in range(tiles):
            kept = kept_ref[t, at, :]
            tr, ti = cmul(cos[t], sin[t], sr[t], si[t])
            sr[t] = kept * tr + feed_ref[t, at, :]
            si[t] = kept * ti + feed_ref[tiles + t, at, :]
            states_ref[t, at, :] = sr[t]
            states_ref[tiles + t, at, :] = si[t]

    lane = lax.broadcasted_iota(jnp.int32, (ROWS, GROUP), 1)

    def group_norm(r):
        held = jnp.zeros((ROWS, GROUP), F32)
        for g in range(width // GROUP):
            cols = slice(g * GROUP, (g + 1) * GROUP)
            v = gate_ref[r, cols] * states_ref[g, r, :]
            centre = v - jnp.mean(v, axis=1, keepdims=True)
            scale = lax.rsqrt(jnp.mean(centre * centre, axis=1, keepdims=True) + EPS)
            gn = centre * scale
            gn_ref[r, cols] = gn
            gated_ref[r, cols] = (gn * p_ref[1:2, cols]).astype(BF16)
            held = jnp.where(lane == g, scale, held)
        rg_ref[r, :] = held

    over_rows(rows, group_norm)
    load_wait(pairs, sem)
    after_ref[...] = x_ref[...].astype(F32) + dot(gated_ref[...], out_ref[...])

    def norm(r):
        after = after_ref[r, :]
        scale = lax.rsqrt(jnp.mean(after * after, axis=1, keepdims=True) + EPS)
        lifted_ref[r, :] = (after * scale * p_ref[2:3, :]).astype(BF16)

    over_rows(rows, norm)


def mid(plan, me, x, params, gate, kept, feed, sub, every, weights):
    rows, width = x.shape
    half = width // 2
    return pl.pallas_call(
        functools.partial(mid_kernel, plan, len(weights)),
        out_shape=(
            sds((width // GROUP, rows, GROUP)),
            sds((2, SUB, half)),
            sds((rows, width)),
            sds((rows, GROUP)),
            sds((rows, width), BF16),
            sds((rows, width)),
            sds((rows, width), BF16),
        ),
        in_specs=[SMEM] + [VMEM] * 7 + [ANY] * len(weights),
        out_specs=(VMEM,) * 7,
        scratch_shapes=[pltpu.VMEM((width, width), BF16), pltpu.SemaphoreType.DMA],
        compiler_params=pltpu.CompilerParams(vmem_limit_bytes=24 << 20),
        cost_estimate=COST,
        name="mid",
    )(me, x, params, gate, kept, feed, sub, every, *weights)


def ffn_kernel(plan, count, me_ref, after_ref, lifted_ref, *refs):
    w_hbm, refs = refs[:count], refs[count:]
    both_ref, hidden_ref, next_ref, up_ref, down_ref, sems = refs
    inner = hidden_ref.shape[1]
    up_pairs = pairs_of(plan, w_hbm, me_ref, "up", up_ref)
    down_pairs = pairs_of(plan, w_hbm, me_ref, "down", down_ref)
    load_start(up_pairs, sems.at[0])
    load_start(down_pairs, sems.at[1])
    load_wait(up_pairs, sems.at[0])
    lifted = lifted_ref[...]
    step = after_ref.shape[1] // 2
    for k in range(inner // step):
        cols = slice(k * step, (k + 1) * step)
        more = slice(inner + k * step, inner + (k + 1) * step)
        a = dot(lifted, up_ref[:, cols])
        b = dot(lifted, up_ref[:, more])
        both_ref[:, cols] = a
        both_ref[:, more] = b
        hidden_ref[:, cols] = (a * jax.nn.sigmoid(a) * b).astype(BF16)
    load_wait(down_pairs, sems.at[1])
    next_ref[...] = (after_ref[...] + dot(hidden_ref[...], down_ref[...])).astype(next_ref.dtype)


def ffn(plan, me, after, lifted, weights, dtype):
    rows, width = after.shape
    inner = 2 * width
    return pl.pallas_call(
        functools.partial(ffn_kernel, plan, len(weights)),
        out_shape=(sds((rows, 2 * inner)), sds((rows, inner), BF16), sds((rows, width), dtype)),
        in_specs=[SMEM] + [VMEM] * 2 + [ANY] * len(weights),
        out_specs=(VMEM,) * 3,
        scratch_shapes=[
            pltpu.VMEM((width, 2 * inner), BF16),
            pltpu.VMEM((inner, width), BF16),
            pltpu.SemaphoreType.DMA((2,)),
        ],
        compiler_params=pltpu.CompilerParams(vmem_limit_bytes=24 << 20),
        cost_estimate=COST,
        name="ffn",
    )(me, after, lifted, *weights)


def back_ffn_kernel(plan, count, me_ref, dx_ref, p_ref, both_ref, after_ref, *refs):
    w_hbm, refs = refs[:count], refs[count:]
    dlow_ref, dboth_ref, dafter_ref, dmid_ref, gain_ref, work_ref, up_ref, down_ref, sems = refs
    rows, width = dx_ref.shape
    inner = down_ref.shape[0]
    up_pairs = pairs_of(plan, w_hbm, me_ref, "up", up_ref)
    down_pairs = pairs_of(plan, w_hbm, me_ref, "down", down_ref)
    load_start(down_pairs, sems.at[1])
    load_start(up_pairs, sems.at[0])
    if dx_ref.dtype == BF16:
        at = lax.broadcasted_iota(jnp.int32, (rows, GROUP), 0)
        live = at < me_ref[4]
        for t in range(width // GROUP):
            cols = slice(t * GROUP, (t + 1) * GROUP)
            dlow_ref[:, cols] = jnp.where(live, dx_ref[:, cols].astype(F32), 0.0).astype(BF16)
        grad_ref = dlow_ref
    else:
        dlow_ref[...] = dx_ref[...].astype(BF16)
        grad_ref = dx_ref
    dlow = dlow_ref[...]
    load_wait(down_pairs, sems.at[1])
    step = width // 2
    for k in range(inner // step):
        cols = slice(k * step, (k + 1) * step)
        more = slice(inner + k * step, inner + (k + 1) * step)
        dh = dot_t(dlow, down_ref[cols, :])
        a = both_ref[:, cols]
        sig = jax.nn.sigmoid(a)
        dboth_ref[:, cols] = (dh * both_ref[:, more] * (sig * (1.0 + a * (1.0 - sig)))).astype(BF16)
        dboth_ref[:, more] = (dh * (a * sig)).astype(BF16)
    load_wait(up_pairs, sems.at[0])
    work_ref[...] = dot_t(dboth_ref[...], up_ref[...])

    def norm_back(r):
        after = after_ref[r, :]
        scale = lax.rsqrt(jnp.mean(after * after, axis=1, keepdims=True) + EPS)
        normal = after * scale
        lift = work_ref[r, :]
        e = lift * p_ref[2:3, :]
        d = grad_ref[r, :].astype(F32) + scale * (e - normal * jnp.mean(e * normal, axis=1, keepdims=True))
        dafter_ref[r, :] = d
        dmid_ref[r, :] = d.astype(BF16)
        work_ref[r, :] = lift * normal

    over_rows(rows, norm_back)
    gain_ref[...] = jnp.sum(work_ref[...], axis=0, keepdims=True)


def back_ffn(plan, me, dx, params, both, after, weights):
    rows, width = dx.shape
    inner = 2 * width
    return pl.pallas_call(
        functools.partial(back_ffn_kernel, plan, len(weights)),
        out_shape=(
            sds((rows, width), BF16),
            sds((rows, 2 * inner), BF16),
            sds((rows, width)),
            sds((rows, width), BF16),
            sds((1, width)),
        ),
        in_specs=[SMEM] + [VMEM] * 4 + [ANY] * len(weights),
        out_specs=(VMEM,) * 5,
        scratch_shapes=[
            pltpu.VMEM((rows, width), F32),
            pltpu.VMEM((width, 2 * inner), BF16),
            pltpu.VMEM((inner, width), BF16),
            pltpu.SemaphoreType.DMA((2,)),
        ],
        compiler_params=pltpu.CompilerParams(vmem_limit_bytes=24 << 20),
        cost_estimate=COST,
        name="back_ffn",
    )(me, dx, params, both, after, *weights)


def back_mid_kernel(
    plan, count, me_ref, dmid_ref, p_ref, gn_ref, rg_ref, gate_ref, states_ref, kept_ref, sub_ref, *refs
):
    w_hbm, refs = refs[:count], refs[count:]
    dgpre_ref, dstates_ref, gain_ref, rsub_ref, rtotal_ref, work_ref, out_ref, sem = refs
    rows, width = dmid_ref.shape
    half = width // 2
    block = rows // SUB
    pairs = pairs_of(plan, w_hbm, me_ref, "out", out_ref)
    load_start(pairs, sem)
    load_wait(pairs, sem)
    work_ref[...] = dot_t(dmid_ref[...], out_ref[...])

    def group_back(r):
        held = rg_ref[r, :]
        for g in range(width // GROUP):
            cols = slice(g * GROUP, (g + 1) * GROUP)
            gn = gn_ref[r, cols]
            dg = work_ref[r, cols]
            e = dg * p_ref[1:2, cols]
            dv = held[:, g : g + 1] * (
                e - jnp.mean(e, axis=1, keepdims=True) - gn * jnp.mean(e * gn, axis=1, keepdims=True)
            )
            gate = gate_ref[r, cols]
            dgpre_ref[r, cols] = (dv * states_ref[g, r, :] * gate * (1.0 - gate)).astype(BF16)
            dstates_ref[g, r, :] = dv * gate
            work_ref[r, cols] = dg * gn

    over_rows(rows, group_back)
    gain_ref[...] = jnp.sum(work_ref[...], axis=0, keepdims=True)

    cos, sin = turns(p_ref, half)
    tiles = half // GROUP
    zr = [jnp.zeros((SUB, GROUP), F32)] * tiles
    zi = [jnp.zeros((SUB, GROUP), F32)] * tiles
    for j in reversed(range(block)):
        at = pl.ds(j, SUB, stride=block)
        for t in range(tiles):
            kept = kept_ref[t, at, :]
            qr = dstates_ref[t, at, :] + zr[t]
            qi = dstates_ref[tiles + t, at, :] + zi[t]
            zr[t] = kept * (cos[t] * qr + sin[t] * qi)
            zi[t] = kept * (cos[t] * qi - sin[t] * qr)
    zr, zi = jnp.concatenate(zr, axis=1), jnp.concatenate(zi, axis=1)
    rsub_ref[0] = zr
    rsub_ref[1] = zi
    tr = jnp.zeros((1, half), F32)
    ti = jnp.zeros((1, half), F32)
    for k in reversed(range(SUB)):
        ar, ai = sub_ref[0, k : k + 1, :], sub_ref[1, k : k + 1, :]
        tr, ti = ar * tr + ai * ti + zr[k : k + 1], ar * ti - ai * tr + zi[k : k + 1]
    rtotal_ref[0:1, :] = tr
    rtotal_ref[1:2, :] = ti


def back_mid(plan, me, dmid, params, gn, rg, gate, states, kept, sub, weights):
    rows, width = dmid.shape
    half = width // 2
    return pl.pallas_call(
        functools.partial(back_mid_kernel, plan, len(weights)),
        out_shape=(
            sds((rows, width), BF16),
            sds((width // GROUP, rows, GROUP)),
            sds((1, width)),
            sds((2, SUB, half)),
            sds((2, half)),
        ),
        in_specs=[SMEM] + [VMEM] * 8 + [ANY] * len(weights),
        out_specs=(VMEM,) * 5,
        scratch_shapes=[
            pltpu.VMEM((rows, width), F32),
            pltpu.VMEM((width, width), BF16),
            pltpu.SemaphoreType.DMA,
        ],
        compiler_params=pltpu.CompilerParams(vmem_limit_bytes=24 << 20),
        cost_estimate=COST,
        name="back_mid",
    )(me, dmid, params, gn, rg, gate, states, kept, sub, *weights)


def back_two_kernel(
    plan, count, me_ref, x_ref, p_ref, dafter_ref, dgpre_ref, dstates_ref, states_ref, kept_ref, rate_ref, cpre_ref,
    first_ref, sub_ref, rsub_ref, every_ref, revery_ref, *refs
):
    w_hbm, refs = refs[:count], refs[count:]
    (
    dmixin_ref, dx_ref, gains_ref,
    work_ref, q_ref, turn_ref, start_ref, w_ref, sem,
    ) = refs
    rows, width = x_ref.shape
    half = width // 2
    block = rows // SUB
    pairs = pairs_of(plan, w_hbm, me_ref, "mix", w_ref)
    load_start(pairs, sem)
    zr = jnp.zeros((1, half), F32)
    zi = jnp.zeros((1, half), F32)
    for k in reversed(range(every_ref.shape[0])):
        at = k ^ me_ref[3]
        ar, ai = every_ref[at, 0:1, :], every_ref[at, 1:2, :]
        later = k > me_ref[0]
        nr = ar * zr + ai * zi + revery_ref[at, 0:1, :]
        ni = ar * zi - ai * zr + revery_ref[at, 1:2, :]
        zr = jnp.where(later, nr, zr)
        zi = jnp.where(later, ni, zi)
    for k in reversed(range(SUB)):
        start_ref[0, k : k + 1, :] = zr
        start_ref[1, k : k + 1, :] = zi
        ar, ai = sub_ref[0, k : k + 1, :], sub_ref[1, k : k + 1, :]
        zr, zi = (
            ar * zr + ai * zi + rsub_ref[0, k : k + 1, :],
            ar * zi - ai * zr + rsub_ref[1, k : k + 1, :],
        )
    cos, sin = turns(p_ref, half)
    tiles = half // GROUP
    zr = parts(start_ref, 0, tiles)
    zi = parts(start_ref, 1, tiles)
    angle = [jnp.zeros((SUB, GROUP), F32)] * tiles
    for j in reversed(range(block)):
        at = pl.ds(j, SUB, stride=block)
        before = pl.ds(max(j - 1, 0), SUB, stride=block)
        for t in range(tiles):
            kept = kept_ref[t, at, :]
            qr = dstates_ref[t, at, :] + zr[t]
            qi = dstates_ref[tiles + t, at, :] + zi[t]
            q_ref[t, at, :] = qr
            q_ref[tiles + t, at, :] = qi
            zr[t] = kept * (cos[t] * qr + sin[t] * qi)
            zi[t] = kept * (cos[t] * qi - sin[t] * qr)
            if j:
                sr, si = states_ref[t, before, :], states_ref[tiles + t, before, :]
            else:
                sr, si = (first_ref[k, :, t * GROUP : (t + 1) * GROUP] for k in range(2))
            turn_ref[t, at, :] = zr[t] * sr + zi[t] * si
            angle[t] = angle[t] + (zi[t] * sr - zr[t] * si)
    gains_ref[1:2, half:] = jnp.sum(jnp.concatenate(angle, axis=1), axis=0, keepdims=True)

    def activations(r):
        for t in range(tiles):
            rate = rate_ref[r, t * GROUP : (t + 1) * GROUP]
            left = 1.0 - rate
            meet = jnp.zeros_like(rate)
            for k in range(2):
                cols = slice((k * tiles + t) * GROUP, (k * tiles + t + 1) * GROUP)
                pre = cpre_ref[r, cols]
                sig = jax.nn.sigmoid(pre)
                q = q_ref[k * tiles + t, r, :]
                meet = meet + q * (pre * sig)
                dmixin_ref[r, cols] = (left * q * (sig * (1.0 + pre * (1.0 - sig)))).astype(BF16)
            dfpre = left * (turn_ref[t, r, :] - rate * meet)
            dmixin_ref[r, 2 * width + t * GROUP : 2 * width + (t + 1) * GROUP] = dfpre.astype(BF16)
            turn_ref[t, r, :] = dfpre
        dmixin_ref[r, width : 2 * width] = dgpre_ref[r, :]

    over_rows(rows, activations)
    for t in range(tiles):
        gains_ref[1:2, t * GROUP : (t + 1) * GROUP] = jnp.sum(turn_ref[t], axis=0, keepdims=True)
    load_wait(pairs, sem)
    work_ref[...] = dot_t(dmixin_ref[...], w_ref[:, : dmixin_ref.shape[1]])

    def norm_back(r):
        x = x_ref[r, :].astype(F32)
        scale = lax.rsqrt(jnp.mean(x * x, axis=1, keepdims=True) + EPS)
        normal = x * scale
        dn = work_ref[r, :]
        e = dn * p_ref[0:1, :]
        dx_ref[r, :] = dafter_ref[r, :] + scale * (e - normal * jnp.mean(e * normal, axis=1, keepdims=True))
        work_ref[r, :] = dn * normal

    over_rows(rows, norm_back)
    gains_ref[0:1, :] = jnp.sum(work_ref[...], axis=0, keepdims=True)


def back_two(plan, me, x, params, dafter, dgpre, dstates, states, kept, rate, cpre, first, sub, rsub, every, revery, weights):
    rows, width = x.shape
    half = width // 2
    return pl.pallas_call(
        functools.partial(back_two_kernel, plan, len(weights)),
        out_shape=(
            sds((rows, 2 * width + half), BF16),
            sds((rows, width)),
            sds((2, width)),
        ),
        in_specs=[SMEM] + [VMEM] * 14 + [ANY] * len(weights),
        out_specs=(VMEM,) * 3,
        scratch_shapes=[
            pltpu.VMEM((rows, width), F32),
            pltpu.VMEM((width // GROUP, rows, GROUP), F32),
            pltpu.VMEM((half // GROUP, rows, GROUP), F32),
            pltpu.VMEM((2, SUB, half), F32),
            pltpu.VMEM((width, mix_width(plan, width)), BF16),
            pltpu.SemaphoreType.DMA,
        ],
        compiler_params=pltpu.CompilerParams(vmem_limit_bytes=24 << 20),
        cost_estimate=COST,
        name="back_two",
    )(me, x, params, dafter, dgpre, dstates, states, kept, rate, cpre, first, sub, rsub, every, revery, *weights)


def row_product(left, right):
    return lax.dot_general(left, right, (((0,), (0,)), ((), ())), preferred_element_type=F32)


def export(info_ref, rels, name, grad, column, columns, keep_ref, send_ref, sem):
    chip, core = info_ref[1], info_ref[2]
    pairs = []
    for half, target in ((1 - core, send_ref), (core, keep_ref)):
        for b, (zero, one) in enumerate(zip(*rels)):
            block = chip ^ (zero + half * (one - zero))
            if name == "down":
                row, left = block * (2 * UNIT) + half * UNIT, 0
            else:
                row, left = block * UNIT, half * HALVES[name]
            pairs.append(
                (
                    grad.at[pl.ds(pl.multiple_of(row, UNIT), UNIT), pl.ds(pl.multiple_of(left, GROUP), columns)],
                    target.at[b, :, pl.ds(column, columns)],
                )
            )
    load_start(pairs, sem)
    return pairs


def products(left, right_ref, grad_ref, size):
    step = HALVES["out"]
    for k in range(size // step):
        cols = slice(k * step, (k + 1) * step)
        grad_ref[:, cols] = row_product(left, right_ref[:, cols]).astype(BF16)


def grad_ud_kernel(
    rels, info_ref, lifted_ref, dboth_ref, hidden_ref, dlow_ref, keep_ref, send_ref, up_ref, down_ref, sem
):
    width = dlow_ref.shape[1]
    products(hidden_ref[...], dlow_ref, down_ref, width)
    pairs = export(info_ref, rels, "down", down_ref, HALVES["up"], width, keep_ref, send_ref, sem)
    products(lifted_ref[...], dboth_ref, up_ref, up_ref.shape[1])
    pairs += export(info_ref, rels, "up", up_ref, 0, HALVES["up"], keep_ref, send_ref, sem)
    load_wait(pairs, sem)


def grad_ud(rels, info, lifted, dboth, hidden, dlow):
    rows, width = dlow.shape
    inner = hidden.shape[1]
    shape = sds((len(rels[0]), UNIT, HALVES["up"] + width), BF16)
    return pl.pallas_call(
        functools.partial(grad_ud_kernel, rels),
        out_shape=(shape, shape),
        in_specs=[SMEM] + [VMEM] * 4,
        out_specs=(ANY, ANY),
        scratch_shapes=[
            pltpu.VMEM((width, 2 * inner), BF16),
            pltpu.VMEM((inner, width), BF16),
            pltpu.SemaphoreType.DMA,
        ],
        compiler_params=pltpu.CompilerParams(vmem_limit_bytes=24 << 20),
        cost_estimate=COST,
        name="grad_ud",
    )(info, lifted, dboth, hidden, dlow)


def grad_mo_kernel(rels, info_ref, gated_ref, dmid_ref, normed_ref, dmixin_ref, *refs):
    extra, (keep_ref, send_ref, out_ref, mix_ref, held_ref, sem) = refs[:-6], refs[-6:]
    width = dmid_ref.shape[1]
    products(gated_ref[...], dmid_ref, out_ref, width)
    pairs = export(info_ref, rels, "out", out_ref, HALVES["mix"], HALVES["out"], keep_ref, send_ref, sem)
    size = dmixin_ref.shape[1]
    held_ref[...] = jnp.zeros_like(held_ref)
    for k in range(len(extra) // 3):
        two, mid_gain, ffn_gain = extra[3 * k : 3 * k + 3]
        held_ref[4 * k : 4 * k + 1, :] = two[0:1, :]
        held_ref[4 * k + 1 : 4 * k + 2, :] = mid_gain[...]
        held_ref[4 * k + 2 : 4 * k + 3, :] = ffn_gain[...]
        held_ref[4 * k + 3 : 4 * k + 4, :] = two[1:2, :]
    mix_ref[:, size:] = jnp.transpose(held_ref[...]).astype(BF16)
    products(normed_ref[...], dmixin_ref, mix_ref, size)
    pairs += export(info_ref, rels, "mix", mix_ref, 0, HALVES["mix"], keep_ref, send_ref, sem)
    load_wait(pairs, sem)


def grad_mo(rels, info, gated, dmid, normed, dmixin, extra):
    rows, width = normed.shape
    shape = sds((len(rels[0]), UNIT, HALVES["mix"] + HALVES["out"]), BF16)
    return pl.pallas_call(
        functools.partial(grad_mo_kernel, rels),
        out_shape=(shape, shape),
        in_specs=[SMEM] + [VMEM] * (4 + len(extra)),
        out_specs=(ANY, ANY),
        scratch_shapes=[
            pltpu.VMEM((width, width), BF16),
            pltpu.VMEM((width, 2 * HALVES["mix"]), BF16),
            pltpu.VMEM((GROUP, width), F32),
            pltpu.SemaphoreType.DMA,
        ],
        compiler_params=pltpu.CompilerParams(vmem_limit_bytes=24 << 20),
        cost_estimate=COST,
        name="grad_mo",
    )(info, gated, dmid, normed, dmixin, *extra)


def table_kernel(plan, count, me_ref, *refs):
    sources, (table_ref, held_ref, sem) = refs[:count], refs[count:]
    pairs = pairs_of(plan, sources, me_ref, "small", held_ref)
    load_start(pairs, sem)
    load_wait(pairs, sem)
    depth = table_ref.shape[0]
    half = table_ref.shape[2] // 2
    table = jnp.transpose(held_ref[:, GROUP:].astype(F32))
    table_ref[...] = jnp.zeros_like(table_ref)
    for l in range(depth):
        chan = table[3 * depth + l : 3 * depth + l + 1]
        table_ref[l, 0:3, :] = table[3 * l : 3 * l + 3]
        table_ref[l, 3:4, :half] = chan[:, :half]
        table_ref[l, 3:4, half:] = jnp.cos(chan[:, half:])
        table_ref[l, 4:5, :half] = jnp.sin(chan[:, half:])


def table_of(plan, me, weights, depth, width):
    return pl.pallas_call(
        functools.partial(table_kernel, plan, len(weights)),
        out_shape=sds((depth, 8, width)),
        in_specs=[SMEM] + [ANY] * len(weights),
        out_specs=VMEM,
        scratch_shapes=[pltpu.VMEM((width, 2 * GROUP), BF16), pltpu.SemaphoreType.DMA],
        compiler_params=pltpu.CompilerParams(vmem_limit_bytes=16 << 20),
        cost_estimate=COST,
        name="table",
    )(me, *weights)


def swap(x, bits):
    count = lax.axis_size("dp") * lax.axis_size("seq")
    return lax.ppermute(x, ALL, [(i, i ^ bits[i % 2]) for i in range(count)])


class Order:
    def __init__(self):
        self.last = None

    def step(self, *values):
        if self.last is not None:
            values = lax.optimization_barrier(values + (self.last,))[: len(values)]
        self.last = values[0]
        return values

    def join(self, *moves):
        for move in moves:
            (move.got,) = self.step(move.got)

    def join_core(self, move):
        (move.last_core, move.held_core) = self.step(move.last_core, move.held_core)


def rels_of(stages):
    rels = ([0], [0])
    for bits in stages:
        for core in range(2):
            rels[core].extend([rel ^ bits[core] for rel in rels[core]])
    return rels


class Spread:
    def __init__(self, unit, stages):
        self.held, self.stages, self.at = unit[None], stages, 0
        self.got = None

    def join(self):
        if self.got is not None:
            self.held = jnp.concatenate([self.held, self.got])

    def next(self):
        self.join()
        one, two = self.stages[self.at]
        self.at += 1
        self.got = swap(self.held, (2 * one, 2 * two))

    def end(self):
        self.near, self.last = self.held, self.got
        self.last_core = swap(self.last, (1, 1))

    def near_core(self):
        self.held_core = swap(self.held, (1, 1))

    def arrays(self):
        return (self.near, self.held_core, self.last, self.last_core)

    def sources(self):
        rels = rels_of(self.stages)
        half = len(rels[0]) // 2
        low = tuple(tuple(rel[:half]) for rel in rels)
        high = tuple(tuple(rel[half:]) for rel in rels)
        return ((0, low), (1, low), (0, high), (1, high))


class Reduce:
    def __init__(self, keep, send, stages):
        self.held, self.stages = keep, list(stages)
        self.got = swap(send, (1, 1))

    def add(self):
        half = self.held.shape[0] // 2
        if not half:
            return self.held[0].astype(F32) + self.got[0].astype(F32)

        def joined(part):
            return (self.held[part].astype(F32) + self.got[part].astype(F32)).astype(BF16)

        self.low, self.high = joined(slice(0, half)), joined(slice(half, None))

    def send(self):
        one, two = self.stages.pop()
        self.got = swap(self.high, (2 * one, 2 * two))
        self.held = self.low

    def next(self):
        self.add()
        self.send()


def exchange(x):
    pair = jnp.stack([x, swap(x, (1, 1))])
    got = [swap(pair, (k, k)) for k in range(2, lax.axis_size("seq"), 2)]
    return jnp.concatenate([pair] + got)


def finish_kernel(info_ref, *refs):
    depth = (len(refs) - 5) // 3
    mine, other, downs = refs[:depth], refs[depth : 2 * depth], refs[2 * depth : 3 * depth]
    mix_ref, out_ref, up_ref, down_ref, tail_ref = refs[3 * depth :]
    width = down_ref.shape[2]
    mix_cols = mix_ref.shape[2]
    size = HALVES["mix"]

    def place(first, second):
        for l in range(depth):
            mix_ref[l, :, :size] = first[l][:, :size]
            mix_ref[l, :, size:] = second[l][:, : mix_cols - size]
            at = size
            for name, ref in (("out", out_ref), ("up", up_ref)):
                step = HALVES[name]
                ref[l, :, :step] = first[l][:, at : at + step]
                ref[l, :, step:] = second[l][:, at : at + step]
                at += step
        tail_ref[...] = second[0][:, size - GROUP : size]

    @pl.when(info_ref[2] == 0)
    def _():
        place(mine, other)

    @pl.when(info_ref[2] == 1)
    def _():
        place(other, mine)

    for l in range(depth):
        down_ref[l] = downs[l][:, downs[l].shape[1] - width :]


def finish(info, mine, other, downs, shapes):
    share = mine[0].shape[0]
    return pl.pallas_call(
        finish_kernel,
        out_shape=tuple(sds(shape) for shape in shapes) + (sds((share, GROUP)),),
        in_specs=[SMEM] + [VMEM] * (3 * len(mine)),
        out_specs=(VMEM,) * 5,
        compiler_params=pltpu.CompilerParams(vmem_limit_bytes=32 << 20),
        cost_estimate=COST,
        name="finish",
    )(info, *mine, *other, *downs)


def layer_params(gains, chan):
    half = chan.shape[0] // 2
    angle = chan[half:]
    rows = [
        gains[0],
        gains[1],
        gains[2],
        jnp.concatenate([chan[:half], jnp.cos(angle)]),
        jnp.concatenate([jnp.sin(angle), jnp.zeros((half,), F32)]),
    ]
    return jnp.concatenate([jnp.stack(rows), jnp.zeros((3, 2 * half), F32)], axis=0)


STAGES = ((4, 8), (8, 4), (1, 2), (2, 1))


def small_of(gains, chan_params):
    depth, _, share = gains.shape
    return jnp.concatenate(
        [gains.reshape(depth * 3, share).T, chan_params.T, jnp.zeros((share, GROUP - 4 * depth), BF16)], axis=1
    )


def info_of(lengths, rows, turned):
    where = lax.axis_index("seq")
    base = where * rows
    ends = [lengths[0, 0]]
    for j in range(1, lengths.shape[1]):
        ends.append(ends[-1] + lengths[0, j])
    chip = (lax.axis_index("dp") * lax.axis_size("seq") + where) // 2
    values = [where, chip, where % 2, where if turned else jnp.zeros_like(where), ends[-1] - base]
    values += [end - lengths[0, j] - base for j, end in enumerate(ends)]
    return jnp.stack([value.astype(jnp.int32) for value in values])


def plain_body(stream, w_mix, w_out, w_up, w_down, gains, chan_params, lengths, cotangent):
    rows, width = stream.shape
    depth = w_mix.shape[0]
    info = info_of(lengths, rows, False)
    small = small_of(gains, chan_params)
    table = lax.all_gather(small, ALL, axis=0, tiled=True)[:, : 4 * depth].T.astype(F32)
    params = [layer_params(table[3 * l : 3 * l + 3], table[3 * depth + l]) for l in range(depth)]
    weights = [
        tuple(lax.all_gather(w[l], ALL, axis=0, tiled=True) for w in (w_mix, w_out, w_up, w_down))
        for l in range(depth)
    ]
    x = stream
    saved = []
    for l in range(depth):
        head = front(None, info, x, params[l], weights[l])
        every = lax.all_gather(head[-1], "seq")
        middle = mid(None, info, x, params[l], head[2], head[4], head[5], head[6], every, weights[l])
        tail = ffn(None, info, middle[5], middle[6], weights[l], F32)
        saved.append((x, every, head, middle, tail))
        x = tail[-1]
    mixed = x.astype(BF16)
    dx = cotangent
    sums = [None] * depth
    for l in reversed(range(depth)):
        x, every, (normed, cpre, gate, rate, kept, feed, sub, _), middle, (both, hidden, _) = saved[l]
        states, first, gn, rg, gated, after, lifted = middle
        dlow, dboth, dafter, dmid, ffn_gain = back_ffn(None, info, dx, params[l], both, after, weights[l])
        dgpre, dstates, mid_gain, rsub, rtotal = back_mid(
            None, info, dmid, params[l], gn, rg, gate, states, kept, sub, weights[l]
        )
        revery = lax.all_gather(rtotal, "seq")
        dmixin, dx, gains_b = back_two(
            None, info, x, params[l], dafter, dgpre, dstates, states, kept, rate, cpre, first, sub, rsub, every, revery,
            weights[l],
        )
        grads = [row_product(normed, dmixin), row_product(gated, dmid), row_product(lifted, dboth), row_product(hidden, dlow)]
        grads.append(jnp.stack([gains_b[0], mid_gain[0], ffn_gain[0], gains_b[1]], axis=1))
        sums[l] = [lax.psum_scatter(g.astype(BF16), ALL, scatter_dimension=0, tiled=True).astype(F32) for g in grads]
    outs = [jnp.stack([sums[l][k] for l in range(depth)]) for k in range(5)]
    tail = outs.pop()
    return (mixed, dx, *outs, jnp.swapaxes(tail[:, :, :3], 1, 2), tail[:, :, 3])


def fast_body(stream, w_mix, w_out, w_up, w_down, gains, chan_params, lengths, cotangent):
    rows, width = stream.shape
    depth, share, mix_cols = w_mix.shape
    info = info_of(lengths, rows, True)
    small = small_of(gains, chan_params)
    core = lax.axis_index("seq") % 2
    padding = jnp.zeros((share, 2 * HALVES["mix"] - mix_cols - GROUP), BF16)
    halves = ([], [])
    for l in range(depth):
        mix = jnp.concatenate([w_mix[l], padding, small if l == 0 else jnp.zeros_like(small)], axis=1)
        for h in range(2):
            for w, size in ((mix, HALVES["mix"]), (w_out[l], HALVES["out"]), (w_up[l], HALVES["up"])):
                halves[h].append(w[:, h * size : (h + 1) * size])
    halves = [jnp.concatenate(half, axis=1) for half in halves]
    mine = jnp.where(core == 0, halves[0], halves[1])
    other = swap(jnp.where(core == 0, halves[1], halves[0]), (1, 1))
    units = jnp.where(core == 0, jnp.concatenate([mine, other]), jnp.concatenate([other, mine]))
    joint = HALVES["mix"] + HALVES["out"]
    size = joint + HALVES["up"]
    mos, uds = [], []
    for l in range(depth):
        unit = units[:, l * size : (l + 1) * size]
        mos.append(Spread(unit[:, :joint], STAGES))
        uds.append(Spread(jnp.concatenate([unit[:, joint:], w_down[l]], axis=1), STAGES))
    rels = rels_of(STAGES)
    plan = {
        "sources": mos[0].sources(),
        "mix": (0, HALVES["mix"]),
        "out": (HALVES["mix"], HALVES["out"]),
        "small": (HALVES["mix"] - GROUP, GROUP),
        "up": (0, HALVES["up"]),
        "down": (HALVES["up"], width),
    }

    order = Order()

    def go(move):
        order.join(move)
        move.next()

    mo, ud = mos[0], uds[0]
    more = depth > 1
    ud.next()
    mo.next()
    go(ud)
    go(mo)
    go(mo)
    if more:
        mos[1].next()
    go(mo)
    mo.near_core()
    go(ud)
    if more:
        go(mos[1])
        uds[1].next()
        order.join(mos[1])
        go(uds[1])
    order.join(ud)
    order.join(mo)
    mo.end()
    ud.next()
    ud.near_core()
    x = stream
    saved = []
    params = None
    for l in range(depth):
        mo, ud = mos[l], uds[l]
        more = l + 1 < depth
        order.join_core(mo)
        if l == 0:
            params = table_of(plan, info, mo.arrays(), depth, width)
        (layer,) = order.step(params[l])
        head = front(plan, info, x, layer, mo.arrays())
        (total,) = order.step(head[-1])
        every = exchange(total)
        (every,) = order.step(every)
        order.join(ud)
        ud.end()
        if more:
            mos[l + 1].next()
            uds[l + 1].next()
        middle = mid(plan, info, x, layer, head[2], head[4], head[5], head[6], order.step(every)[0], mo.arrays())
        middle = (*middle[:-1], *order.step(middle[-1]))
        if more:
            go(mos[l + 1])
            mos[l + 1].near_core()
        order.join_core(ud)
        tail = ffn(plan, info, middle[5], middle[6], ud.arrays(), F32 if more else BF16)
        saved.append((x, every, head, middle, tail, layer))
        (x,) = order.step(tail[-1])
        if more:
            go(uds[l + 1])
            uds[l + 1].near_core()
            order.join(mos[l + 1])
            mos[l + 1].end()
    mixed = x
    dx = cotangent
    sums = [None] * depth
    extra = ()
    for l in reversed(range(depth)):
        x, every, (normed, cpre, gate, rate, kept, feed, sub, _), middle, (both, hidden, _), layer = saved[l]
        states, first, gn, rg, gated, after, lifted = middle
        mo_up, ud_up = sums[l + 1] if l + 1 < depth else (None, None)
        (dx,) = order.step(dx)
        dlow, dboth, dafter, dmid, ffn_gain = back_ffn(plan, info, dx, layer, both, after, uds[l].arrays())
        (dlow,) = order.step(dlow)
        if mo_up:
            go(ud_up)
            go(mo_up)
        (lifted,) = order.step(lifted)
        ud = Reduce(*grad_ud(rels, info, lifted, dboth, hidden, dlow), STAGES)
        (ud.held,) = order.step(ud.held)
        (dmid,) = order.step(dmid)
        dgpre, dstates, mid_gain, rsub, rtotal = back_mid(
            plan, info, dmid, layer, gn, rg, gate, states, kept, sub, mos[l].arrays()
        )
        (rtotal,) = order.step(rtotal)
        revery = exchange(rtotal)
        order.join(ud)
        ud.add()
        (revery,) = order.step(revery)
        (ud.high,) = order.step(ud.high)
        ud.send()
        if mo_up:
            go(ud_up)
            go(mo_up)
        (dstates,) = order.step(dstates)
        dmixin, dx, gains_b = back_two(
            plan, info, x, layer, dafter, dgpre, dstates, states, kept, rate, cpre, first, sub, rsub, every, revery,
            mos[l].arrays(),
        )
        (dmixin,) = order.step(dmixin)
        extra = (gains_b, mid_gain, ffn_gain) + extra
        mo = Reduce(*grad_mo(rels, info, gated, dmid, normed, dmixin, extra if l == 0 else ()), STAGES)
        (mo.held,) = order.step(mo.held)
        if mo_up:
            go(ud_up)
            go(mo_up)
        sums[l] = (mo, ud)
    mo, ud = sums[0]
    go(ud)
    go(mo)
    if depth > 1:
        go(sums[1][0])
    go(ud)
    go(mo)
    go(ud)
    go(mo)
    go(mo)
    mine, other, downs = [], [], []
    for mo, ud in reversed(sums):
        ready = ud.add()
        line = jnp.concatenate([mo.add(), ready[:, : HALVES["up"]]], axis=1)
        first, second = line[:share], line[share:]
        mine.insert(0, jnp.where(core == 0, first, second))
        other.insert(0, swap(jnp.where(core == 0, second, first), (1, 1)))
        downs.insert(0, ready)
    shapes = (w_mix.shape, w_out.shape, w_up.shape, w_down.shape)
    *grads, tail = finish(info, mine, other, downs, shapes)
    tail = tail[:, : 4 * depth].T.reshape(depth, 4, share)
    return (mixed, dx, *grads, tail[:, :3], tail[:, 3])


def body(stream, w_mix, *others):
    n_dp, n_seq = lax.axis_size("dp"), lax.axis_size("seq")
    fast = n_seq == 8 and n_dp & (n_dp - 1) == 0 and 2 * w_mix.shape[1] == UNIT
    return (fast_body if fast else plain_body)(stream, w_mix, *others)


def solution(mesh):
    placed = (
        P(ALL, None),
        P(None, ALL, None),
        P(None, ALL, None),
        P(None, ALL, None),
        P(None, ALL, None),
        P(None, None, ALL),
        P(None, ALL),
        P("dp", None),
        P(ALL, None),
    )
    return jax.shard_map(
        body,
        mesh=mesh,
        in_specs=placed,
        out_specs=(
            P(ALL, None),
            P(ALL, None),
            P(None, ALL, None),
            P(None, ALL, None),
            P(None, ALL, None),
            P(None, ALL, None),
            P(None, None, ALL),
            P(None, ALL),
        ),
        check_vma=False,
    )
```

```python
import functools

import jax
import jax.numpy as jnp
from jax import lax
from jax.experimental import pallas as pl
from jax.experimental.pallas import tpu as pltpu
from jax.sharding import PartitionSpec as P

GROUP = 128
EPS = 1e-06
SUB = 8
UNIT = 48
HALVES = {"mix": 1024, "out": 384, "up": 1536, "gate": 384, "cell": 640}
ROWS = 32
F32 = jnp.float32
BF16 = jnp.bfloat16
ALL = ("dp", "seq")
VMEM = pl.BlockSpec(memory_space=pltpu.VMEM)
SMEM = pl.BlockSpec(memory_space=pltpu.SMEM)
ANY = pl.BlockSpec(memory_space=pl.ANY)
COST = pl.CostEstimate(flops=1000, bytes_accessed=1000, transcendentals=0)


def sds(shape, dtype=F32):
    return jax.ShapeDtypeStruct(shape, dtype)


def over_rows(total, body):
    def step(i, _):
        body(pl.ds(pl.multiple_of(i * ROWS, ROWS), ROWS))
        return 0

    lax.fori_loop(0, total // ROWS, step, 0)


def dot(left, right):
    return jnp.dot(left, right, preferred_element_type=F32)


def dot_t(left, right):
    return lax.dot_general(left, right, (((1,), (1,)), ((), ())), preferred_element_type=F32)


def cmul(ar, ai, br, bi):
    return ar * br - ai * bi, ar * bi + ai * br


def power(cos, sin, times):
    while times > 1:
        cos, sin = cos * cos - sin * sin, 2.0 * cos * sin
        times //= 2
    return cos, sin


def turns(p_ref, half):
    cos, sin = p_ref[3:4, half:], p_ref[4:5, :half]
    return tuple(
        [jnp.broadcast_to(part[:, t * GROUP : (t + 1) * GROUP], (SUB, GROUP)) for t in range(half // GROUP)]
        for part in (cos, sin)
    )


def parts(ref, k, tiles):
    return [ref[k, :, t * GROUP : (t + 1) * GROUP] for t in range(tiles)]


def mix_width(plan, width):
    return 2 * width + width // 2 if plan is None else 2 * HALVES["mix"]


def load_start(pairs, sem):
    for source, target in pairs:
        pltpu.make_async_copy(source, target, sem).start()


def load_wait(pairs, sem):
    for source, target in pairs:
        pltpu.make_async_copy(source, target, sem).wait()


def pairs_of(plan, sources, me_ref, name, target):
    if plan is None:
        return [(sources[{"mix": 0, "out": 1, "up": 2, "down": 3}[name]], target)]
    chip, core = me_ref[1], me_ref[2]
    column, columns = plan[name]
    pairs = []
    for source, (other_core, rels) in enumerate(plan["sources"]):
        half = core ^ other_core
        for b, (zero, one) in enumerate(zip(*rels)):
            block = chip ^ (zero + half * (one - zero))
            if name == "down":
                row, left = block * (2 * UNIT) + half * UNIT, 0
            elif name == "small":
                row, left = block * UNIT, half * GROUP
            else:
                row, left = block * UNIT, half * HALVES[name]
            to = target.at[pl.ds(pl.multiple_of(row, UNIT), UNIT), pl.ds(pl.multiple_of(left, GROUP), columns)]
            pairs.append((sources[source].at[b, :, pl.ds(column, columns)], to))
    return pairs


def front_kernel(
    plan, count, me_ref, x_ref, p_ref, *refs
):
    w_hbm, refs = refs[:count], refs[count:]
    (
    normed_ref, cpre_ref, gate_ref, rate_ref, kept_ref, feed_ref, sub_ref, total_ref,
    w_ref, sem,
    ) = refs
    rows, width = x_ref.shape
    half = width // 2
    block = rows // SUB
    pairs = pairs_of(plan, w_hbm, me_ref, "mix", w_ref)
    load_start(pairs, sem)

    def norm(r):
        x = x_ref[r, :].astype(F32)
        scale = lax.rsqrt(jnp.mean(x * x, axis=1, keepdims=True) + EPS)
        normed_ref[r, :] = (x * scale * p_ref[0:1, :]).astype(BF16)

    over_rows(rows, norm)
    load_wait(pairs, sem)
    normed = normed_ref[...]
    rate = jax.nn.sigmoid(dot(normed, w_ref[:, 2 * width : 2 * width + half]) + p_ref[3:4, :half])
    rate_ref[...] = rate
    at = lax.broadcasted_iota(jnp.int32, (rows, GROUP), 0)
    fresh = at == me_ref[5]
    for j in range(6, me_ref.shape[0]):
        fresh = jnp.logical_or(fresh, at == me_ref[j])
    tiles = half // GROUP
    for t in range(tiles):
        kept_ref[t] = jnp.where(fresh, 0.0, rate[:, t * GROUP : (t + 1) * GROUP])
    for k in range(2):
        cols = slice(k * half, (k + 1) * half)
        pre = dot(normed, w_ref[:, cols])
        cpre_ref[:, cols] = pre
        feed = (1.0 - rate_ref[...]) * (pre * jax.nn.sigmoid(pre))
        for t in range(tiles):
            feed_ref[k * tiles + t] = feed[:, t * GROUP : (t + 1) * GROUP]
    cos, sin = turns(p_ref, half)

    mag = [jnp.ones((SUB, GROUP), F32)] * tiles
    br = [jnp.zeros((SUB, GROUP), F32)] * tiles
    bi = [jnp.zeros((SUB, GROUP), F32)] * tiles
    for j in range(block):
        at = pl.ds(j, SUB, stride=block)
        for t in range(tiles):
            kept = kept_ref[t, at, :]
            tr, ti = cmul(cos[t], sin[t], br[t], bi[t])
            br[t] = kept * tr + feed_ref[t, at, :]
            bi[t] = kept * ti + feed_ref[tiles + t, at, :]
            mag[t] = mag[t] * kept
    mag, br, bi = (jnp.concatenate(part, axis=1) for part in (mag, br, bi))
    far_cos, far_sin = power(jnp.concatenate(cos, axis=1), jnp.concatenate(sin, axis=1), block)
    ar, ai = mag * far_cos, mag * far_sin
    sub_ref[0] = ar
    sub_ref[1] = ai
    sub_ref[2] = br
    sub_ref[3] = bi
    one_r, one_i, sum_r, sum_i = (part[0:1] for part in (ar, ai, br, bi))
    for k in range(1, SUB):
        kr, ki = ar[k : k + 1], ai[k : k + 1]
        one_r, one_i = cmul(kr, ki, one_r, one_i)
        sum_r, sum_i = cmul(kr, ki, sum_r, sum_i)
        sum_r = sum_r + br[k : k + 1]
        sum_i = sum_i + bi[k : k + 1]
    total_ref[0:1, :] = one_r
    total_ref[1:2, :] = one_i
    total_ref[2:3, :] = sum_r
    total_ref[3:4, :] = sum_i
    for k in range(2):
        cols = slice(width + k * half, width + (k + 1) * half)
        gate_ref[:, k * half : (k + 1) * half] = jax.nn.sigmoid(dot(normed, w_ref[:, cols]))


def front(plan, me, x, params, weights):
    rows, width = x.shape
    half = width // 2
    return pl.pallas_call(
        functools.partial(front_kernel, plan, len(weights)),
        out_shape=(
            sds((rows, width), BF16),
            sds((rows, width)),
            sds((rows, width)),
            sds((rows, half)),
            sds((half // GROUP, rows, GROUP)),
            sds((width // GROUP, rows, GROUP)),
            sds((4, SUB, half)),
            sds((4, half)),
        ),
        in_specs=[SMEM, VMEM, VMEM] + [ANY] * len(weights),
        out_specs=(VMEM,) * 8,
        scratch_shapes=[pltpu.VMEM((width, mix_width(plan, width)), BF16), pltpu.SemaphoreType.DMA],
        compiler_params=pltpu.CompilerParams(vmem_limit_bytes=12 << 20),
        cost_estimate=COST,
        name="front",
    )(me, x, params, *weights)


def mid_kernel(plan, count, me_ref, x_ref, p_ref, gate_ref, kept_ref, feed_ref, sub_ref, every_ref, *refs):
    w_hbm, refs = refs[:count], refs[count:]
    states_ref, first_ref, gn_ref, rg_ref, gated_ref, after_ref, lifted_ref, out_ref, sem = refs
    rows, width = x_ref.shape
    half = width // 2
    block = rows // SUB
    pairs = pairs_of(plan, w_hbm, me_ref, "out", out_ref)
    load_start(pairs, sem)

    sr = jnp.zeros((1, half), F32)
    si = jnp.zeros((1, half), F32)
    for k in range(every_ref.shape[0]):
        at = k ^ me_ref[3]
        nr, ni = cmul(every_ref[at, 0:1, :], every_ref[at, 1:2, :], sr, si)
        earlier = k < me_ref[0]
        sr = jnp.where(earlier, nr + every_ref[at, 2:3, :], sr)
        si = jnp.where(earlier, ni + every_ref[at, 3:4, :], si)
    for k in range(SUB):
        first_ref[0, k : k + 1, :] = sr
        first_ref[1, k : k + 1, :] = si
        nr, ni = cmul(sub_ref[0, k : k + 1, :], sub_ref[1, k : k + 1, :], sr, si)
        sr = nr + sub_ref[2, k : k + 1, :]
        si = ni + sub_ref[3, k : k + 1, :]
    cos, sin = turns(p_ref, half)
    tiles = half // GROUP
    sr = parts(first_ref, 0, tiles)
    si = parts(first_ref, 1, tiles)
    for j in range(block):
        at = pl.ds(j, SUB, stride=block)
        for t in range(tiles):
            kept = kept_ref[t, at, :]
            tr, ti = cmul(cos[t], sin[t], sr[t], si[t])
            sr[t] = kept * tr + feed_ref[t, at, :]
            si[t] = kept * ti + feed_ref[tiles + t, at, :]
            states_ref[t, at, :] = sr[t]
            states_ref[tiles + t, at, :] = si[t]

    lane = lax.broadcasted_iota(jnp.int32, (ROWS, GROUP), 1)

    def group_norm(r):
        held = jnp.zeros((ROWS, GROUP), F32)
        for g in range(width // GROUP):
            cols = slice(g * GROUP, (g + 1) * GROUP)
            v = gate_ref[r, cols] * states_ref[g, r, :]
            centre = v - jnp.mean(v, axis=1, keepdims=True)
            scale = lax.rsqrt(jnp.mean(centre * centre, axis=1, keepdims=True) + EPS)
            gn = centre * scale
            gn_ref[r, cols] = gn
            gated_ref[r, cols] = (gn * p_ref[1:2, cols]).astype(BF16)
            held = jnp.where(lane == g, scale, held)
        rg_ref[r, :] = held

    over_rows(rows, group_norm)
    load_wait(pairs, sem)
    after_ref[...] = x_ref[...].astype(F32) + dot(gated_ref[...], out_ref[...])

    def norm(r):
        after = after_ref[r, :]
        scale = lax.rsqrt(jnp.mean(after * after, axis=1, keepdims=True) + EPS)
        lifted_ref[r, :] = (after * scale * p_ref[2:3, :]).astype(BF16)

    over_rows(rows, norm)


def mid(plan, me, x, params, gate, kept, feed, sub, every, weights):
    rows, width = x.shape
    half = width // 2
    return pl.pallas_call(
        functools.partial(mid_kernel, plan, len(weights)),
        out_shape=(
            sds((width // GROUP, rows, GROUP)),
            sds((2, SUB, half)),
            sds((rows, width)),
            sds((rows, GROUP)),
            sds((rows, width), BF16),
            sds((rows, width)),
            sds((rows, width), BF16),
        ),
        in_specs=[SMEM] + [VMEM] * 7 + [ANY] * len(weights),
        out_specs=(VMEM,) * 7,
        scratch_shapes=[pltpu.VMEM((width, width), BF16), pltpu.SemaphoreType.DMA],
        compiler_params=pltpu.CompilerParams(vmem_limit_bytes=12 << 20),
        cost_estimate=COST,
        name="mid",
    )(me, x, params, gate, kept, feed, sub, every, *weights)


def ffn_kernel(plan, count, me_ref, after_ref, lifted_ref, *refs):
    w_hbm, refs = refs[:count], refs[count:]
    both_ref, hidden_ref, next_ref, up_ref, down_ref, sems = refs
    inner = hidden_ref.shape[1]
    up_pairs = pairs_of(plan, w_hbm, me_ref, "up", up_ref)
    down_pairs = pairs_of(plan, w_hbm, me_ref, "down", down_ref)
    load_start(up_pairs, sems.at[0])
    load_start(down_pairs, sems.at[1])
    load_wait(up_pairs, sems.at[0])
    lifted = lifted_ref[...]
    step = after_ref.shape[1] // 2
    for k in range(inner // step):
        cols = slice(k * step, (k + 1) * step)
        more = slice(inner + k * step, inner + (k + 1) * step)
        a = dot(lifted, up_ref[:, cols])
        b = dot(lifted, up_ref[:, more])
        both_ref[:, cols] = a
        both_ref[:, more] = b
        hidden_ref[:, cols] = (a * jax.nn.sigmoid(a) * b).astype(BF16)
    load_wait(down_pairs, sems.at[1])
    next_ref[...] = (after_ref[...] + dot(hidden_ref[...], down_ref[...])).astype(next_ref.dtype)


def ffn(plan, me, after, lifted, weights, dtype):
    rows, width = after.shape
    inner = 2 * width
    return pl.pallas_call(
        functools.partial(ffn_kernel, plan, len(weights)),
        out_shape=(sds((rows, 2 * inner)), sds((rows, inner), BF16), sds((rows, width), dtype)),
        in_specs=[SMEM] + [VMEM] * 2 + [ANY] * len(weights),
        out_specs=(VMEM,) * 3,
        scratch_shapes=[
            pltpu.VMEM((width, 2 * inner), BF16),
            pltpu.VMEM((inner, width), BF16),
            pltpu.SemaphoreType.DMA((2,)),
        ],
        compiler_params=pltpu.CompilerParams(vmem_limit_bytes=17 << 20),
        cost_estimate=COST,
        name="ffn",
    )(me, after, lifted, *weights)


def lower(me_ref, dx_ref, dlow_ref):
    rows, width = dx_ref.shape
    if dx_ref.dtype == BF16:
        at = lax.broadcasted_iota(jnp.int32, (rows, GROUP), 0)
        live = at < me_ref[4]
        for t in range(width // GROUP):
            cols = slice(t * GROUP, (t + 1) * GROUP)
            dlow_ref[:, cols] = jnp.where(live, dx_ref[:, cols].astype(F32), 0.0).astype(BF16)
        return dlow_ref
    dlow_ref[...] = dx_ref[...].astype(BF16)
    return dx_ref


def lift_back(grad_ref, p_ref, after_ref, work_ref, dafter_ref, dmid_ref, gain_ref):
    def norm_back(r):
        after = after_ref[r, :]
        scale = lax.rsqrt(jnp.mean(after * after, axis=1, keepdims=True) + EPS)
        normal = after * scale
        lift = work_ref[r, :]
        e = lift * p_ref[2:3, :]
        d = grad_ref[r, :].astype(F32) + scale * (e - normal * jnp.mean(e * normal, axis=1, keepdims=True))
        dafter_ref[r, :] = d
        dmid_ref[r, :] = d.astype(BF16)
        work_ref[r, :] = lift * normal

    over_rows(after_ref.shape[0], norm_back)
    gain_ref[...] = jnp.sum(work_ref[...], axis=0, keepdims=True)


def back_ffn_kernel(plan, count, rels, me_ref, dx_ref, p_ref, both_ref, after_ref, *refs):
    w_hbm, refs = refs[:count], refs[count:]
    if rels is not None:
        lifted_ref, keep_ref, send_ref, *refs, dboth_ref, grad_up_ref, out_sem = refs
        dlow_ref, *refs = refs
    else:
        dlow_ref, dboth_ref, *refs = refs
    dafter_ref, dmid_ref, gain_ref, work_ref, up_ref, down_ref, sems = refs
    rows, width = dx_ref.shape
    inner = down_ref.shape[0]
    up_pairs = pairs_of(plan, w_hbm, me_ref, "up", up_ref)
    down_pairs = pairs_of(plan, w_hbm, me_ref, "down", down_ref)
    load_start(down_pairs, sems.at[1])
    load_start(up_pairs, sems.at[0])
    grad_ref = lower(me_ref, dx_ref, dlow_ref)
    dlow = dlow_ref[...]
    load_wait(down_pairs, sems.at[1])
    step = width // 2
    for k in range(inner // step):
        cols = slice(k * step, (k + 1) * step)
        more = slice(inner + k * step, inner + (k + 1) * step)
        dh = dot_t(dlow, down_ref[cols, :])
        a = both_ref[:, cols]
        sig = jax.nn.sigmoid(a)
        dboth_ref[:, cols] = (dh * both_ref[:, more] * (sig * (1.0 + a * (1.0 - sig)))).astype(BF16)
        dboth_ref[:, more] = (dh * (a * sig)).astype(BF16)
    if rels is not None:
        products(lifted_ref[...], dboth_ref, grad_up_ref, grad_up_ref.shape[1])
        pairs = export(me_ref, rels, "up", grad_up_ref, 0, HALVES["up"], keep_ref, send_ref, out_sem)
    load_wait(up_pairs, sems.at[0])
    work_ref[...] = dot_t(dboth_ref[...], up_ref[...])

    lift_back(grad_ref, p_ref, after_ref, work_ref, dafter_ref, dmid_ref, gain_ref)
    if rels is not None:
        load_wait(pairs, out_sem)


def turn_kernel(plan, count, rels, me_ref, dx_ref, p_ref, after_ref, lifted_ref, *refs):
    w_hbm, refs = refs[:count], refs[count:]
    (
        keep_ref, send_ref, next_ref, hidden_ref, dlow_ref, dafter_ref, dmid_ref, gain_ref,
        dboth_ref, grad_up_ref, work_ref, up_ref, down_ref, sems, out_sem,
    ) = refs
    width = dx_ref.shape[1]
    inner = down_ref.shape[0]
    up_pairs = pairs_of(plan, w_hbm, me_ref, "up", up_ref)
    down_pairs = pairs_of(plan, w_hbm, me_ref, "down", down_ref)
    load_start(up_pairs, sems.at[0])
    load_start(down_pairs, sems.at[1])
    grad_ref = lower(me_ref, dx_ref, dlow_ref)
    dlow = dlow_ref[...]
    lifted = lifted_ref[...]
    load_wait(up_pairs, sems.at[0])
    load_wait(down_pairs, sems.at[1])
    step = width // 2
    for k in range(inner // step):
        cols = slice(k * step, (k + 1) * step)
        more = slice(inner + k * step, inner + (k + 1) * step)
        a = dot(lifted, up_ref[:, cols])
        b = dot(lifted, up_ref[:, more])
        dh = dot_t(dlow, down_ref[cols, :])
        sig = jax.nn.sigmoid(a)
        gated = a * sig
        hidden_ref[:, cols] = (gated * b).astype(BF16)
        dboth_ref[:, cols] = (dh * b * (sig * (1.0 + a * (1.0 - sig)))).astype(BF16)
        dboth_ref[:, more] = (dh * gated).astype(BF16)
    products(lifted, dboth_ref, grad_up_ref, grad_up_ref.shape[1])
    pairs = export(me_ref, rels, "up", grad_up_ref, 0, HALVES["up"], keep_ref, send_ref, out_sem)
    work_ref[...] = dot_t(dboth_ref[...], up_ref[...])
    lift_back(grad_ref, p_ref, after_ref, work_ref, dafter_ref, dmid_ref, gain_ref)
    next_ref[...] = (after_ref[...] + dot(hidden_ref[...], down_ref[...])).astype(next_ref.dtype)
    load_wait(pairs, out_sem)


def turn(plan, rels, me, dx, params, after, lifted, weights):
    rows, width = dx.shape
    inner = 2 * width
    block = sds((2 ** len(STAGES), UNIT, HALVES["up"]), BF16)
    low = sds((rows, width), BF16)
    return pl.pallas_call(
        functools.partial(turn_kernel, plan, len(weights), rels),
        out_shape=(block, block, low, sds((rows, inner), BF16), low, sds((rows, width)), low, sds((1, width))),
        in_specs=[SMEM] + [VMEM] * 4 + [ANY] * len(weights),
        out_specs=(ANY, ANY) + (VMEM,) * 6,
        scratch_shapes=[
            pltpu.VMEM((rows, 2 * inner), BF16),
            pltpu.VMEM((width, 2 * inner), BF16),
            pltpu.VMEM((rows, width), F32),
            pltpu.VMEM((width, 2 * inner), BF16),
            pltpu.VMEM((inner, width), BF16),
            pltpu.SemaphoreType.DMA((2,)),
            pltpu.SemaphoreType.DMA,
        ],
        compiler_params=pltpu.CompilerParams(vmem_limit_bytes=22 << 20),
        cost_estimate=COST,
        name="turn",
    )(me, dx, params, after, lifted, *weights)


def back_ffn(plan, me, dx, params, both, after, weights, rels=None, lifted=()):
    rows, width = dx.shape
    inner = 2 * width
    block = sds((2 ** len(STAGES), UNIT, HALVES["up"]), BF16)
    dboth = (rows, 2 * inner)
    outs = (sds((rows, width), BF16), sds(dboth, BF16), sds((rows, width)), sds((rows, width), BF16), sds((1, width)))
    specs, more = (VMEM,) * 5, []
    if rels is not None:
        outs, specs = (block, block, outs[0], *outs[2:]), (ANY, ANY, *specs[1:])
        more = [pltpu.VMEM(dboth, BF16), pltpu.VMEM((width, 2 * inner), BF16), pltpu.SemaphoreType.DMA]
    return pl.pallas_call(
        functools.partial(back_ffn_kernel, plan, len(weights), rels),
        out_shape=outs,
        in_specs=[SMEM] + [VMEM] * 4 + [ANY] * len(weights) + [VMEM] * len(lifted),
        out_specs=specs,
        scratch_shapes=[
            pltpu.VMEM((rows, width), F32),
            pltpu.VMEM((width, 2 * inner), BF16),
            pltpu.VMEM((inner, width), BF16),
            pltpu.SemaphoreType.DMA((2,)),
        ]
        + more,
        compiler_params=pltpu.CompilerParams(vmem_limit_bytes=25 << 20),
        cost_estimate=COST,
        name="back_ffn",
    )(me, dx, params, both, after, *weights, *lifted)


def back_mid_kernel(
    plan, count, me_ref, dmid_ref, p_ref, gn_ref, rg_ref, gate_ref, states_ref, kept_ref, sub_ref, *refs
):
    w_hbm, refs = refs[:count], refs[count:]
    dgpre_ref, dstates_ref, gain_ref, rsub_ref, rtotal_ref, work_ref, out_ref, sem = refs
    rows, width = dmid_ref.shape
    half = width // 2
    block = rows // SUB
    pairs = pairs_of(plan, w_hbm, me_ref, "out", out_ref)
    load_start(pairs, sem)
    load_wait(pairs, sem)
    work_ref[...] = dot_t(dmid_ref[...], out_ref[...])

    def group_back(r):
        held = rg_ref[r, :]
        for g in range(width // GROUP):
            cols = slice(g * GROUP, (g + 1) * GROUP)
            gn = gn_ref[r, cols]
            dg = work_ref[r, cols]
            e = dg * p_ref[1:2, cols]
            dv = held[:, g : g + 1] * (
                e - jnp.mean(e, axis=1, keepdims=True) - gn * jnp.mean(e * gn, axis=1, keepdims=True)
            )
            gate = gate_ref[r, cols]
            dgpre_ref[r, cols] = (dv * states_ref[g, r, :] * gate * (1.0 - gate)).astype(BF16)
            dstates_ref[g, r, :] = dv * gate
            work_ref[r, cols] = dg * gn

    over_rows(rows, group_back)
    gain_ref[...] = jnp.sum(work_ref[...], axis=0, keepdims=True)

    cos, sin = turns(p_ref, half)
    tiles = half // GROUP
    zr = [jnp.zeros((SUB, GROUP), F32)] * tiles
    zi = [jnp.zeros((SUB, GROUP), F32)] * tiles
    for j in reversed(range(block)):
        at = pl.ds(j, SUB, stride=block)
        for t in range(tiles):
            kept = kept_ref[t, at, :]
            qr = dstates_ref[t, at, :] + zr[t]
            qi = dstates_ref[tiles + t, at, :] + zi[t]
            zr[t] = kept * (cos[t] * qr + sin[t] * qi)
            zi[t] = kept * (cos[t] * qi - sin[t] * qr)
    zr, zi = jnp.concatenate(zr, axis=1), jnp.concatenate(zi, axis=1)
    rsub_ref[0] = zr
    rsub_ref[1] = zi
    tr = jnp.zeros((1, half), F32)
    ti = jnp.zeros((1, half), F32)
    for k in reversed(range(SUB)):
        ar, ai = sub_ref[0, k : k + 1, :], sub_ref[1, k : k + 1, :]
        tr, ti = ar * tr + ai * ti + zr[k : k + 1], ar * ti - ai * tr + zi[k : k + 1]
    rtotal_ref[0:1, :] = tr
    rtotal_ref[1:2, :] = ti


def back_mid(plan, me, dmid, params, gn, rg, gate, states, kept, sub, weights):
    rows, width = dmid.shape
    half = width // 2
    return pl.pallas_call(
        functools.partial(back_mid_kernel, plan, len(weights)),
        out_shape=(
            sds((rows, width), BF16),
            sds((width // GROUP, rows, GROUP)),
            sds((1, width)),
            sds((2, SUB, half)),
            sds((2, half)),
        ),
        in_specs=[SMEM] + [VMEM] * 8 + [ANY] * len(weights),
        out_specs=(VMEM,) * 5,
        scratch_shapes=[
            pltpu.VMEM((rows, width), F32),
            pltpu.VMEM((width, width), BF16),
            pltpu.SemaphoreType.DMA,
        ],
        compiler_params=pltpu.CompilerParams(vmem_limit_bytes=11 << 20),
        cost_estimate=COST,
        name="back_mid",
    )(me, dmid, params, gn, rg, gate, states, kept, sub, *weights)


def back_two_kernel(
    plan, count, rels, spare, me_ref, x_ref, p_ref, dafter_ref, dgpre_ref, dstates_ref, states_ref, kept_ref, rate_ref, cpre_ref,
    first_ref, sub_ref, rsub_ref, every_ref, revery_ref, *refs
):
    w_hbm, extra, refs = refs[:count], refs[count : count + spare], refs[count + spare :]
    if rels is not None:
        normed_ref, *extra = extra
        keep_ref, send_ref, dx_ref, gains_ref, *refs, mix_ref, held_ref, out_sem = refs
        dmixin_ref, *refs = refs
    else:
        dmixin_ref, dx_ref, gains_ref, *refs = refs
    work_ref, q_ref, turn_ref, start_ref, w_ref, sem = refs
    rows, width = x_ref.shape
    half = width // 2
    block = rows // SUB
    pairs = pairs_of(plan, w_hbm, me_ref, "mix", w_ref)
    load_start(pairs, sem)
    zr = jnp.zeros((1, half), F32)
    zi = jnp.zeros((1, half), F32)
    for k in reversed(range(every_ref.shape[0])):
        at = k ^ me_ref[3]
        ar, ai = every_ref[at, 0:1, :], every_ref[at, 1:2, :]
        later = k > me_ref[0]
        nr = ar * zr + ai * zi + revery_ref[at, 0:1, :]
        ni = ar * zi - ai * zr + revery_ref[at, 1:2, :]
        zr = jnp.where(later, nr, zr)
        zi = jnp.where(later, ni, zi)
    for k in reversed(range(SUB)):
        start_ref[0, k : k + 1, :] = zr
        start_ref[1, k : k + 1, :] = zi
        ar, ai = sub_ref[0, k : k + 1, :], sub_ref[1, k : k + 1, :]
        zr, zi = (
            ar * zr + ai * zi + rsub_ref[0, k : k + 1, :],
            ar * zi - ai * zr + rsub_ref[1, k : k + 1, :],
        )
    cos, sin = turns(p_ref, half)
    tiles = half // GROUP
    zr = parts(start_ref, 0, tiles)
    zi = parts(start_ref, 1, tiles)
    angle = [jnp.zeros((SUB, GROUP), F32)] * tiles
    for j in reversed(range(block)):
        at = pl.ds(j, SUB, stride=block)
        before = pl.ds(max(j - 1, 0), SUB, stride=block)
        for t in range(tiles):
            kept = kept_ref[t, at, :]
            qr = dstates_ref[t, at, :] + zr[t]
            qi = dstates_ref[tiles + t, at, :] + zi[t]
            q_ref[t, at, :] = qr
            q_ref[tiles + t, at, :] = qi
            zr[t] = kept * (cos[t] * qr + sin[t] * qi)
            zi[t] = kept * (cos[t] * qi - sin[t] * qr)
            if j:
                sr, si = states_ref[t, before, :], states_ref[tiles + t, before, :]
            else:
                sr, si = (first_ref[k, :, t * GROUP : (t + 1) * GROUP] for k in range(2))
            turn_ref[t, at, :] = zr[t] * sr + zi[t] * si
            angle[t] = angle[t] + (zi[t] * sr - zr[t] * si)
    gains_ref[1:2, half:] = jnp.sum(jnp.concatenate(angle, axis=1), axis=0, keepdims=True)

    def activations(r):
        for t in range(tiles):
            rate = rate_ref[r, t * GROUP : (t + 1) * GROUP]
            left = 1.0 - rate
            meet = jnp.zeros_like(rate)
            for k in range(2):
                cols = slice((k * tiles + t) * GROUP, (k * tiles + t + 1) * GROUP)
                pre = cpre_ref[r, cols]
                sig = jax.nn.sigmoid(pre)
                q = q_ref[k * tiles + t, r, :]
                meet = meet + q * (pre * sig)
                dmixin_ref[r, cols] = (left * q * (sig * (1.0 + pre * (1.0 - sig)))).astype(BF16)
            dfpre = left * (turn_ref[t, r, :] - rate * meet)
            dmixin_ref[r, 2 * width + t * GROUP : 2 * width + (t + 1) * GROUP] = dfpre.astype(BF16)
            turn_ref[t, r, :] = dfpre
        dmixin_ref[r, width : 2 * width] = dgpre_ref[r, :]

    over_rows(rows, activations)
    for t in range(tiles):
        gains_ref[1:2, t * GROUP : (t + 1) * GROUP] = jnp.sum(turn_ref[t], axis=0, keepdims=True)
    load_wait(pairs, sem)
    work_ref[...] = dot_t(dmixin_ref[...], w_ref[:, : dmixin_ref.shape[1]])

    def norm_back(r):
        x = x_ref[r, :].astype(F32)
        scale = lax.rsqrt(jnp.mean(x * x, axis=1, keepdims=True) + EPS)
        normal = x * scale
        dn = work_ref[r, :]
        e = dn * p_ref[0:1, :]
        dx_ref[r, :] = dafter_ref[r, :] + scale * (e - normal * jnp.mean(e * normal, axis=1, keepdims=True))
        work_ref[r, :] = dn * normal

    over_rows(rows, norm_back)
    gains_ref[0:1, :] = jnp.sum(work_ref[...], axis=0, keepdims=True)

    if rels is None:
        return
    held_ref[...] = jnp.zeros_like(held_ref)
    for k in range(spare // 3):
        two, mid_gain, ffn_gain = (gains_ref, *extra)[3 * k : 3 * k + 3]
        held_ref[4 * k : 4 * k + 1, :] = two[0:1, :]
        held_ref[4 * k + 1 : 4 * k + 2, :] = mid_gain[...]
        held_ref[4 * k + 2 : 4 * k + 3, :] = ffn_gain[...]
        held_ref[4 * k + 3 : 4 * k + 4, :] = two[1:2, :]
    normed = normed_ref[...]
    products(normed, dmixin_ref, mix_ref, width)
    products(normed, dmixin_ref, mix_ref, half, 2 * width, width)
    mix_ref[:, width + half :] = jnp.transpose(held_ref[...]).astype(BF16)
    pairs = export(me_ref, rels, "cell", mix_ref, 0, HALVES["cell"], keep_ref, send_ref, out_sem)
    load_wait(pairs, out_sem)


def back_two(plan, me, x, params, dafter, dgpre, dstates, states, kept, rate, cpre, first, sub, rsub, every, revery, weights, rels=None, extra=()):
    rows, width = x.shape
    half = width // 2
    size = 2 * width + half
    block = sds((2 ** len(STAGES), UNIT, HALVES["cell"]), BF16)
    scratch = [
        pltpu.VMEM((rows, width), F32),
        pltpu.VMEM((width // GROUP, rows, GROUP), F32),
        pltpu.VMEM((half // GROUP, rows, GROUP), F32),
        pltpu.VMEM((2, SUB, half), F32),
        pltpu.VMEM((width, mix_width(plan, width)), BF16),
        pltpu.SemaphoreType.DMA,
    ]
    if rels is None:
        first_out, specs, more = (sds((rows, size), BF16),), (VMEM,), []
    else:
        first_out, specs = (block, block), (ANY, ANY)
        scratch.insert(0, pltpu.VMEM((rows, size), BF16))
        more = [pltpu.VMEM((width, 2 * HALVES["cell"]), BF16), pltpu.VMEM((GROUP, width), F32), pltpu.SemaphoreType.DMA]
    return pl.pallas_call(
        functools.partial(back_two_kernel, plan, len(weights), rels, len(extra)),
        out_shape=first_out + (sds((rows, width)), sds((2, width))),
        in_specs=[SMEM] + [VMEM] * 14 + [ANY] * len(weights) + [VMEM] * len(extra),
        out_specs=specs + (VMEM, VMEM),
        scratch_shapes=scratch + more,
        compiler_params=pltpu.CompilerParams(vmem_limit_bytes=18 << 20),
        cost_estimate=COST,
        name="back_two",
    )(me, x, params, dafter, dgpre, dstates, states, kept, rate, cpre, first, sub, rsub, every, revery, *weights, *extra)


def row_product(left, right):
    return lax.dot_general(left, right, (((0,), (0,)), ((), ())), preferred_element_type=F32)


def export(info_ref, rels, name, grad, column, columns, keep_ref, send_ref, sem):
    chip, core = info_ref[1], info_ref[2]
    pairs = []
    for half, target in ((1 - core, send_ref), (core, keep_ref)):
        for b, (zero, one) in enumerate(zip(*rels)):
            block = chip ^ (zero + half * (one - zero))
            if name == "down":
                row, left = block * (2 * UNIT) + half * UNIT, 0
            else:
                row, left = block * UNIT, half * HALVES[name]
            pairs.append(
                (
                    grad.at[pl.ds(pl.multiple_of(row, UNIT), UNIT), pl.ds(pl.multiple_of(left, GROUP), columns)],
                    target.at[b, :, pl.ds(column, columns)],
                )
            )
    load_start(pairs, sem)
    return pairs


def products(left, right_ref, grad_ref, size, source=0, target=0):
    step = HALVES["out"]
    for k in range(0, size, step):
        right = right_ref[:, source + k : source + k + step]
        grad_ref[:, target + k : target + k + step] = row_product(left, right).astype(BF16)


def grad_od_kernel(
    rels, info_ref, gated_ref, dmid_ref, hidden_ref, dlow_ref, normed_ref, dgpre_ref, keep_ref, send_ref,
    out_ref, gate_ref, down_ref, sem,
):
    width = dlow_ref.shape[1]
    products(hidden_ref[...], dlow_ref, down_ref, width)
    at = HALVES["out"] + HALVES["gate"]
    pairs = export(info_ref, rels, "down", down_ref, at, width, keep_ref, send_ref, sem)
    products(gated_ref[...], dmid_ref, out_ref, width)
    pairs += export(info_ref, rels, "out", out_ref, 0, HALVES["out"], keep_ref, send_ref, sem)
    products(normed_ref[...], dgpre_ref, gate_ref, width)
    pairs += export(info_ref, rels, "gate", gate_ref, HALVES["out"], HALVES["gate"], keep_ref, send_ref, sem)
    load_wait(pairs, sem)


def grad_od(rels, info, gated, dmid, hidden, dlow, normed, dgpre):
    width = dlow.shape[1]
    shape = sds((len(rels[0]), UNIT, HALVES["out"] + HALVES["gate"] + width), BF16)
    return pl.pallas_call(
        functools.partial(grad_od_kernel, rels),
        out_shape=(shape, shape),
        in_specs=[SMEM] + [VMEM] * 6,
        out_specs=(ANY, ANY),
        scratch_shapes=[
            pltpu.VMEM((width, width), BF16),
            pltpu.VMEM((width, width), BF16),
            pltpu.VMEM((hidden.shape[1], width), BF16),
            pltpu.SemaphoreType.DMA,
        ],
        compiler_params=pltpu.CompilerParams(vmem_limit_bytes=11 << 20),
        cost_estimate=COST,
        name="grad_od",
    )(info, gated, dmid, hidden, dlow, normed, dgpre)


def table_kernel(plan, count, me_ref, *refs):
    sources, (table_ref, held_ref, sem) = refs[:count], refs[count:]
    pairs = pairs_of(plan, sources, me_ref, "small", held_ref)
    load_start(pairs, sem)
    load_wait(pairs, sem)
    depth = table_ref.shape[0]
    half = table_ref.shape[2] // 2
    table = jnp.transpose(held_ref[:, GROUP:].astype(F32))
    table_ref[...] = jnp.zeros_like(table_ref)
    for l in range(depth):
        chan = table[3 * depth + l : 3 * depth + l + 1]
        table_ref[l, 0:3, :] = table[3 * l : 3 * l + 3]
        table_ref[l, 3:4, :half] = chan[:, :half]
        table_ref[l, 3:4, half:] = jnp.cos(chan[:, half:])
        table_ref[l, 4:5, :half] = jnp.sin(chan[:, half:])


def table_of(plan, me, weights, depth, width):
    return pl.pallas_call(
        functools.partial(table_kernel, plan, len(weights)),
        out_shape=sds((depth, 8, width)),
        in_specs=[SMEM] + [ANY] * len(weights),
        out_specs=VMEM,
        scratch_shapes=[pltpu.VMEM((width, 2 * GROUP), BF16), pltpu.SemaphoreType.DMA],
        compiler_params=pltpu.CompilerParams(vmem_limit_bytes=6 << 20),
        cost_estimate=COST,
        name="table",
    )(me, *weights)


def swap(x, bits):
    count = lax.axis_size("dp") * lax.axis_size("seq")
    return lax.ppermute(x, ALL, [(i, i ^ bits[i % 2]) for i in range(count)])


class Order:
    def __init__(self):
        self.last = None

    def step(self, *values):
        if self.last is not None:
            values = lax.optimization_barrier(values + (self.last,))[: len(values)]
        self.last = values[0]
        return values

    def join(self, *moves, cores=()):
        values = [move.got for move in moves]
        for move in cores:
            values += [move.last_core, move.held_core]
        values = list(self.step(*values))
        for move in moves:
            move.got = values.pop(0)
        for move in cores:
            move.last_core, move.held_core = values.pop(0), values.pop(0)


    def pass_on(self, *moves):
        for move in moves:
            move.ready()
        for move, value in zip(moves, self.step(*(move.out for move in moves))):
            move.out = value
            move.send()


def rels_of(stages):
    rels = ([0], [0])
    for bits in stages:
        for core in range(2):
            rels[core].extend([rel ^ bits[core] for rel in rels[core]])
    return rels


class Spread:
    def __init__(self, unit, stages):
        self.held, self.stages, self.at = unit[None], stages, 0
        self.got = None

    def join(self):
        if self.got is not None:
            self.held = jnp.concatenate([self.held, self.got])

    def ready(self):
        self.join()
        self.out = self.held

    def send(self):
        self.held = self.out
        one, two = self.stages[self.at]
        self.at += 1
        self.got = swap(self.held, (2 * one, 2 * two))

    def end(self):
        self.near, self.last = self.held, self.got
        self.last_core = swap(self.last, (1, 1))

    def near_core(self):
        self.held_core = swap(self.held, (1, 1))

    def arrays(self):
        return (self.near, self.held_core, self.last, self.last_core)

    def sources(self):
        rels = rels_of(self.stages)
        half = len(rels[0]) // 2
        low = tuple(tuple(rel[:half]) for rel in rels)
        high = tuple(tuple(rel[half:]) for rel in rels)
        return ((0, low), (1, low), (0, high), (1, high))


class Reduce:
    def __init__(self, keep, send, stages):
        self.held, self.stages = keep, list(stages)
        self.got = swap(send, (1, 1))

    def add(self):
        half = self.held.shape[0] // 2
        if not half:
            return self.held[0].astype(F32) + self.got[0].astype(F32)

        def joined(part):
            return (self.held[part].astype(F32) + self.got[part].astype(F32)).astype(BF16)

        self.held, self.out = joined(slice(0, half)), joined(slice(half, None))
        self.got = None

    def ready(self):
        if self.got is not None:
            self.add()

    def send(self):
        one, two = self.stages.pop()
        self.got = swap(self.out, (2 * one, 2 * two))


def exchange(x, order=None):
    other = swap(x, (1, 1))
    if order is not None:
        (other,) = order.step(other)
    pair = jnp.stack([x, other])
    got = [swap(pair, (k, k)) for k in range(2, lax.axis_size("seq"), 2)]
    return jnp.concatenate([pair] + got)


def finish_kernel(info_ref, *refs):
    depth = (len(refs) - 5) // 3
    mine, other, downs = refs[:depth], refs[depth : 2 * depth], refs[2 * depth : 3 * depth]
    mix_ref, out_ref, up_ref, down_ref, tail_ref = refs[3 * depth :]
    width = down_ref.shape[2]
    size = HALVES["cell"]

    def place(first, second):
        for l in range(depth):
            rest = width - size
            mix_ref[l, :, :size] = first[l][:, :size]
            mix_ref[l, :, size:width] = second[l][:, :rest]
            mix_ref[l, :, 2 * width :] = second[l][:, rest : size - GROUP]
            at = size
            for name, ref, begin in (("out", out_ref, 0), ("gate", mix_ref, width), ("up", up_ref, 0)):
                step = HALVES[name]
                ref[l, :, begin : begin + step] = first[l][:, at : at + step]
                ref[l, :, begin + step : begin + 2 * step] = second[l][:, at : at + step]
                at += step
        tail_ref[...] = second[0][:, size - GROUP : size]

    @pl.when(info_ref[2] == 0)
    def _():
        place(mine, other)

    @pl.when(info_ref[2] == 1)
    def _():
        place(other, mine)

    for l in range(depth):
        down_ref[l] = downs[l][:, downs[l].shape[1] - width :]


def finish(info, mine, other, downs, shapes):
    share = mine[0].shape[0]
    return pl.pallas_call(
        finish_kernel,
        out_shape=tuple(sds(shape) for shape in shapes) + (sds((share, GROUP)),),
        in_specs=[SMEM] + [VMEM] * (3 * len(mine)),
        out_specs=(VMEM,) * 5,
        compiler_params=pltpu.CompilerParams(vmem_limit_bytes=8 << 20),
        cost_estimate=COST,
        name="finish",
    )(info, *mine, *other, *downs)


def layer_params(gains, chan):
    half = chan.shape[0] // 2
    angle = chan[half:]
    rows = [
        gains[0],
        gains[1],
        gains[2],
        jnp.concatenate([chan[:half], jnp.cos(angle)]),
        jnp.concatenate([jnp.sin(angle), jnp.zeros((half,), F32)]),
    ]
    return jnp.concatenate([jnp.stack(rows), jnp.zeros((3, 2 * half), F32)], axis=0)


STAGES = ((4, 8), (8, 4), (1, 2), (2, 1))
LATER = ((1, 2), (4, 8), (8, 4), (2, 1))
UPPER = (STAGES, LATER, STAGES)


def small_of(gains, chan_params):
    depth, _, share = gains.shape
    return jnp.concatenate(
        [gains.reshape(depth * 3, share).T, chan_params.T, jnp.zeros((share, GROUP - 4 * depth), BF16)], axis=1
    )


def info_of(lengths, rows, turned):
    where = lax.axis_index("seq")
    base = where * rows
    ends = [lengths[0, 0]]
    for j in range(1, lengths.shape[1]):
        ends.append(ends[-1] + lengths[0, j])
    chip = (lax.axis_index("dp") * lax.axis_size("seq") + where) // 2
    values = [where, chip, where % 2, where if turned else jnp.zeros_like(where), ends[-1] - base]
    values += [end - lengths[0, j] - base for j, end in enumerate(ends)]
    return jnp.stack([value.astype(jnp.int32) for value in values])


def plain_body(stream, w_mix, w_out, w_up, w_down, gains, chan_params, lengths, cotangent):
    rows, width = stream.shape
    depth = w_mix.shape[0]
    info = info_of(lengths, rows, False)
    small = small_of(gains, chan_params)
    table = lax.all_gather(small, ALL, axis=0, tiled=True)[:, : 4 * depth].T.astype(F32)
    params = [layer_params(table[3 * l : 3 * l + 3], table[3 * depth + l]) for l in range(depth)]
    weights = [
        tuple(lax.all_gather(w[l], ALL, axis=0, tiled=True) for w in (w_mix, w_out, w_up, w_down))
        for l in range(depth)
    ]
    x = stream
    saved = []
    for l in range(depth):
        head = front(None, info, x, params[l], weights[l])
        every = lax.all_gather(head[-1], "seq")
        middle = mid(None, info, x, params[l], head[2], head[4], head[5], head[6], every, weights[l])
        tail = ffn(None, info, middle[5], middle[6], weights[l], F32)
        saved.append((x, every, head, middle, tail))
        x = tail[-1]
    mixed = x.astype(BF16)
    dx = cotangent
    sums = [None] * depth
    for l in reversed(range(depth)):
        x, every, (normed, cpre, gate, rate, kept, feed, sub, _), middle, (both, hidden, _) = saved[l]
        states, first, gn, rg, gated, after, lifted = middle
        dlow, dboth, dafter, dmid, ffn_gain = back_ffn(None, info, dx, params[l], both, after, weights[l])
        dgpre, dstates, mid_gain, rsub, rtotal = back_mid(
            None, info, dmid, params[l], gn, rg, gate, states, kept, sub, weights[l]
        )
        revery = lax.all_gather(rtotal, "seq")
        dmixin, dx, gains_b = back_two(
            None, info, x, params[l], dafter, dgpre, dstates, states, kept, rate, cpre, first, sub, rsub, every, revery,
            weights[l],
        )
        grads = [row_product(normed, dmixin), row_product(gated, dmid), row_product(lifted, dboth), row_product(hidden, dlow)]
        grads.append(jnp.stack([gains_b[0], mid_gain[0], ffn_gain[0], gains_b[1]], axis=1))
        sums[l] = [lax.psum_scatter(g.astype(BF16), ALL, scatter_dimension=0, tiled=True).astype(F32) for g in grads]
    outs = [jnp.stack([sums[l][k] for l in range(depth)]) for k in range(5)]
    tail = outs.pop()
    return (mixed, dx, *outs, jnp.swapaxes(tail[:, :, :3], 1, 2), tail[:, :, 3])


def fast_body(stream, w_mix, w_out, w_up, w_down, gains, chan_params, lengths, cotangent):
    rows, width = stream.shape
    depth, share, mix_cols = w_mix.shape
    info = info_of(lengths, rows, True)
    small = small_of(gains, chan_params)
    core = lax.axis_index("seq") % 2
    padding = jnp.zeros((share, 2 * HALVES["mix"] - mix_cols - GROUP), BF16)
    halves = ([], [])
    for l in range(depth):
        mix = jnp.concatenate([w_mix[l], padding, small if l == 0 else jnp.zeros_like(small)], axis=1)
        for h in range(2):
            for w, size in ((mix, HALVES["mix"]), (w_out[l], HALVES["out"]), (w_up[l], HALVES["up"])):
                halves[h].append(w[:, h * size : (h + 1) * size])
    halves = [jnp.concatenate(half, axis=1) for half in halves]
    mine = jnp.where(core == 0, halves[0], halves[1])
    other = swap(jnp.where(core == 0, halves[1], halves[0]), (1, 1))
    units = jnp.where(core == 0, jnp.concatenate([mine, other]), jnp.concatenate([other, mine]))
    joint = HALVES["mix"] + HALVES["out"]
    size = joint + HALVES["up"]
    mos, uds = [], []
    for l in range(depth):
        unit = units[:, l * size : (l + 1) * size]
        stages = LATER if l else STAGES
        mos.append(Spread(unit[:, :joint], stages))
        uds.append(Spread(jnp.concatenate([unit[:, joint:], w_down[l]], axis=1), stages))
    plan = {
        "mix": (0, HALVES["mix"]),
        "out": (HALVES["mix"], HALVES["out"]),
        "small": (HALVES["mix"] - GROUP, GROUP),
        "up": (0, HALVES["up"]),
        "down": (HALVES["up"], width),
    }
    plans = [dict(plan, sources=mo.sources()) for mo in mos]

    order = Order()
    mo, ud = mos[0], uds[0]
    later = [move for l in range(1, depth) for move in (mos[l], uds[l])]
    order.pass_on(ud, mo, *later)
    order.join(ud, mo, *later)
    order.pass_on(mo, ud, *later)
    order.join(mo, ud)
    order.pass_on(mo, ud)
    order.join(mo, *later[:1])
    order.pass_on(mo, *later[:1])
    mo.near_core()
    order.join(ud, *later[1:2])
    if later:
        order.pass_on(*later[1:2])
    order.join(mo, *later[:1])
    mo.end()
    order.pass_on(ud)
    ud.near_core()
    x = stream
    saved = []
    params = None
    for l in range(depth):
        mo, ud, plan = mos[l], uds[l], plans[l]
        more = l + 1 < depth
        order.join(cores=(mo,))
        if l == 0:
            params = table_of(plan, info, mo.arrays(), depth, width)
        (layer,) = order.step(params[l])
        head = front(plan, info, x, layer, mo.arrays())
        (total,) = order.step(head[-1])
        if more:
            order.join(ud, uds[l + 1])
        else:
            order.join(ud)
        ud.end()
        every = exchange(order.step(total)[0])
        (every,) = order.step(every)
        if more:
            order.pass_on(mos[l + 1])
            mos[l + 1].near_core()
        middle = mid(plan, info, x, layer, head[2], head[4], head[5], head[6], order.step(every)[0], mo.arrays())
        middle = (*middle[:-1], *order.step(middle[-1]))
        if more:
            order.join(mos[l + 1], cores=(ud,))
            mos[l + 1].end()
            order.pass_on(uds[l + 1])
            uds[l + 1].near_core()
        else:
            order.join(cores=(ud,))
        if more:
            tail = ffn(plan, info, middle[5], middle[6], ud.arrays(), F32)
            saved.append((x, every, head, middle, tail, layer))
            (x,) = order.step(tail[-1])
    later_stages = UPPER if depth > 1 else (STAGES,) * 3
    keep, send, mixed, hidden, dlow, dafter, dmid, ffn_gain = turn(
        plan, rels_of(later_stages[0]), info, cotangent, layer, middle[5], middle[6], ud.arrays()
    )
    saved.append((x, every, head, middle, (None, hidden, None), layer))
    above = None
    sums = [None] * depth
    extra = ()
    for l in reversed(range(depth)):
        x, every, (normed, cpre, gate, rate, kept, feed, sub, _), middle, (both, hidden, _), layer = saved[l]
        states, first, gn, rg, gated, after, lifted = middle
        plan = plans[l]
        u_stages, od_stages, c_stages = UPPER if l else (STAGES,) * 3
        if above:
            (dx,) = order.step(dx)
            keep, send, dlow, dafter, dmid, ffn_gain = back_ffn(
                plan, info, dx, layer, both, after, uds[l].arrays(), rels_of(u_stages), (lifted,)
            )
        (keep,) = order.step(keep)
        u = Reduce(keep, send, u_stages)
        if above:
            u_up, od_up, c_up = above
            order.join(od_up, c_up, u_up)
            od_up.ready()
            order.pass_on(c_up, u_up)
        (dmid,) = order.step(dmid)
        dgpre, dstates, mid_gain, rsub, rtotal = back_mid(
            plan, info, dmid, layer, gn, rg, gate, states, kept, sub, mos[l].arrays()
        )
        (rtotal,) = order.step(rtotal)
        order.join(u, *((c_up, u_up) if above else ()))
        revery = exchange(rtotal, order)
        waiting = [u] + ([od_up, c_up, u_up] if above else [])
        for move in waiting:
            move.ready()
        (dlow,) = order.step(dlow)
        od = Reduce(
            *grad_od(rels_of(od_stages), info, gated, dmid, hidden, dlow, normed, dgpre), od_stages
        )
        (od.held,) = order.step(od.held)
        (revery,) = order.step(revery)
        order.pass_on(*waiting)
        (dstates,) = order.step(dstates)
        more = (normed,)
        if l == 0:
            more = (normed, mid_gain, ffn_gain, *extra)
        keep, send, dx, gains_b = back_two(
            plan, info, x, layer, dafter, dgpre, dstates, states, kept, rate, cpre, first, sub, rsub, every, revery,
            mos[l].arrays(), rels_of(c_stages), more,
        )
        extra = (gains_b, mid_gain, ffn_gain) + extra
        (keep,) = order.step(keep)
        c = Reduce(keep, send, c_stages)
        order.join(*waiting, od)
        order.pass_on(od, u, *((od_up, c_up) if above else ()))
        above = sums[l] = (u, od, c)
    u, od, c = sums[0]
    others = ()
    if depth > 1:
        u_up, od_up, c_up = sums[1]
        others = (od_up, c_up)
    for moves in ((c,), (od, *others), (u,), (c,), (od,), (u,), (c,), (od,), (c,)):
        order.join(*moves)
        order.pass_on(*moves)
    mine, other, downs = [], [], []
    for u, od, c in reversed(sums):
        ready = od.add()
        line = jnp.concatenate([c.add(), ready[:, : HALVES["out"] + HALVES["gate"]], u.add()], axis=1)
        first, second = line[:share], line[share:]
        mine.insert(0, jnp.where(core == 0, first, second))
        other.insert(0, swap(jnp.where(core == 0, second, first), (1, 1)))
        downs.insert(0, ready)
    shapes = (w_mix.shape, w_out.shape, w_up.shape, w_down.shape)
    *grads, tail = finish(info, mine, other, downs, shapes)
    tail = tail[:, : 4 * depth].T.reshape(depth, 4, share)
    return (mixed, dx, *grads, tail[:, :3], tail[:, 3])


def body(stream, w_mix, *others):
    n_dp, n_seq = lax.axis_size("dp"), lax.axis_size("seq")
    fast = n_seq == 8 and n_dp == 4 and 2 * w_mix.shape[1] == UNIT and w_mix.shape[0] == 2
    return (fast_body if fast else plain_body)(stream, w_mix, *others)


def solution(mesh):
    placed = (
        P(ALL, None),
        P(None, ALL, None),
        P(None, ALL, None),
        P(None, ALL, None),
        P(None, ALL, None),
        P(None, None, ALL),
        P(None, ALL),
        P("dp", None),
        P(ALL, None),
    )
    return jax.shard_map(
        body,
        mesh=mesh,
        in_specs=placed,
        out_specs=(
            P(ALL, None),
            P(ALL, None),
            P(None, ALL, None),
            P(None, ALL, None),
            P(None, ALL, None),
            P(None, ALL, None),
            P(None, None, ALL),
            P(None, ALL),
        ),
        check_vma=False,
    )
```

```python
import functools

import jax
import jax.numpy as jnp
from jax import lax
from jax.experimental import pallas as pl
from jax.experimental.pallas import tpu as pltpu
from jax.sharding import PartitionSpec as P

GROUP = 128
EPS = 1e-06
SUB = 8
UNIT = 48
HALVES = {"mix": 1024, "out": 384, "up": 1536, "gate": 384, "cell": 640}
ROWS = 32
F32 = jnp.float32
BF16 = jnp.bfloat16
ALL = ("dp", "seq")
VMEM = pl.BlockSpec(memory_space=pltpu.VMEM)
SMEM = pl.BlockSpec(memory_space=pltpu.SMEM)
ANY = pl.BlockSpec(memory_space=pl.ANY)
COST = pl.CostEstimate(flops=1000, bytes_accessed=1000, transcendentals=0)


def sds(shape, dtype=F32):
    return jax.ShapeDtypeStruct(shape, dtype)


def over_rows(total, body):
    def step(i, _):
        body(pl.ds(pl.multiple_of(i * ROWS, ROWS), ROWS))
        return 0

    lax.fori_loop(0, total // ROWS, step, 0)


def dot(left, right):
    return jnp.dot(left, right, preferred_element_type=F32)


def dot_t(left, right):
    return lax.dot_general(left, right, (((1,), (1,)), ((), ())), preferred_element_type=F32)


def cmul(ar, ai, br, bi):
    return ar * br - ai * bi, ar * bi + ai * br


def power(cos, sin, times):
    while times > 1:
        cos, sin = cos * cos - sin * sin, 2.0 * cos * sin
        times //= 2
    return cos, sin


def turns(p_ref, half):
    cos, sin = p_ref[3:4, half:], p_ref[4:5, :half]
    return tuple(
        [jnp.broadcast_to(part[:, t * GROUP : (t + 1) * GROUP], (SUB, GROUP)) for t in range(half // GROUP)]
        for part in (cos, sin)
    )


def parts(ref, k, tiles):
    return [ref[k, :, t * GROUP : (t + 1) * GROUP] for t in range(tiles)]


def mix_width(plan, width):
    return 2 * width + width // 2 if plan is None else 2 * HALVES["mix"]


def load_start(pairs, sem):
    for source, target in pairs:
        pltpu.make_async_copy(source, target, sem).start()


def load_wait(pairs, sem):
    for source, target in pairs:
        pltpu.make_async_copy(source, target, sem).wait()


def pairs_of(plan, sources, me_ref, name, target):
    if plan is None:
        return [(sources[{"mix": 0, "out": 1, "up": 2, "down": 3}[name]], target)]
    chip, core = me_ref[1], me_ref[2]
    column, columns = plan[name]
    pairs = []
    for source, (other_core, rels) in enumerate(plan["sources"]):
        half = core ^ other_core
        for b, (zero, one) in enumerate(zip(*rels)):
            block = chip ^ (zero + half * (one - zero))
            if name == "down":
                row, left = block * (2 * UNIT) + half * UNIT, 0
            elif name == "small":
                row, left = block * UNIT, half * GROUP
            else:
                row, left = block * UNIT, half * HALVES[name]
            to = target.at[pl.ds(pl.multiple_of(row, UNIT), UNIT), pl.ds(pl.multiple_of(left, GROUP), columns)]
            pairs.append((sources[source].at[b, :, pl.ds(column, columns)], to))
    return pairs


def front_kernel(
    plan, count, me_ref, x_ref, p_ref, *refs
):
    w_hbm, refs = refs[:count], refs[count:]
    (
    normed_ref, cpre_ref, gate_ref, rate_ref, kept_ref, feed_ref, sub_ref, total_ref,
    w_ref, sem,
    ) = refs
    rows, width = x_ref.shape
    half = width // 2
    block = rows // SUB
    pairs = pairs_of(plan, w_hbm, me_ref, "mix", w_ref)
    load_start(pairs, sem)

    def norm(r):
        x = x_ref[r, :].astype(F32)
        scale = lax.rsqrt(jnp.mean(x * x, axis=1, keepdims=True) + EPS)
        normed_ref[r, :] = (x * scale * p_ref[0:1, :]).astype(BF16)

    over_rows(rows, norm)
    load_wait(pairs, sem)
    normed = normed_ref[...]
    rate = jax.nn.sigmoid(dot(normed, w_ref[:, 2 * width : 2 * width + half]) + p_ref[3:4, :half])
    rate_ref[...] = rate
    at = lax.broadcasted_iota(jnp.int32, (rows, GROUP), 0)
    fresh = at == me_ref[5]
    for j in range(6, me_ref.shape[0]):
        fresh = jnp.logical_or(fresh, at == me_ref[j])
    tiles = half // GROUP
    for t in range(tiles):
        kept_ref[t] = jnp.where(fresh, 0.0, rate[:, t * GROUP : (t + 1) * GROUP])
    for k in range(2):
        cols = slice(k * half, (k + 1) * half)
        pre = dot(normed, w_ref[:, cols])
        cpre_ref[:, cols] = pre
        feed = (1.0 - rate_ref[...]) * (pre * jax.nn.sigmoid(pre))
        for t in range(tiles):
            feed_ref[k * tiles + t] = feed[:, t * GROUP : (t + 1) * GROUP]
    cos, sin = turns(p_ref, half)

    mag = [jnp.ones((SUB, GROUP), F32)] * tiles
    br = [jnp.zeros((SUB, GROUP), F32)] * tiles
    bi = [jnp.zeros((SUB, GROUP), F32)] * tiles
    for j in range(block):
        at = pl.ds(j, SUB, stride=block)
        for t in range(tiles):
            kept = kept_ref[t, at, :]
            tr, ti = cmul(cos[t], sin[t], br[t], bi[t])
            br[t] = kept * tr + feed_ref[t, at, :]
            bi[t] = kept * ti + feed_ref[tiles + t, at, :]
            mag[t] = mag[t] * kept
    mag, br, bi = (jnp.concatenate(part, axis=1) for part in (mag, br, bi))
    far_cos, far_sin = power(jnp.concatenate(cos, axis=1), jnp.concatenate(sin, axis=1), block)
    ar, ai = mag * far_cos, mag * far_sin
    sub_ref[0] = ar
    sub_ref[1] = ai
    sub_ref[2] = br
    sub_ref[3] = bi
    one_r, one_i, sum_r, sum_i = (part[0:1] for part in (ar, ai, br, bi))
    for k in range(1, SUB):
        kr, ki = ar[k : k + 1], ai[k : k + 1]
        one_r, one_i = cmul(kr, ki, one_r, one_i)
        sum_r, sum_i = cmul(kr, ki, sum_r, sum_i)
        sum_r = sum_r + br[k : k + 1]
        sum_i = sum_i + bi[k : k + 1]
    total_ref[0:1, :] = one_r
    total_ref[1:2, :] = one_i
    total_ref[2:3, :] = sum_r
    total_ref[3:4, :] = sum_i
    for k in range(2):
        cols = slice(width + k * half, width + (k + 1) * half)
        gate_ref[:, k * half : (k + 1) * half] = jax.nn.sigmoid(dot(normed, w_ref[:, cols]))


def front(plan, me, x, params, weights):
    rows, width = x.shape
    half = width // 2
    return pl.pallas_call(
        functools.partial(front_kernel, plan, len(weights)),
        out_shape=(
            sds((rows, width), BF16),
            sds((rows, width)),
            sds((rows, width)),
            sds((rows, half)),
            sds((half // GROUP, rows, GROUP)),
            sds((width // GROUP, rows, GROUP)),
            sds((4, SUB, half)),
            sds((4, half)),
        ),
        in_specs=[SMEM, VMEM, VMEM] + [ANY] * len(weights),
        out_specs=(VMEM,) * 8,
        scratch_shapes=[pltpu.VMEM((width, mix_width(plan, width)), BF16), pltpu.SemaphoreType.DMA],
        compiler_params=pltpu.CompilerParams(vmem_limit_bytes=12 << 20),
        cost_estimate=COST,
        name="front",
    )(me, x, params, *weights)


def mid_kernel(plan, count, me_ref, x_ref, p_ref, gate_ref, kept_ref, feed_ref, sub_ref, every_ref, *refs):
    w_hbm, refs = refs[:count], refs[count:]
    states_ref, first_ref, gn_ref, rg_ref, gated_ref, after_ref, lifted_ref, out_ref, sem = refs
    rows, width = x_ref.shape
    half = width // 2
    block = rows // SUB
    pairs = pairs_of(plan, w_hbm, me_ref, "out", out_ref)
    load_start(pairs, sem)

    sr = jnp.zeros((1, half), F32)
    si = jnp.zeros((1, half), F32)
    for k in range(every_ref.shape[0]):
        at = k ^ me_ref[3]
        nr, ni = cmul(every_ref[at, 0:1, :], every_ref[at, 1:2, :], sr, si)
        earlier = k < me_ref[0]
        sr = jnp.where(earlier, nr + every_ref[at, 2:3, :], sr)
        si = jnp.where(earlier, ni + every_ref[at, 3:4, :], si)
    for k in range(SUB):
        first_ref[0, k : k + 1, :] = sr
        first_ref[1, k : k + 1, :] = si
        nr, ni = cmul(sub_ref[0, k : k + 1, :], sub_ref[1, k : k + 1, :], sr, si)
        sr = nr + sub_ref[2, k : k + 1, :]
        si = ni + sub_ref[3, k : k + 1, :]
    cos, sin = turns(p_ref, half)
    tiles = half // GROUP
    sr = parts(first_ref, 0, tiles)
    si = parts(first_ref, 1, tiles)
    for j in range(block):
        at = pl.ds(j, SUB, stride=block)
        for t in range(tiles):
            kept = kept_ref[t, at, :]
            tr, ti = cmul(cos[t], sin[t], sr[t], si[t])
            sr[t] = kept * tr + feed_ref[t, at, :]
            si[t] = kept * ti + feed_ref[tiles + t, at, :]
            states_ref[t, at, :] = sr[t]
            states_ref[tiles + t, at, :] = si[t]

    lane = lax.broadcasted_iota(jnp.int32, (ROWS, GROUP), 1)

    def group_norm(r):
        held = jnp.zeros((ROWS, GROUP), F32)
        for g in range(width // GROUP):
            cols = slice(g * GROUP, (g + 1) * GROUP)
            v = gate_ref[r, cols] * states_ref[g, r, :]
            centre = v - jnp.mean(v, axis=1, keepdims=True)
            scale = lax.rsqrt(jnp.mean(centre * centre, axis=1, keepdims=True) + EPS)
            gn = centre * scale
            gn_ref[r, cols] = gn
            gated_ref[r, cols] = (gn * p_ref[1:2, cols]).astype(BF16)
            held = jnp.where(lane == g, scale, held)
        rg_ref[r, :] = held

    over_rows(rows, group_norm)
    load_wait(pairs, sem)
    after_ref[...] = x_ref[...].astype(F32) + dot(gated_ref[...], out_ref[...])

    def norm(r):
        after = after_ref[r, :]
        scale = lax.rsqrt(jnp.mean(after * after, axis=1, keepdims=True) + EPS)
        lifted_ref[r, :] = (after * scale * p_ref[2:3, :]).astype(BF16)

    over_rows(rows, norm)


def mid(plan, me, x, params, gate, kept, feed, sub, every, weights):
    rows, width = x.shape
    half = width // 2
    return pl.pallas_call(
        functools.partial(mid_kernel, plan, len(weights)),
        out_shape=(
            sds((width // GROUP, rows, GROUP)),
            sds((2, SUB, half)),
            sds((rows, width)),
            sds((rows, GROUP)),
            sds((rows, width), BF16),
            sds((rows, width)),
            sds((rows, width), BF16),
        ),
        in_specs=[SMEM] + [VMEM] * 7 + [ANY] * len(weights),
        out_specs=(VMEM,) * 7,
        scratch_shapes=[pltpu.VMEM((width, width), BF16), pltpu.SemaphoreType.DMA],
        compiler_params=pltpu.CompilerParams(vmem_limit_bytes=12 << 20),
        cost_estimate=COST,
        name="mid",
    )(me, x, params, gate, kept, feed, sub, every, *weights)


def ffn_kernel(plan, count, me_ref, after_ref, lifted_ref, *refs):
    w_hbm, refs = refs[:count], refs[count:]
    both_ref, hidden_ref, next_ref, up_ref, down_ref, sems = refs
    inner = hidden_ref.shape[1]
    up_pairs = pairs_of(plan, w_hbm, me_ref, "up", up_ref)
    down_pairs = pairs_of(plan, w_hbm, me_ref, "down", down_ref)
    load_start(up_pairs, sems.at[0])
    load_start(down_pairs, sems.at[1])
    load_wait(up_pairs, sems.at[0])
    lifted = lifted_ref[...]
    step = after_ref.shape[1] // 2
    for k in range(inner // step):
        cols = slice(k * step, (k + 1) * step)
        more = slice(inner + k * step, inner + (k + 1) * step)
        a = dot(lifted, up_ref[:, cols])
        b = dot(lifted, up_ref[:, more])
        both_ref[:, cols] = a
        both_ref[:, more] = b
        hidden_ref[:, cols] = (a * jax.nn.sigmoid(a) * b).astype(BF16)
    load_wait(down_pairs, sems.at[1])
    next_ref[...] = (after_ref[...] + dot(hidden_ref[...], down_ref[...])).astype(next_ref.dtype)


def ffn(plan, me, after, lifted, weights, dtype):
    rows, width = after.shape
    inner = 2 * width
    return pl.pallas_call(
        functools.partial(ffn_kernel, plan, len(weights)),
        out_shape=(sds((rows, 2 * inner)), sds((rows, inner), BF16), sds((rows, width), dtype)),
        in_specs=[SMEM] + [VMEM] * 2 + [ANY] * len(weights),
        out_specs=(VMEM,) * 3,
        scratch_shapes=[
            pltpu.VMEM((width, 2 * inner), BF16),
            pltpu.VMEM((inner, width), BF16),
            pltpu.SemaphoreType.DMA((2,)),
        ],
        compiler_params=pltpu.CompilerParams(vmem_limit_bytes=17 << 20),
        cost_estimate=COST,
        name="ffn",
    )(me, after, lifted, *weights)


def lower(me_ref, dx_ref, dlow_ref):
    rows, width = dx_ref.shape
    if dx_ref.dtype == BF16:
        at = lax.broadcasted_iota(jnp.int32, (rows, GROUP), 0)
        live = at < me_ref[4]
        for t in range(width // GROUP):
            cols = slice(t * GROUP, (t + 1) * GROUP)
            dlow_ref[:, cols] = jnp.where(live, dx_ref[:, cols].astype(F32), 0.0).astype(BF16)
        return dlow_ref
    dlow_ref[...] = dx_ref[...].astype(BF16)
    return dx_ref


def lift_back(grad_ref, p_ref, after_ref, work_ref, dafter_ref, dmid_ref, gain_ref):
    def norm_back(r):
        after = after_ref[r, :]
        scale = lax.rsqrt(jnp.mean(after * after, axis=1, keepdims=True) + EPS)
        normal = after * scale
        lift = work_ref[r, :]
        e = lift * p_ref[2:3, :]
        d = grad_ref[r, :].astype(F32) + scale * (e - normal * jnp.mean(e * normal, axis=1, keepdims=True))
        dafter_ref[r, :] = d
        dmid_ref[r, :] = d.astype(BF16)
        work_ref[r, :] = lift * normal

    over_rows(after_ref.shape[0], norm_back)
    gain_ref[...] = jnp.sum(work_ref[...], axis=0, keepdims=True)


def back_ffn_kernel(plan, count, rels, me_ref, dx_ref, p_ref, both_ref, after_ref, *refs):
    w_hbm, refs = refs[:count], refs[count:]
    if rels is not None:
        lifted_ref, keep_ref, send_ref, *refs, dboth_ref, grad_up_ref, out_sem = refs
        dlow_ref, *refs = refs
    else:
        dlow_ref, dboth_ref, *refs = refs
    dafter_ref, dmid_ref, gain_ref, work_ref, up_ref, down_ref, sems = refs
    rows, width = dx_ref.shape
    inner = down_ref.shape[0]
    up_pairs = pairs_of(plan, w_hbm, me_ref, "up", up_ref)
    down_pairs = pairs_of(plan, w_hbm, me_ref, "down", down_ref)
    load_start(down_pairs, sems.at[1])
    load_start(up_pairs, sems.at[0])
    grad_ref = lower(me_ref, dx_ref, dlow_ref)
    dlow = dlow_ref[...]
    load_wait(down_pairs, sems.at[1])
    step = width // 2
    for k in range(inner // step):
        cols = slice(k * step, (k + 1) * step)
        more = slice(inner + k * step, inner + (k + 1) * step)
        dh = dot_t(dlow, down_ref[cols, :])
        a = both_ref[:, cols]
        sig = jax.nn.sigmoid(a)
        dboth_ref[:, cols] = (dh * both_ref[:, more] * (sig * (1.0 + a * (1.0 - sig)))).astype(BF16)
        dboth_ref[:, more] = (dh * (a * sig)).astype(BF16)
    if rels is not None:
        products(lifted_ref[...], dboth_ref, grad_up_ref, grad_up_ref.shape[1])
        pairs = export(me_ref, rels, "up", grad_up_ref, 0, HALVES["up"], keep_ref, send_ref, out_sem)
    load_wait(up_pairs, sems.at[0])
    work_ref[...] = dot_t(dboth_ref[...], up_ref[...])

    lift_back(grad_ref, p_ref, after_ref, work_ref, dafter_ref, dmid_ref, gain_ref)
    if rels is not None:
        load_wait(pairs, out_sem)


def turn_kernel(plan, count, rels, me_ref, dx_ref, p_ref, after_ref, lifted_ref, *refs):
    w_hbm, refs = refs[:count], refs[count:]
    (
        keep_ref, send_ref, next_ref, hidden_ref, dlow_ref, dafter_ref, dmid_ref, gain_ref,
        dboth_ref, grad_up_ref, work_ref, up_ref, down_ref, sems, out_sem,
    ) = refs
    width = dx_ref.shape[1]
    inner = down_ref.shape[0]
    up_pairs = pairs_of(plan, w_hbm, me_ref, "up", up_ref)
    down_pairs = pairs_of(plan, w_hbm, me_ref, "down", down_ref)
    load_start(up_pairs, sems.at[0])
    load_start(down_pairs, sems.at[1])
    grad_ref = lower(me_ref, dx_ref, dlow_ref)
    dlow = dlow_ref[...]
    lifted = lifted_ref[...]
    load_wait(up_pairs, sems.at[0])
    load_wait(down_pairs, sems.at[1])
    step = width // 2
    for k in range(inner // step):
        cols = slice(k * step, (k + 1) * step)
        more = slice(inner + k * step, inner + (k + 1) * step)
        a = dot(lifted, up_ref[:, cols])
        b = dot(lifted, up_ref[:, more])
        dh = dot_t(dlow, down_ref[cols, :])
        sig = jax.nn.sigmoid(a)
        gated = a * sig
        hidden_ref[:, cols] = (gated * b).astype(BF16)
        dboth_ref[:, cols] = (dh * b * (sig * (1.0 + a * (1.0 - sig)))).astype(BF16)
        dboth_ref[:, more] = (dh * gated).astype(BF16)
    products(lifted, dboth_ref, grad_up_ref, grad_up_ref.shape[1])
    pairs = export(me_ref, rels, "up", grad_up_ref, 0, HALVES["up"], keep_ref, send_ref, out_sem)
    work_ref[...] = dot_t(dboth_ref[...], up_ref[...])
    lift_back(grad_ref, p_ref, after_ref, work_ref, dafter_ref, dmid_ref, gain_ref)
    next_ref[...] = (after_ref[...] + dot(hidden_ref[...], down_ref[...])).astype(next_ref.dtype)
    load_wait(pairs, out_sem)


def turn(plan, rels, me, dx, params, after, lifted, weights):
    rows, width = dx.shape
    inner = 2 * width
    block = sds((2 ** len(STAGES), UNIT, HALVES["up"]), BF16)
    low = sds((rows, width), BF16)
    return pl.pallas_call(
        functools.partial(turn_kernel, plan, len(weights), rels),
        out_shape=(block, block, low, sds((rows, inner), BF16), low, sds((rows, width)), low, sds((1, width))),
        in_specs=[SMEM] + [VMEM] * 4 + [ANY] * len(weights),
        out_specs=(ANY, ANY) + (VMEM,) * 6,
        scratch_shapes=[
            pltpu.VMEM((rows, 2 * inner), BF16),
            pltpu.VMEM((width, 2 * inner), BF16),
            pltpu.VMEM((rows, width), F32),
            pltpu.VMEM((width, 2 * inner), BF16),
            pltpu.VMEM((inner, width), BF16),
            pltpu.SemaphoreType.DMA((2,)),
            pltpu.SemaphoreType.DMA,
        ],
        compiler_params=pltpu.CompilerParams(vmem_limit_bytes=22 << 20),
        cost_estimate=COST,
        name="turn",
    )(me, dx, params, after, lifted, *weights)


def back_ffn(plan, me, dx, params, both, after, weights, rels=None, lifted=()):
    rows, width = dx.shape
    inner = 2 * width
    block = sds((2 ** len(STAGES), UNIT, HALVES["up"]), BF16)
    dboth = (rows, 2 * inner)
    outs = (sds((rows, width), BF16), sds(dboth, BF16), sds((rows, width)), sds((rows, width), BF16), sds((1, width)))
    specs, more = (VMEM,) * 5, []
    if rels is not None:
        outs, specs = (block, block, outs[0], *outs[2:]), (ANY, ANY, *specs[1:])
        more = [pltpu.VMEM(dboth, BF16), pltpu.VMEM((width, 2 * inner), BF16), pltpu.SemaphoreType.DMA]
    return pl.pallas_call(
        functools.partial(back_ffn_kernel, plan, len(weights), rels),
        out_shape=outs,
        in_specs=[SMEM] + [VMEM] * 4 + [ANY] * len(weights) + [VMEM] * len(lifted),
        out_specs=specs,
        scratch_shapes=[
            pltpu.VMEM((rows, width), F32),
            pltpu.VMEM((width, 2 * inner), BF16),
            pltpu.VMEM((inner, width), BF16),
            pltpu.SemaphoreType.DMA((2,)),
        ]
        + more,
        compiler_params=pltpu.CompilerParams(vmem_limit_bytes=25 << 20),
        cost_estimate=COST,
        name="back_ffn",
    )(me, dx, params, both, after, *weights, *lifted)


def back_mid_kernel(
    plan, count, me_ref, dmid_ref, p_ref, gn_ref, rg_ref, gate_ref, states_ref, kept_ref, sub_ref, *refs
):
    w_hbm, refs = refs[:count], refs[count:]
    dgpre_ref, dstates_ref, gain_ref, rsub_ref, rtotal_ref, work_ref, out_ref, sem = refs
    rows, width = dmid_ref.shape
    half = width // 2
    block = rows // SUB
    pairs = pairs_of(plan, w_hbm, me_ref, "out", out_ref)
    load_start(pairs, sem)
    load_wait(pairs, sem)
    work_ref[...] = dot_t(dmid_ref[...], out_ref[...])

    def group_back(r):
        held = rg_ref[r, :]
        for g in range(width // GROUP):
            cols = slice(g * GROUP, (g + 1) * GROUP)
            gn = gn_ref[r, cols]
            dg = work_ref[r, cols]
            e = dg * p_ref[1:2, cols]
            dv = held[:, g : g + 1] * (
                e - jnp.mean(e, axis=1, keepdims=True) - gn * jnp.mean(e * gn, axis=1, keepdims=True)
            )
            gate = gate_ref[r, cols]
            dgpre_ref[r, cols] = (dv * states_ref[g, r, :] * gate * (1.0 - gate)).astype(BF16)
            dstates_ref[g, r, :] = dv * gate
            work_ref[r, cols] = dg * gn

    over_rows(rows, group_back)
    gain_ref[...] = jnp.sum(work_ref[...], axis=0, keepdims=True)

    cos, sin = turns(p_ref, half)
    tiles = half // GROUP
    zr = [jnp.zeros((SUB, GROUP), F32)] * tiles
    zi = [jnp.zeros((SUB, GROUP), F32)] * tiles
    for j in reversed(range(block)):
        at = pl.ds(j, SUB, stride=block)
        for t in range(tiles):
            kept = kept_ref[t, at, :]
            qr = dstates_ref[t, at, :] + zr[t]
            qi = dstates_ref[tiles + t, at, :] + zi[t]
            zr[t] = kept * (cos[t] * qr + sin[t] * qi)
            zi[t] = kept * (cos[t] * qi - sin[t] * qr)
    zr, zi = jnp.concatenate(zr, axis=1), jnp.concatenate(zi, axis=1)
    rsub_ref[0] = zr
    rsub_ref[1] = zi
    tr = jnp.zeros((1, half), F32)
    ti = jnp.zeros((1, half), F32)
    for k in reversed(range(SUB)):
        ar, ai = sub_ref[0, k : k + 1, :], sub_ref[1, k : k + 1, :]
        tr, ti = ar * tr + ai * ti + zr[k : k + 1], ar * ti - ai * tr + zi[k : k + 1]
    rtotal_ref[0:1, :] = tr
    rtotal_ref[1:2, :] = ti


def back_mid(plan, me, dmid, params, gn, rg, gate, states, kept, sub, weights):
    rows, width = dmid.shape
    half = width // 2
    return pl.pallas_call(
        functools.partial(back_mid_kernel, plan, len(weights)),
        out_shape=(
            sds((rows, width), BF16),
            sds((width // GROUP, rows, GROUP)),
            sds((1, width)),
            sds((2, SUB, half)),
            sds((2, half)),
        ),
        in_specs=[SMEM] + [VMEM] * 8 + [ANY] * len(weights),
        out_specs=(VMEM,) * 5,
        scratch_shapes=[
            pltpu.VMEM((rows, width), F32),
            pltpu.VMEM((width, width), BF16),
            pltpu.SemaphoreType.DMA,
        ],
        compiler_params=pltpu.CompilerParams(vmem_limit_bytes=11 << 20),
        cost_estimate=COST,
        name="back_mid",
    )(me, dmid, params, gn, rg, gate, states, kept, sub, *weights)


def back_two_kernel(
    plan, count, rels, spare, me_ref, x_ref, p_ref, dafter_ref, dgpre_ref, dstates_ref, states_ref, kept_ref, rate_ref, cpre_ref,
    first_ref, sub_ref, rsub_ref, every_ref, revery_ref, *refs
):
    w_hbm, extra, refs = refs[:count], refs[count : count + spare], refs[count + spare :]
    if rels is not None:
        normed_ref, *extra = extra
        keep_ref, send_ref, dx_ref, gains_ref, *refs, mix_ref, held_ref, out_sem = refs
        dmixin_ref, *refs = refs
    else:
        dmixin_ref, dx_ref, gains_ref, *refs = refs
    work_ref, q_ref, turn_ref, start_ref, w_ref, sem = refs
    rows, width = x_ref.shape
    half = width // 2
    block = rows // SUB
    pairs = pairs_of(plan, w_hbm, me_ref, "mix", w_ref)
    load_start(pairs, sem)
    zr = jnp.zeros((1, half), F32)
    zi = jnp.zeros((1, half), F32)
    for k in reversed(range(every_ref.shape[0])):
        at = k ^ me_ref[3]
        ar, ai = every_ref[at, 0:1, :], every_ref[at, 1:2, :]
        later = k > me_ref[0]
        nr = ar * zr + ai * zi + revery_ref[at, 0:1, :]
        ni = ar * zi - ai * zr + revery_ref[at, 1:2, :]
        zr = jnp.where(later, nr, zr)
        zi = jnp.where(later, ni, zi)
    for k in reversed(range(SUB)):
        start_ref[0, k : k + 1, :] = zr
        start_ref[1, k : k + 1, :] = zi
        ar, ai = sub_ref[0, k : k + 1, :], sub_ref[1, k : k + 1, :]
        zr, zi = (
            ar * zr + ai * zi + rsub_ref[0, k : k + 1, :],
            ar * zi - ai * zr + rsub_ref[1, k : k + 1, :],
        )
    cos, sin = turns(p_ref, half)
    tiles = half // GROUP
    zr = parts(start_ref, 0, tiles)
    zi = parts(start_ref, 1, tiles)
    angle = [jnp.zeros((SUB, GROUP), F32)] * tiles
    for j in reversed(range(block)):
        at = pl.ds(j, SUB, stride=block)
        before = pl.ds(max(j - 1, 0), SUB, stride=block)
        for t in range(tiles):
            kept = kept_ref[t, at, :]
            qr = dstates_ref[t, at, :] + zr[t]
            qi = dstates_ref[tiles + t, at, :] + zi[t]
            q_ref[t, at, :] = qr
            q_ref[tiles + t, at, :] = qi
            zr[t] = kept * (cos[t] * qr + sin[t] * qi)
            zi[t] = kept * (cos[t] * qi - sin[t] * qr)
            if j:
                sr, si = states_ref[t, before, :], states_ref[tiles + t, before, :]
            else:
                sr, si = (first_ref[k, :, t * GROUP : (t + 1) * GROUP] for k in range(2))
            turn_ref[t, at, :] = zr[t] * sr + zi[t] * si
            angle[t] = angle[t] + (zi[t] * sr - zr[t] * si)
    gains_ref[1:2, half:] = jnp.sum(jnp.concatenate(angle, axis=1), axis=0, keepdims=True)

    def activations(r):
        for t in range(tiles):
            rate = rate_ref[r, t * GROUP : (t + 1) * GROUP]
            left = 1.0 - rate
            meet = jnp.zeros_like(rate)
            for k in range(2):
                cols = slice((k * tiles + t) * GROUP, (k * tiles + t + 1) * GROUP)
                pre = cpre_ref[r, cols]
                sig = jax.nn.sigmoid(pre)
                q = q_ref[k * tiles + t, r, :]
                meet = meet + q * (pre * sig)
                dmixin_ref[r, cols] = (left * q * (sig * (1.0 + pre * (1.0 - sig)))).astype(BF16)
            dfpre = left * (turn_ref[t, r, :] - rate * meet)
            dmixin_ref[r, 2 * width + t * GROUP : 2 * width + (t + 1) * GROUP] = dfpre.astype(BF16)
            turn_ref[t, r, :] = dfpre
        dmixin_ref[r, width : 2 * width] = dgpre_ref[r, :]

    over_rows(rows, activations)
    for t in range(tiles):
        gains_ref[1:2, t * GROUP : (t + 1) * GROUP] = jnp.sum(turn_ref[t], axis=0, keepdims=True)
    load_wait(pairs, sem)
    work_ref[...] = dot_t(dmixin_ref[...], w_ref[:, : dmixin_ref.shape[1]])

    def norm_back(r):
        x = x_ref[r, :].astype(F32)
        scale = lax.rsqrt(jnp.mean(x * x, axis=1, keepdims=True) + EPS)
        normal = x * scale
        dn = work_ref[r, :]
        e = dn * p_ref[0:1, :]
        dx_ref[r, :] = dafter_ref[r, :] + scale * (e - normal * jnp.mean(e * normal, axis=1, keepdims=True))
        work_ref[r, :] = dn * normal

    over_rows(rows, norm_back)
    gains_ref[0:1, :] = jnp.sum(work_ref[...], axis=0, keepdims=True)

    if rels is None:
        return
    held_ref[...] = jnp.zeros_like(held_ref)
    for k in range(spare // 3):
        two, mid_gain, ffn_gain = (gains_ref, *extra)[3 * k : 3 * k + 3]
        held_ref[4 * k : 4 * k + 1, :] = two[0:1, :]
        held_ref[4 * k + 1 : 4 * k + 2, :] = mid_gain[...]
        held_ref[4 * k + 2 : 4 * k + 3, :] = ffn_gain[...]
        held_ref[4 * k + 3 : 4 * k + 4, :] = two[1:2, :]
    normed = normed_ref[...]
    products(normed, dmixin_ref, mix_ref, width)
    products(normed, dmixin_ref, mix_ref, half, 2 * width, width)
    mix_ref[:, width + half :] = jnp.transpose(held_ref[...]).astype(BF16)
    pairs = export(me_ref, rels, "cell", mix_ref, 0, HALVES["cell"], keep_ref, send_ref, out_sem)
    load_wait(pairs, out_sem)


def back_two(plan, me, x, params, dafter, dgpre, dstates, states, kept, rate, cpre, first, sub, rsub, every, revery, weights, rels=None, extra=()):
    rows, width = x.shape
    half = width // 2
    size = 2 * width + half
    block = sds((2 ** len(STAGES), UNIT, HALVES["cell"]), BF16)
    scratch = [
        pltpu.VMEM((rows, width), F32),
        pltpu.VMEM((width // GROUP, rows, GROUP), F32),
        pltpu.VMEM((half // GROUP, rows, GROUP), F32),
        pltpu.VMEM((2, SUB, half), F32),
        pltpu.VMEM((width, mix_width(plan, width)), BF16),
        pltpu.SemaphoreType.DMA,
    ]
    if rels is None:
        first_out, specs, more = (sds((rows, size), BF16),), (VMEM,), []
    else:
        first_out, specs = (block, block), (ANY, ANY)
        scratch.insert(0, pltpu.VMEM((rows, size), BF16))
        more = [pltpu.VMEM((width, 2 * HALVES["cell"]), BF16), pltpu.VMEM((GROUP, width), F32), pltpu.SemaphoreType.DMA]
    return pl.pallas_call(
        functools.partial(back_two_kernel, plan, len(weights), rels, len(extra)),
        out_shape=first_out + (sds((rows, width)), sds((2, width))),
        in_specs=[SMEM] + [VMEM] * 14 + [ANY] * len(weights) + [VMEM] * len(extra),
        out_specs=specs + (VMEM, VMEM),
        scratch_shapes=scratch + more,
        compiler_params=pltpu.CompilerParams(vmem_limit_bytes=18 << 20),
        cost_estimate=COST,
        name="back_two",
    )(me, x, params, dafter, dgpre, dstates, states, kept, rate, cpre, first, sub, rsub, every, revery, *weights, *extra)


def row_product(left, right):
    return lax.dot_general(left, right, (((0,), (0,)), ((), ())), preferred_element_type=F32)


def export(info_ref, rels, name, grad, column, columns, keep_ref, send_ref, sem):
    chip, core = info_ref[1], info_ref[2]
    pairs = []
    for half, target in ((1 - core, send_ref), (core, keep_ref)):
        for b, (zero, one) in enumerate(zip(*rels)):
            block = chip ^ (zero + half * (one - zero))
            if name == "down":
                row, left = block * (2 * UNIT) + half * UNIT, 0
            else:
                row, left = block * UNIT, half * HALVES[name]
            pairs.append(
                (
                    grad.at[pl.ds(pl.multiple_of(row, UNIT), UNIT), pl.ds(pl.multiple_of(left, GROUP), columns)],
                    target.at[b, :, pl.ds(column, columns)],
                )
            )
    load_start(pairs, sem)
    return pairs


def products(left, right_ref, grad_ref, size, source=0, target=0):
    step = HALVES["out"]
    for k in range(0, size, step):
        right = right_ref[:, source + k : source + k + step]
        grad_ref[:, target + k : target + k + step] = row_product(left, right).astype(BF16)


def grad_od_kernel(
    rels, info_ref, gated_ref, dmid_ref, hidden_ref, dlow_ref, normed_ref, dgpre_ref, keep_ref, send_ref,
    out_ref, gate_ref, down_ref, sem,
):
    width = dlow_ref.shape[1]
    products(hidden_ref[...], dlow_ref, down_ref, width)
    at = HALVES["out"] + HALVES["gate"]
    pairs = export(info_ref, rels, "down", down_ref, at, width, keep_ref, send_ref, sem)
    products(gated_ref[...], dmid_ref, out_ref, width)
    pairs += export(info_ref, rels, "out", out_ref, 0, HALVES["out"], keep_ref, send_ref, sem)
    products(normed_ref[...], dgpre_ref, gate_ref, width)
    pairs += export(info_ref, rels, "gate", gate_ref, HALVES["out"], HALVES["gate"], keep_ref, send_ref, sem)
    load_wait(pairs, sem)


def grad_od(rels, info, gated, dmid, hidden, dlow, normed, dgpre):
    width = dlow.shape[1]
    shape = sds((len(rels[0]), UNIT, HALVES["out"] + HALVES["gate"] + width), BF16)
    return pl.pallas_call(
        functools.partial(grad_od_kernel, rels),
        out_shape=(shape, shape),
        in_specs=[SMEM] + [VMEM] * 6,
        out_specs=(ANY, ANY),
        scratch_shapes=[
            pltpu.VMEM((width, width), BF16),
            pltpu.VMEM((width, width), BF16),
            pltpu.VMEM((hidden.shape[1], width), BF16),
            pltpu.SemaphoreType.DMA,
        ],
        compiler_params=pltpu.CompilerParams(vmem_limit_bytes=11 << 20),
        cost_estimate=COST,
        name="grad_od",
    )(info, gated, dmid, hidden, dlow, normed, dgpre)


def table_kernel(plan, count, me_ref, *refs):
    sources, (table_ref, held_ref, sem) = refs[:count], refs[count:]
    pairs = pairs_of(plan, sources, me_ref, "small", held_ref)
    load_start(pairs, sem)
    load_wait(pairs, sem)
    depth = table_ref.shape[0]
    half = table_ref.shape[2] // 2
    table = jnp.transpose(held_ref[:, GROUP:].astype(F32))
    table_ref[...] = jnp.zeros_like(table_ref)
    for l in range(depth):
        chan = table[3 * depth + l : 3 * depth + l + 1]
        table_ref[l, 0:3, :] = table[3 * l : 3 * l + 3]
        table_ref[l, 3:4, :half] = chan[:, :half]
        table_ref[l, 3:4, half:] = jnp.cos(chan[:, half:])
        table_ref[l, 4:5, :half] = jnp.sin(chan[:, half:])


def table_of(plan, me, weights, depth, width):
    return pl.pallas_call(
        functools.partial(table_kernel, plan, len(weights)),
        out_shape=sds((depth, 8, width)),
        in_specs=[SMEM] + [ANY] * len(weights),
        out_specs=VMEM,
        scratch_shapes=[pltpu.VMEM((width, 2 * GROUP), BF16), pltpu.SemaphoreType.DMA],
        compiler_params=pltpu.CompilerParams(vmem_limit_bytes=6 << 20),
        cost_estimate=COST,
        name="table",
    )(me, *weights)


def swap(x, bits):
    count = lax.axis_size("dp") * lax.axis_size("seq")
    return lax.ppermute(x, ALL, [(i, i ^ bits[i % 2]) for i in range(count)])


class Order:
    def __init__(self):
        self.last = None

    def step(self, *values):
        if self.last is not None:
            values = lax.optimization_barrier(values + (self.last,))[: len(values)]
        self.last = values[0]
        return values

    def join(self, *moves, cores=()):
        values = [move.got for move in moves]
        for move in cores:
            values += [move.last_core, move.held_core]
        values = list(self.step(*values))
        for move in moves:
            move.got = values.pop(0)
        for move in cores:
            move.last_core, move.held_core = values.pop(0), values.pop(0)


    def pass_on(self, *moves):
        for move in moves:
            move.ready()
        for move, value in zip(moves, self.step(*(move.out for move in moves))):
            move.out = value
            move.send()


def rels_of(stages):
    rels = ([0], [0])
    for bits in stages:
        for core in range(2):
            rels[core].extend([rel ^ bits[core] for rel in rels[core]])
    return rels


class Spread:
    def __init__(self, unit, stages):
        self.held, self.stages, self.at = unit[None], stages, 0
        self.got = None

    def join(self):
        if self.got is not None:
            self.held = jnp.concatenate([self.held, self.got])

    def ready(self):
        self.join()
        self.out = self.held

    def send(self):
        self.held = self.out
        one, two = self.stages[self.at]
        self.at += 1
        self.got = swap(self.held, (2 * one, 2 * two))

    def end(self):
        self.near, self.last = self.held, self.got
        self.last_core = swap(self.last, (1, 1))

    def near_core(self):
        self.held_core = swap(self.held, (1, 1))

    def arrays(self):
        return (self.near, self.held_core, self.last, self.last_core)

    def sources(self):
        rels = rels_of(self.stages)
        half = len(rels[0]) // 2
        low = tuple(tuple(rel[:half]) for rel in rels)
        high = tuple(tuple(rel[half:]) for rel in rels)
        return ((0, low), (1, low), (0, high), (1, high))


class Reduce:
    def __init__(self, keep, send, stages):
        self.held, self.stages = keep, list(stages)
        self.got = swap(send, (1, 1))

    def add(self):
        half = self.held.shape[0] // 2
        if not half:
            return self.held[0].astype(F32) + self.got[0].astype(F32)

        def joined(part):
            return (self.held[part].astype(F32) + self.got[part].astype(F32)).astype(BF16)

        self.held, self.out = joined(slice(0, half)), joined(slice(half, None))
        self.got = None

    def ready(self):
        if self.got is not None:
            self.add()

    def send(self):
        one, two = self.stages.pop()
        self.got = swap(self.out, (2 * one, 2 * two))


def exchange(x, order=None):
    other = swap(x, (1, 1))
    if order is not None:
        (other,) = order.step(other)
    pair = jnp.stack([x, other])
    got = [swap(pair, (k, k)) for k in range(2, lax.axis_size("seq"), 2)]
    return jnp.concatenate([pair] + got)


def finish_kernel(info_ref, *refs):
    depth = (len(refs) - 5) // 3
    mine, other, downs = refs[:depth], refs[depth : 2 * depth], refs[2 * depth : 3 * depth]
    mix_ref, out_ref, up_ref, down_ref, tail_ref = refs[3 * depth :]
    width = down_ref.shape[2]
    size = HALVES["cell"]

    def place(first, second):
        for l in range(depth):
            rest = width - size
            mix_ref[l, :, :size] = first[l][:, :size]
            mix_ref[l, :, size:width] = second[l][:, :rest]
            mix_ref[l, :, 2 * width :] = second[l][:, rest : size - GROUP]
            at = size
            for name, ref, begin in (("out", out_ref, 0), ("gate", mix_ref, width), ("up", up_ref, 0)):
                step = HALVES[name]
                ref[l, :, begin : begin + step] = first[l][:, at : at + step]
                ref[l, :, begin + step : begin + 2 * step] = second[l][:, at : at + step]
                at += step
        tail_ref[...] = second[0][:, size - GROUP : size]

    @pl.when(info_ref[2] == 0)
    def _():
        place(mine, other)

    @pl.when(info_ref[2] == 1)
    def _():
        place(other, mine)

    for l in range(depth):
        down_ref[l] = downs[l][:, downs[l].shape[1] - width :]


def finish(info, mine, other, downs, shapes):
    share = mine[0].shape[0]
    return pl.pallas_call(
        finish_kernel,
        out_shape=tuple(sds(shape) for shape in shapes) + (sds((share, GROUP)),),
        in_specs=[SMEM] + [VMEM] * (3 * len(mine)),
        out_specs=(VMEM,) * 5,
        compiler_params=pltpu.CompilerParams(vmem_limit_bytes=8 << 20),
        cost_estimate=COST,
        name="finish",
    )(info, *mine, *other, *downs)


def layer_params(gains, chan):
    half = chan.shape[0] // 2
    angle = chan[half:]
    rows = [
        gains[0],
        gains[1],
        gains[2],
        jnp.concatenate([chan[:half], jnp.cos(angle)]),
        jnp.concatenate([jnp.sin(angle), jnp.zeros((half,), F32)]),
    ]
    return jnp.concatenate([jnp.stack(rows), jnp.zeros((3, 2 * half), F32)], axis=0)


STAGES = ((4, 8), (8, 4), (1, 2), (2, 1))
LATER = ((1, 2), (4, 8), (8, 4), (2, 1))
UPPER = (STAGES, LATER, STAGES)
LOWER = (LATER, STAGES, STAGES)


def small_of(gains, chan_params):
    depth, _, share = gains.shape
    return jnp.concatenate(
        [gains.reshape(depth * 3, share).T, chan_params.T, jnp.zeros((share, GROUP - 4 * depth), BF16)], axis=1
    )


def info_of(lengths, rows, turned):
    where = lax.axis_index("seq")
    base = where * rows
    ends = [lengths[0, 0]]
    for j in range(1, lengths.shape[1]):
        ends.append(ends[-1] + lengths[0, j])
    chip = (lax.axis_index("dp") * lax.axis_size("seq") + where) // 2
    values = [where, chip, where % 2, where if turned else jnp.zeros_like(where), ends[-1] - base]
    values += [end - lengths[0, j] - base for j, end in enumerate(ends)]
    return jnp.stack([value.astype(jnp.int32) for value in values])


def plain_body(stream, w_mix, w_out, w_up, w_down, gains, chan_params, lengths, cotangent):
    rows, width = stream.shape
    depth = w_mix.shape[0]
    info = info_of(lengths, rows, False)
    small = small_of(gains, chan_params)
    table = lax.all_gather(small, ALL, axis=0, tiled=True)[:, : 4 * depth].T.astype(F32)
    params = [layer_params(table[3 * l : 3 * l + 3], table[3 * depth + l]) for l in range(depth)]
    weights = [
        tuple(lax.all_gather(w[l], ALL, axis=0, tiled=True) for w in (w_mix, w_out, w_up, w_down))
        for l in range(depth)
    ]
    x = stream
    saved = []
    for l in range(depth):
        head = front(None, info, x, params[l], weights[l])
        every = lax.all_gather(head[-1], "seq")
        middle = mid(None, info, x, params[l], head[2], head[4], head[5], head[6], every, weights[l])
        tail = ffn(None, info, middle[5], middle[6], weights[l], F32)
        saved.append((x, every, head, middle, tail))
        x = tail[-1]
    mixed = x.astype(BF16)
    dx = cotangent
    sums = [None] * depth
    for l in reversed(range(depth)):
        x, every, (normed, cpre, gate, rate, kept, feed, sub, _), middle, (both, hidden, _) = saved[l]
        states, first, gn, rg, gated, after, lifted = middle
        dlow, dboth, dafter, dmid, ffn_gain = back_ffn(None, info, dx, params[l], both, after, weights[l])
        dgpre, dstates, mid_gain, rsub, rtotal = back_mid(
            None, info, dmid, params[l], gn, rg, gate, states, kept, sub, weights[l]
        )
        revery = lax.all_gather(rtotal, "seq")
        dmixin, dx, gains_b = back_two(
            None, info, x, params[l], dafter, dgpre, dstates, states, kept, rate, cpre, first, sub, rsub, every, revery,
            weights[l],
        )
        grads = [row_product(normed, dmixin), row_product(gated, dmid), row_product(lifted, dboth), row_product(hidden, dlow)]
        grads.append(jnp.stack([gains_b[0], mid_gain[0], ffn_gain[0], gains_b[1]], axis=1))
        sums[l] = [lax.psum_scatter(g.astype(BF16), ALL, scatter_dimension=0, tiled=True).astype(F32) for g in grads]
    outs = [jnp.stack([sums[l][k] for l in range(depth)]) for k in range(5)]
    tail = outs.pop()
    return (mixed, dx, *outs, jnp.swapaxes(tail[:, :, :3], 1, 2), tail[:, :, 3])


def fast_body(stream, w_mix, w_out, w_up, w_down, gains, chan_params, lengths, cotangent):
    rows, width = stream.shape
    depth, share, mix_cols = w_mix.shape
    info = info_of(lengths, rows, True)
    small = small_of(gains, chan_params)
    core = lax.axis_index("seq") % 2
    padding = jnp.zeros((share, 2 * HALVES["mix"] - mix_cols - GROUP), BF16)
    halves = ([], [])
    for l in range(depth):
        mix = jnp.concatenate([w_mix[l], padding, small if l == 0 else jnp.zeros_like(small)], axis=1)
        for h in range(2):
            for w, size in ((mix, HALVES["mix"]), (w_out[l], HALVES["out"]), (w_up[l], HALVES["up"])):
                halves[h].append(w[:, h * size : (h + 1) * size])
    halves = [jnp.concatenate(half, axis=1) for half in halves]
    mine = jnp.where(core == 0, halves[0], halves[1])
    other = swap(jnp.where(core == 0, halves[1], halves[0]), (1, 1))
    units = jnp.where(core == 0, jnp.concatenate([mine, other]), jnp.concatenate([other, mine]))
    joint = HALVES["mix"] + HALVES["out"]
    size = joint + HALVES["up"]
    mos, uds = [], []
    for l in range(depth):
        unit = units[:, l * size : (l + 1) * size]
        stages = LATER if l else STAGES
        mos.append(Spread(unit[:, :joint], stages))
        uds.append(Spread(jnp.concatenate([unit[:, joint:], w_down[l]], axis=1), stages))
    plan = {
        "mix": (0, HALVES["mix"]),
        "out": (HALVES["mix"], HALVES["out"]),
        "small": (HALVES["mix"] - GROUP, GROUP),
        "up": (0, HALVES["up"]),
        "down": (HALVES["up"], width),
    }
    plans = [dict(plan, sources=mo.sources()) for mo in mos]

    order = Order()
    mo, ud = mos[0], uds[0]
    later = [move for l in range(1, depth) for move in (mos[l], uds[l])]
    order.pass_on(ud, mo, *later)
    order.join(ud, mo, *later)
    order.pass_on(mo, ud, *later)
    order.join(mo, ud)
    order.pass_on(mo, ud)
    order.join(mo, *later[:1])
    order.pass_on(mo, *later[:1])
    mo.near_core()
    order.join(ud, *later[1:2])
    if later:
        order.pass_on(*later[1:2])
    order.join(mo, *later[:1])
    mo.end()
    order.pass_on(ud)
    ud.near_core()
    x = stream
    saved = []
    params = None
    for l in range(depth):
        mo, ud, plan = mos[l], uds[l], plans[l]
        more = l + 1 < depth
        order.join(cores=(mo,))
        if l == 0:
            params = table_of(plan, info, mo.arrays(), depth, width)
        (layer,) = order.step(params[l])
        head = front(plan, info, x, layer, mo.arrays())
        (total,) = order.step(head[-1])
        if more:
            order.join(ud, uds[l + 1])
        else:
            order.join(ud)
        ud.end()
        every = exchange(order.step(total)[0])
        (every,) = order.step(every)
        if more:
            order.pass_on(mos[l + 1])
            mos[l + 1].near_core()
        middle = mid(plan, info, x, layer, head[2], head[4], head[5], head[6], order.step(every)[0], mo.arrays())
        middle = (*middle[:-1], *order.step(middle[-1]))
        if more:
            order.join(mos[l + 1], cores=(ud,))
            mos[l + 1].end()
            order.pass_on(uds[l + 1])
            uds[l + 1].near_core()
        else:
            order.join(cores=(ud,))
        if more:
            tail = ffn(plan, info, middle[5], middle[6], ud.arrays(), F32)
            saved.append((x, every, head, middle, tail, layer))
            (x,) = order.step(tail[-1])
    later_stages = UPPER if depth > 1 else (STAGES,) * 3
    keep, send, mixed, hidden, dlow, dafter, dmid, ffn_gain = turn(
        plan, rels_of(later_stages[0]), info, cotangent, layer, middle[5], middle[6], ud.arrays()
    )
    saved.append((x, every, head, middle, (None, hidden, None), layer))
    above = None
    sums = [None] * depth
    extra = ()
    for l in reversed(range(depth)):
        x, every, (normed, cpre, gate, rate, kept, feed, sub, _), middle, (both, hidden, _), layer = saved[l]
        states, first, gn, rg, gated, after, lifted = middle
        plan = plans[l]
        u_stages, od_stages, c_stages = UPPER if l else LOWER
        if above:
            (dx,) = order.step(dx)
            keep, send, dlow, dafter, dmid, ffn_gain = back_ffn(
                plan, info, dx, layer, both, after, uds[l].arrays(), rels_of(u_stages), (lifted,)
            )
        (keep,) = order.step(keep)
        u = Reduce(keep, send, u_stages)
        if above:
            u_up, od_up, c_up = above
            order.join(od_up, c_up, u_up)
            od_up.ready()
            order.pass_on(c_up, u_up)
        (dmid,) = order.step(dmid)
        dgpre, dstates, mid_gain, rsub, rtotal = back_mid(
            plan, info, dmid, layer, gn, rg, gate, states, kept, sub, mos[l].arrays()
        )
        (rtotal,) = order.step(rtotal)
        order.join(u, *((c_up, u_up) if above else ()))
        revery = exchange(rtotal, order)
        waiting = [u] + ([od_up, c_up, u_up] if above else [])
        for move in waiting:
            move.ready()
        (dlow,) = order.step(dlow)
        od = Reduce(
            *grad_od(rels_of(od_stages), info, gated, dmid, hidden, dlow, normed, dgpre), od_stages
        )
        (od.held,) = order.step(od.held)
        (revery,) = order.step(revery)
        order.pass_on(*waiting)
        (dstates,) = order.step(dstates)
        more = (normed,)
        if l == 0:
            more = (normed, mid_gain, ffn_gain, *extra)
        keep, send, dx, gains_b = back_two(
            plan, info, x, layer, dafter, dgpre, dstates, states, kept, rate, cpre, first, sub, rsub, every, revery,
            mos[l].arrays(), rels_of(c_stages), more,
        )
        extra = (gains_b, mid_gain, ffn_gain) + extra
        (keep,) = order.step(keep)
        c = Reduce(keep, send, c_stages)
        order.join(*waiting, od)
        order.pass_on(od, u, *((od_up, c_up) if above else ()))
        above = sums[l] = (u, od, c)
    u, od, c = sums[0]
    others = ()
    if depth > 1:
        u_up, od_up, c_up = sums[1]
        others = (od_up, c_up)
    for moves in ((c,), (od, *others), (u,), (c,), (od,), (u,), (c,), (od,), (c,)):
        order.join(*moves)
        order.pass_on(*moves)
    mine, other, downs = [], [], []
    for u, od, c in reversed(sums):
        ready = od.add()
        line = jnp.concatenate([c.add(), ready[:, : HALVES["out"] + HALVES["gate"]], u.add()], axis=1)
        first, second = line[:share], line[share:]
        mine.insert(0, jnp.where(core == 0, first, second))
        other.insert(0, swap(jnp.where(core == 0, second, first), (1, 1)))
        downs.insert(0, ready)
    shapes = (w_mix.shape, w_out.shape, w_up.shape, w_down.shape)
    *grads, tail = finish(info, mine, other, downs, shapes)
    tail = tail[:, : 4 * depth].T.reshape(depth, 4, share)
    return (mixed, dx, *grads, tail[:, :3], tail[:, 3])


def body(stream, w_mix, *others):
    n_dp, n_seq = lax.axis_size("dp"), lax.axis_size("seq")
    fast = n_seq == 8 and n_dp == 4 and 2 * w_mix.shape[1] == UNIT and w_mix.shape[0] == 2
    return (fast_body if fast else plain_body)(stream, w_mix, *others)


def solution(mesh):
    placed = (
        P(ALL, None),
        P(None, ALL, None),
        P(None, ALL, None),
        P(None, ALL, None),
        P(None, ALL, None),
        P(None, None, ALL),
        P(None, ALL),
        P("dp", None),
        P(ALL, None),
    )
    return jax.shard_map(
        body,
        mesh=mesh,
        in_specs=placed,
        out_specs=(
            P(ALL, None),
            P(ALL, None),
            P(None, ALL, None),
            P(None, ALL, None),
            P(None, ALL, None),
            P(None, ALL, None),
            P(None, None, ALL),
            P(None, ALL),
        ),
        check_vma=False,
    )
```

```python
import functools

import jax
import jax.numpy as jnp
from jax import lax
from jax.experimental import pallas as pl
from jax.experimental.pallas import tpu as pltpu
from jax.sharding import PartitionSpec as P

GROUP = 128
EPS = 1e-06
SUB = 8
UNIT = 48
HALVES = {"mix": 1024, "out": 384, "up": 1536, "gate": 384, "cell": 640}
ROWS = 256
F32 = jnp.float32
BF16 = jnp.bfloat16
ALL = ("dp", "seq")
VMEM = pl.BlockSpec(memory_space=pltpu.VMEM)
SMEM = pl.BlockSpec(memory_space=pltpu.SMEM)
ANY = pl.BlockSpec(memory_space=pl.ANY)
COST = pl.CostEstimate(flops=1000, bytes_accessed=1000, transcendentals=0)


def sds(shape, dtype=F32):
    return jax.ShapeDtypeStruct(shape, dtype)


def over_rows(total, body):
    for i in range(total // ROWS):
        body(pl.ds(i * ROWS, ROWS))


def dot(left, right):
    return jnp.dot(left, right, preferred_element_type=F32)


def dot_t(left, right):
    return lax.dot_general(left, right, (((1,), (1,)), ((), ())), preferred_element_type=F32)


def cmul(ar, ai, br, bi):
    return ar * br - ai * bi, ar * bi + ai * br


def power(cos, sin, times):
    while times > 1:
        cos, sin = cos * cos - sin * sin, 2.0 * cos * sin
        times //= 2
    return cos, sin


def turns(p_ref, half):
    cos, sin = p_ref[3:4, half:], p_ref[4:5, :half]
    return tuple(
        [jnp.broadcast_to(part[:, t * GROUP : (t + 1) * GROUP], (SUB, GROUP)) for t in range(half // GROUP)]
        for part in (cos, sin)
    )


def parts(ref, k, tiles):
    return [ref[k, :, t * GROUP : (t + 1) * GROUP] for t in range(tiles)]


def mix_width(plan, width):
    return 2 * width + width // 2 if plan is None else 2 * HALVES["mix"]


def load_start(pairs, sem):
    for source, target in pairs:
        pltpu.make_async_copy(source, target, sem).start()


def load_wait(pairs, sem):
    for source, target in pairs:
        pltpu.make_async_copy(source, target, sem).wait()


def pairs_of(plan, sources, me_ref, name, target):
    if plan is None:
        return [(sources[{"mix": 0, "out": 1, "up": 2, "down": 3}[name]], target)]
    chip, core = me_ref[1], me_ref[2]
    column, columns = plan[name]
    pairs = []
    for source, (other_core, rels) in enumerate(plan["sources"]):
        half = core ^ other_core
        for b, (zero, one) in enumerate(zip(*rels)):
            block = chip ^ (zero + half * (one - zero))
            if name == "down":
                row, left = block * (2 * UNIT) + half * UNIT, 0
            elif name == "small":
                row, left = block * UNIT, half * GROUP
            else:
                row, left = block * UNIT, half * HALVES[name]
            to = target.at[pl.ds(pl.multiple_of(row, UNIT), UNIT), pl.ds(pl.multiple_of(left, GROUP), columns)]
            pairs.append((sources[source].at[b, :, pl.ds(column, columns)], to))
    return pairs


def front_kernel(
    plan, count, me_ref, x_ref, p_ref, *refs
):
    w_hbm, refs = refs[:count], refs[count:]
    (
    normed_ref, cpre_ref, gate_ref, rate_ref, kept_ref, feed_ref, sub_ref, total_ref,
    w_ref, sem,
    ) = refs
    rows, width = x_ref.shape
    half = width // 2
    block = rows // SUB
    pairs = pairs_of(plan, w_hbm, me_ref, "mix", w_ref)
    load_start(pairs, sem)

    def norm(r):
        x = x_ref[r, :].astype(F32)
        scale = lax.rsqrt(jnp.mean(x * x, axis=1, keepdims=True) + EPS)
        normed_ref[r, :] = (x * scale * p_ref[0:1, :]).astype(BF16)

    over_rows(rows, norm)
    load_wait(pairs, sem)
    normed = normed_ref[...]
    rate = jax.nn.sigmoid(dot(normed, w_ref[:, 2 * width : 2 * width + half]) + p_ref[3:4, :half])
    rate_ref[...] = rate
    at = lax.broadcasted_iota(jnp.int32, (rows, GROUP), 0)
    fresh = at == me_ref[5]
    for j in range(6, me_ref.shape[0]):
        fresh = jnp.logical_or(fresh, at == me_ref[j])
    tiles = half // GROUP
    for t in range(tiles):
        kept_ref[t] = jnp.where(fresh, 0.0, rate[:, t * GROUP : (t + 1) * GROUP])
    for k in range(2):
        cols = slice(k * half, (k + 1) * half)
        pre = dot(normed, w_ref[:, cols])
        cpre_ref[:, cols] = pre
        feed = (1.0 - rate_ref[...]) * (pre * jax.nn.sigmoid(pre))
        for t in range(tiles):
            feed_ref[k * tiles + t] = feed[:, t * GROUP : (t + 1) * GROUP]
    cos, sin = turns(p_ref, half)

    mag = [jnp.ones((SUB, GROUP), F32)] * tiles
    br = [jnp.zeros((SUB, GROUP), F32)] * tiles
    bi = [jnp.zeros((SUB, GROUP), F32)] * tiles
    for j in range(block):
        at = pl.ds(j, SUB, stride=block)
        for t in range(tiles):
            kept = kept_ref[t, at, :]
            tr, ti = cmul(cos[t], sin[t], br[t], bi[t])
            br[t] = kept * tr + feed_ref[t, at, :]
            bi[t] = kept * ti + feed_ref[tiles + t, at, :]
            mag[t] = mag[t] * kept
    mag, br, bi = (jnp.concatenate(part, axis=1) for part in (mag, br, bi))
    far_cos, far_sin = power(jnp.concatenate(cos, axis=1), jnp.concatenate(sin, axis=1), block)
    ar, ai = mag * far_cos, mag * far_sin
    sub_ref[0] = ar
    sub_ref[1] = ai
    sub_ref[2] = br
    sub_ref[3] = bi
    one_r, one_i, sum_r, sum_i = (part[0:1] for part in (ar, ai, br, bi))
    for k in range(1, SUB):
        kr, ki = ar[k : k + 1], ai[k : k + 1]
        one_r, one_i = cmul(kr, ki, one_r, one_i)
        sum_r, sum_i = cmul(kr, ki, sum_r, sum_i)
        sum_r = sum_r + br[k : k + 1]
        sum_i = sum_i + bi[k : k + 1]
    total_ref[0:1, :] = one_r
    total_ref[1:2, :] = one_i
    total_ref[2:3, :] = sum_r
    total_ref[3:4, :] = sum_i
    for k in range(2):
        cols = slice(width + k * half, width + (k + 1) * half)
        gate_ref[:, k * half : (k + 1) * half] = jax.nn.sigmoid(dot(normed, w_ref[:, cols]))


def front(plan, me, x, params, weights):
    rows, width = x.shape
    half = width // 2
    return pl.pallas_call(
        functools.partial(front_kernel, plan, len(weights)),
        out_shape=(
            sds((rows, width), BF16),
            sds((rows, width)),
            sds((rows, width)),
            sds((rows, half)),
            sds((half // GROUP, rows, GROUP)),
            sds((width // GROUP, rows, GROUP)),
            sds((4, SUB, half)),
            sds((4, half)),
        ),
        in_specs=[SMEM, VMEM, VMEM] + [ANY] * len(weights),
        out_specs=(VMEM,) * 8,
        scratch_shapes=[pltpu.VMEM((width, mix_width(plan, width)), BF16), pltpu.SemaphoreType.DMA],
        compiler_params=pltpu.CompilerParams(vmem_limit_bytes=12 << 20),
        cost_estimate=COST,
        name="front",
    )(me, x, params, *weights)


def mid_kernel(plan, count, me_ref, x_ref, p_ref, gate_ref, kept_ref, feed_ref, sub_ref, every_ref, *refs):
    w_hbm, refs = refs[:count], refs[count:]
    states_ref, first_ref, gn_ref, rg_ref, gated_ref, after_ref, lifted_ref, out_ref, sem = refs
    rows, width = x_ref.shape
    half = width // 2
    block = rows // SUB
    pairs = pairs_of(plan, w_hbm, me_ref, "out", out_ref)
    load_start(pairs, sem)

    sr = jnp.zeros((1, half), F32)
    si = jnp.zeros((1, half), F32)
    for k in range(every_ref.shape[0]):
        at = k ^ me_ref[3]
        nr, ni = cmul(every_ref[at, 0:1, :], every_ref[at, 1:2, :], sr, si)
        earlier = k < me_ref[0]
        sr = jnp.where(earlier, nr + every_ref[at, 2:3, :], sr)
        si = jnp.where(earlier, ni + every_ref[at, 3:4, :], si)
    for k in range(SUB):
        first_ref[0, k : k + 1, :] = sr
        first_ref[1, k : k + 1, :] = si
        nr, ni = cmul(sub_ref[0, k : k + 1, :], sub_ref[1, k : k + 1, :], sr, si)
        sr = nr + sub_ref[2, k : k + 1, :]
        si = ni + sub_ref[3, k : k + 1, :]
    cos, sin = turns(p_ref, half)
    tiles = half // GROUP
    sr = parts(first_ref, 0, tiles)
    si = parts(first_ref, 1, tiles)
    for j in range(block):
        at = pl.ds(j, SUB, stride=block)
        for t in range(tiles):
            kept = kept_ref[t, at, :]
            tr, ti = cmul(cos[t], sin[t], sr[t], si[t])
            sr[t] = kept * tr + feed_ref[t, at, :]
            si[t] = kept * ti + feed_ref[tiles + t, at, :]
            states_ref[t, at, :] = sr[t]
            states_ref[tiles + t, at, :] = si[t]

    lane = lax.broadcasted_iota(jnp.int32, (ROWS, GROUP), 1)

    def group_norm(r):
        held = jnp.zeros((ROWS, GROUP), F32)
        for g in range(width // GROUP):
            cols = slice(g * GROUP, (g + 1) * GROUP)
            v = gate_ref[r, cols] * states_ref[g, r, :]
            centre = v - jnp.mean(v, axis=1, keepdims=True)
            scale = lax.rsqrt(jnp.mean(centre * centre, axis=1, keepdims=True) + EPS)
            gn = centre * scale
            gn_ref[r, cols] = gn
            gated_ref[r, cols] = (gn * p_ref[1:2, cols]).astype(BF16)
            held = jnp.where(lane == g, scale, held)
        rg_ref[r, :] = held

    over_rows(rows, group_norm)
    load_wait(pairs, sem)
    after_ref[...] = x_ref[...].astype(F32) + dot(gated_ref[...], out_ref[...])

    def norm(r):
        after = after_ref[r, :]
        scale = lax.rsqrt(jnp.mean(after * after, axis=1, keepdims=True) + EPS)
        lifted_ref[r, :] = (after * scale * p_ref[2:3, :]).astype(BF16)

    over_rows(rows, norm)


def mid(plan, me, x, params, gate, kept, feed, sub, every, weights):
    rows, width = x.shape
    half = width // 2
    return pl.pallas_call(
        functools.partial(mid_kernel, plan, len(weights)),
        out_shape=(
            sds((width // GROUP, rows, GROUP)),
            sds((2, SUB, half)),
            sds((rows, width)),
            sds((rows, GROUP)),
            sds((rows, width), BF16),
            sds((rows, width)),
            sds((rows, width), BF16),
        ),
        in_specs=[SMEM] + [VMEM] * 7 + [ANY] * len(weights),
        out_specs=(VMEM,) * 7,
        scratch_shapes=[pltpu.VMEM((width, width), BF16), pltpu.SemaphoreType.DMA],
        compiler_params=pltpu.CompilerParams(vmem_limit_bytes=12 << 20),
        cost_estimate=COST,
        name="mid",
    )(me, x, params, gate, kept, feed, sub, every, *weights)


def ffn_kernel(plan, count, me_ref, after_ref, lifted_ref, *refs):
    w_hbm, refs = refs[:count], refs[count:]
    both_ref, hidden_ref, next_ref, up_ref, down_ref, sems = refs
    inner = hidden_ref.shape[1]
    up_pairs = pairs_of(plan, w_hbm, me_ref, "up", up_ref)
    down_pairs = pairs_of(plan, w_hbm, me_ref, "down", down_ref)
    load_start(up_pairs, sems.at[0])
    load_start(down_pairs, sems.at[1])
    load_wait(up_pairs, sems.at[0])
    lifted = lifted_ref[...]
    step = after_ref.shape[1] // 2
    for k in range(inner // step):
        cols = slice(k * step, (k + 1) * step)
        more = slice(inner + k * step, inner + (k + 1) * step)
        a = dot(lifted, up_ref[:, cols])
        b = dot(lifted, up_ref[:, more])
        both_ref[:, cols] = a
        both_ref[:, more] = b
        hidden_ref[:, cols] = (a * jax.nn.sigmoid(a) * b).astype(BF16)
    load_wait(down_pairs, sems.at[1])
    next_ref[...] = (after_ref[...] + dot(hidden_ref[...], down_ref[...])).astype(next_ref.dtype)


def ffn(plan, me, after, lifted, weights, dtype):
    rows, width = after.shape
    inner = 2 * width
    return pl.pallas_call(
        functools.partial(ffn_kernel, plan, len(weights)),
        out_shape=(sds((rows, 2 * inner)), sds((rows, inner), BF16), sds((rows, width), dtype)),
        in_specs=[SMEM] + [VMEM] * 2 + [ANY] * len(weights),
        out_specs=(VMEM,) * 3,
        scratch_shapes=[
            pltpu.VMEM((width, 2 * inner), BF16),
            pltpu.VMEM((inner, width), BF16),
            pltpu.SemaphoreType.DMA((2,)),
        ],
        compiler_params=pltpu.CompilerParams(vmem_limit_bytes=17 << 20),
        cost_estimate=COST,
        name="ffn",
    )(me, after, lifted, *weights)


def lower(me_ref, dx_ref, dlow_ref):
    rows, width = dx_ref.shape
    if dx_ref.dtype == BF16:
        at = lax.broadcasted_iota(jnp.int32, (rows, GROUP), 0)
        live = at < me_ref[4]
        for t in range(width // GROUP):
            cols = slice(t * GROUP, (t + 1) * GROUP)
            dlow_ref[:, cols] = jnp.where(live, dx_ref[:, cols].astype(F32), 0.0).astype(BF16)
        return dlow_ref
    dlow_ref[...] = dx_ref[...].astype(BF16)
    return dx_ref


def lift_back(grad_ref, p_ref, after_ref, work_ref, dafter_ref, dmid_ref, gain_ref):
    def norm_back(r):
        after = after_ref[r, :]
        scale = lax.rsqrt(jnp.mean(after * after, axis=1, keepdims=True) + EPS)
        normal = after * scale
        lift = work_ref[r, :]
        e = lift * p_ref[2:3, :]
        d = grad_ref[r, :].astype(F32) + scale * (e - normal * jnp.mean(e * normal, axis=1, keepdims=True))
        dafter_ref[r, :] = d
        dmid_ref[r, :] = d.astype(BF16)
        work_ref[r, :] = lift * normal

    over_rows(after_ref.shape[0], norm_back)
    gain_ref[...] = jnp.sum(work_ref[...], axis=0, keepdims=True)


def back_ffn_kernel(plan, count, rels, me_ref, dx_ref, p_ref, both_ref, after_ref, *refs):
    w_hbm, refs = refs[:count], refs[count:]
    if rels is not None:
        lifted_ref, keep_ref, send_ref, *refs, dboth_ref, grad_up_ref, out_sem = refs
        dlow_ref, *refs = refs
    else:
        dlow_ref, dboth_ref, *refs = refs
    dafter_ref, dmid_ref, gain_ref, work_ref, up_ref, down_ref, sems = refs
    rows, width = dx_ref.shape
    inner = down_ref.shape[0]
    up_pairs = pairs_of(plan, w_hbm, me_ref, "up", up_ref)
    down_pairs = pairs_of(plan, w_hbm, me_ref, "down", down_ref)
    load_start(down_pairs, sems.at[1])
    load_start(up_pairs, sems.at[0])
    grad_ref = lower(me_ref, dx_ref, dlow_ref)
    dlow = dlow_ref[...]
    load_wait(down_pairs, sems.at[1])
    step = width // 2
    for k in range(inner // step):
        cols = slice(k * step, (k + 1) * step)
        more = slice(inner + k * step, inner + (k + 1) * step)
        dh = dot_t(dlow, down_ref[cols, :])
        a = both_ref[:, cols]
        sig = jax.nn.sigmoid(a)
        dboth_ref[:, cols] = (dh * both_ref[:, more] * (sig * (1.0 + a * (1.0 - sig)))).astype(BF16)
        dboth_ref[:, more] = (dh * (a * sig)).astype(BF16)
    if rels is not None:
        products(lifted_ref[...], dboth_ref, grad_up_ref, grad_up_ref.shape[1])
        pairs = export(me_ref, rels, "up", grad_up_ref, 0, HALVES["up"], keep_ref, send_ref, out_sem)
    load_wait(up_pairs, sems.at[0])
    work_ref[...] = dot_t(dboth_ref[...], up_ref[...])

    lift_back(grad_ref, p_ref, after_ref, work_ref, dafter_ref, dmid_ref, gain_ref)
    if rels is not None:
        load_wait(pairs, out_sem)


def turn_kernel(plan, count, rels, me_ref, dx_ref, p_ref, after_ref, lifted_ref, *refs):
    w_hbm, refs = refs[:count], refs[count:]
    (
        keep_ref, send_ref, next_ref, hidden_ref, dlow_ref, dafter_ref, dmid_ref, gain_ref,
        dboth_ref, grad_up_ref, work_ref, up_ref, down_ref, sems, out_sem,
    ) = refs
    width = dx_ref.shape[1]
    inner = down_ref.shape[0]
    up_pairs = pairs_of(plan, w_hbm, me_ref, "up", up_ref)
    down_pairs = pairs_of(plan, w_hbm, me_ref, "down", down_ref)
    load_start(up_pairs, sems.at[0])
    load_start(down_pairs, sems.at[1])
    grad_ref = lower(me_ref, dx_ref, dlow_ref)
    dlow = dlow_ref[...]
    lifted = lifted_ref[...]
    load_wait(up_pairs, sems.at[0])
    load_wait(down_pairs, sems.at[1])
    step = width // 2
    for k in range(inner // step):
        cols = slice(k * step, (k + 1) * step)
        more = slice(inner + k * step, inner + (k + 1) * step)
        a = dot(lifted, up_ref[:, cols])
        b = dot(lifted, up_ref[:, more])
        dh = dot_t(dlow, down_ref[cols, :])
        sig = jax.nn.sigmoid(a)
        gated = a * sig
        hidden_ref[:, cols] = (gated * b).astype(BF16)
        dboth_ref[:, cols] = (dh * b * (sig * (1.0 + a * (1.0 - sig)))).astype(BF16)
        dboth_ref[:, more] = (dh * gated).astype(BF16)
    products(lifted, dboth_ref, grad_up_ref, grad_up_ref.shape[1])
    pairs = export(me_ref, rels, "up", grad_up_ref, 0, HALVES["up"], keep_ref, send_ref, out_sem)
    work_ref[...] = dot_t(dboth_ref[...], up_ref[...])
    lift_back(grad_ref, p_ref, after_ref, work_ref, dafter_ref, dmid_ref, gain_ref)
    next_ref[...] = (after_ref[...] + dot(hidden_ref[...], down_ref[...])).astype(next_ref.dtype)
    load_wait(pairs, out_sem)


def turn(plan, rels, me, dx, params, after, lifted, weights):
    rows, width = dx.shape
    inner = 2 * width
    block = sds((2 ** len(STAGES), UNIT, HALVES["up"]), BF16)
    low = sds((rows, width), BF16)
    return pl.pallas_call(
        functools.partial(turn_kernel, plan, len(weights), rels),
        out_shape=(block, block, low, sds((rows, inner), BF16), low, sds((rows, width)), low, sds((1, width))),
        in_specs=[SMEM] + [VMEM] * 4 + [ANY] * len(weights),
        out_specs=(ANY, ANY) + (VMEM,) * 6,
        scratch_shapes=[
            pltpu.VMEM((rows, 2 * inner), BF16),
            pltpu.VMEM((width, 2 * inner), BF16),
            pltpu.VMEM((rows, width), F32),
            pltpu.VMEM((width, 2 * inner), BF16),
            pltpu.VMEM((inner, width), BF16),
            pltpu.SemaphoreType.DMA((2,)),
            pltpu.SemaphoreType.DMA,
        ],
        compiler_params=pltpu.CompilerParams(vmem_limit_bytes=22 << 20),
        cost_estimate=COST,
        name="turn",
    )(me, dx, params, after, lifted, *weights)


def back_ffn(plan, me, dx, params, both, after, weights, rels=None, lifted=()):
    rows, width = dx.shape
    inner = 2 * width
    block = sds((2 ** len(STAGES), UNIT, HALVES["up"]), BF16)
    dboth = (rows, 2 * inner)
    outs = (sds((rows, width), BF16), sds(dboth, BF16), sds((rows, width)), sds((rows, width), BF16), sds((1, width)))
    specs, more = (VMEM,) * 5, []
    if rels is not None:
        outs, specs = (block, block, outs[0], *outs[2:]), (ANY, ANY, *specs[1:])
        more = [pltpu.VMEM(dboth, BF16), pltpu.VMEM((width, 2 * inner), BF16), pltpu.SemaphoreType.DMA]
    return pl.pallas_call(
        functools.partial(back_ffn_kernel, plan, len(weights), rels),
        out_shape=outs,
        in_specs=[SMEM] + [VMEM] * 4 + [ANY] * len(weights) + [VMEM] * len(lifted),
        out_specs=specs,
        scratch_shapes=[
            pltpu.VMEM((rows, width), F32),
            pltpu.VMEM((width, 2 * inner), BF16),
            pltpu.VMEM((inner, width), BF16),
            pltpu.SemaphoreType.DMA((2,)),
        ]
        + more,
        compiler_params=pltpu.CompilerParams(vmem_limit_bytes=25 << 20),
        cost_estimate=COST,
        name="back_ffn",
    )(me, dx, params, both, after, *weights, *lifted)


def back_mid_kernel(
    plan, count, me_ref, dmid_ref, p_ref, gn_ref, rg_ref, gate_ref, states_ref, kept_ref, sub_ref, *refs
):
    w_hbm, refs = refs[:count], refs[count:]
    dgpre_ref, dstates_ref, gain_ref, rsub_ref, rtotal_ref, work_ref, out_ref, sem = refs
    rows, width = dmid_ref.shape
    half = width // 2
    block = rows // SUB
    pairs = pairs_of(plan, w_hbm, me_ref, "out", out_ref)
    load_start(pairs, sem)
    load_wait(pairs, sem)
    work_ref[...] = dot_t(dmid_ref[...], out_ref[...])

    def group_back(r):
        held = rg_ref[r, :]
        for g in range(width // GROUP):
            cols = slice(g * GROUP, (g + 1) * GROUP)
            gn = gn_ref[r, cols]
            dg = work_ref[r, cols]
            e = dg * p_ref[1:2, cols]
            dv = held[:, g : g + 1] * (
                e - jnp.mean(e, axis=1, keepdims=True) - gn * jnp.mean(e * gn, axis=1, keepdims=True)
            )
            gate = gate_ref[r, cols]
            dgpre_ref[r, cols] = (dv * states_ref[g, r, :] * gate * (1.0 - gate)).astype(BF16)
            dstates_ref[g, r, :] = dv * gate
            work_ref[r, cols] = dg * gn

    over_rows(rows, group_back)
    gain_ref[...] = jnp.sum(work_ref[...], axis=0, keepdims=True)

    cos, sin = turns(p_ref, half)
    tiles = half // GROUP
    zr = [jnp.zeros((SUB, GROUP), F32)] * tiles
    zi = [jnp.zeros((SUB, GROUP), F32)] * tiles
    for j in reversed(range(block)):
        at = pl.ds(j, SUB, stride=block)
        for t in range(tiles):
            kept = kept_ref[t, at, :]
            qr = dstates_ref[t, at, :] + zr[t]
            qi = dstates_ref[tiles + t, at, :] + zi[t]
            zr[t] = kept * (cos[t] * qr + sin[t] * qi)
            zi[t] = kept * (cos[t] * qi - sin[t] * qr)
    zr, zi = jnp.concatenate(zr, axis=1), jnp.concatenate(zi, axis=1)
    rsub_ref[0] = zr
    rsub_ref[1] = zi
    tr = jnp.zeros((1, half), F32)
    ti = jnp.zeros((1, half), F32)
    for k in reversed(range(SUB)):
        ar, ai = sub_ref[0, k : k + 1, :], sub_ref[1, k : k + 1, :]
        tr, ti = ar * tr + ai * ti + zr[k : k + 1], ar * ti - ai * tr + zi[k : k + 1]
    rtotal_ref[0:1, :] = tr
    rtotal_ref[1:2, :] = ti


def back_mid(plan, me, dmid, params, gn, rg, gate, states, kept, sub, weights):
    rows, width = dmid.shape
    half = width // 2
    return pl.pallas_call(
        functools.partial(back_mid_kernel, plan, len(weights)),
        out_shape=(
            sds((rows, width), BF16),
            sds((width // GROUP, rows, GROUP)),
            sds((1, width)),
            sds((2, SUB, half)),
            sds((2, half)),
        ),
        in_specs=[SMEM] + [VMEM] * 8 + [ANY] * len(weights),
        out_specs=(VMEM,) * 5,
        scratch_shapes=[
            pltpu.VMEM((rows, width), F32),
            pltpu.VMEM((width, width), BF16),
            pltpu.SemaphoreType.DMA,
        ],
        compiler_params=pltpu.CompilerParams(vmem_limit_bytes=11 << 20),
        cost_estimate=COST,
        name="back_mid",
    )(me, dmid, params, gn, rg, gate, states, kept, sub, *weights)


def back_two_kernel(
    plan, count, rels, spare, me_ref, x_ref, p_ref, dafter_ref, dgpre_ref, dstates_ref, states_ref, kept_ref, rate_ref, cpre_ref,
    first_ref, sub_ref, rsub_ref, every_ref, revery_ref, *refs
):
    w_hbm, extra, refs = refs[:count], refs[count : count + spare], refs[count + spare :]
    if rels is not None:
        normed_ref, *extra = extra
        keep_ref, send_ref, dx_ref, gains_ref, *refs, mix_ref, held_ref, out_sem = refs
        dmixin_ref, *refs = refs
    else:
        dmixin_ref, dx_ref, gains_ref, *refs = refs
    work_ref, q_ref, turn_ref, start_ref, w_ref, sem = refs
    rows, width = x_ref.shape
    half = width // 2
    block = rows // SUB
    pairs = pairs_of(plan, w_hbm, me_ref, "mix", w_ref)
    load_start(pairs, sem)
    zr = jnp.zeros((1, half), F32)
    zi = jnp.zeros((1, half), F32)
    for k in reversed(range(every_ref.shape[0])):
        at = k ^ me_ref[3]
        ar, ai = every_ref[at, 0:1, :], every_ref[at, 1:2, :]
        later = k > me_ref[0]
        nr = ar * zr + ai * zi + revery_ref[at, 0:1, :]
        ni = ar * zi - ai * zr + revery_ref[at, 1:2, :]
        zr = jnp.where(later, nr, zr)
        zi = jnp.where(later, ni, zi)
    for k in reversed(range(SUB)):
        start_ref[0, k : k + 1, :] = zr
        start_ref[1, k : k + 1, :] = zi
        ar, ai = sub_ref[0, k : k + 1, :], sub_ref[1, k : k + 1, :]
        zr, zi = (
            ar * zr + ai * zi + rsub_ref[0, k : k + 1, :],
            ar * zi - ai * zr + rsub_ref[1, k : k + 1, :],
        )
    cos, sin = turns(p_ref, half)
    tiles = half // GROUP
    zr = parts(start_ref, 0, tiles)
    zi = parts(start_ref, 1, tiles)
    angle = [jnp.zeros((SUB, GROUP), F32)] * tiles
    for j in reversed(range(block)):
        at = pl.ds(j, SUB, stride=block)
        before = pl.ds(max(j - 1, 0), SUB, stride=block)
        for t in range(tiles):
            kept = kept_ref[t, at, :]
            qr = dstates_ref[t, at, :] + zr[t]
            qi = dstates_ref[tiles + t, at, :] + zi[t]
            q_ref[t, at, :] = qr
            q_ref[tiles + t, at, :] = qi
            zr[t] = kept * (cos[t] * qr + sin[t] * qi)
            zi[t] = kept * (cos[t] * qi - sin[t] * qr)
            if j:
                sr, si = states_ref[t, before, :], states_ref[tiles + t, before, :]
            else:
                sr, si = (first_ref[k, :, t * GROUP : (t + 1) * GROUP] for k in range(2))
            turn_ref[t, at, :] = zr[t] * sr + zi[t] * si
            angle[t] = angle[t] + (zi[t] * sr - zr[t] * si)
    gains_ref[1:2, half:] = jnp.sum(jnp.concatenate(angle, axis=1), axis=0, keepdims=True)

    def activations(r):
        for t in range(tiles):
            rate = rate_ref[r, t * GROUP : (t + 1) * GROUP]
            left = 1.0 - rate
            meet = jnp.zeros_like(rate)
            for k in range(2):
                cols = slice((k * tiles + t) * GROUP, (k * tiles + t + 1) * GROUP)
                pre = cpre_ref[r, cols]
                sig = jax.nn.sigmoid(pre)
                q = q_ref[k * tiles + t, r, :]
                meet = meet + q * (pre * sig)
                dmixin_ref[r, cols] = (left * q * (sig * (1.0 + pre * (1.0 - sig)))).astype(BF16)
            dfpre = left * (turn_ref[t, r, :] - rate * meet)
            dmixin_ref[r, 2 * width + t * GROUP : 2 * width + (t + 1) * GROUP] = dfpre.astype(BF16)
            turn_ref[t, r, :] = dfpre
        dmixin_ref[r, width : 2 * width] = dgpre_ref[r, :]

    over_rows(rows, activations)
    for t in range(tiles):
        gains_ref[1:2, t * GROUP : (t + 1) * GROUP] = jnp.sum(turn_ref[t], axis=0, keepdims=True)
    load_wait(pairs, sem)
    work_ref[...] = dot_t(dmixin_ref[...], w_ref[:, : dmixin_ref.shape[1]])

    def norm_back(r):
        x = x_ref[r, :].astype(F32)
        scale = lax.rsqrt(jnp.mean(x * x, axis=1, keepdims=True) + EPS)
        normal = x * scale
        dn = work_ref[r, :]
        e = dn * p_ref[0:1, :]
        dx_ref[r, :] = dafter_ref[r, :] + scale * (e - normal * jnp.mean(e * normal, axis=1, keepdims=True))
        work_ref[r, :] = dn * normal

    over_rows(rows, norm_back)
    gains_ref[0:1, :] = jnp.sum(work_ref[...], axis=0, keepdims=True)

    if rels is None:
        return
    held_ref[...] = jnp.zeros_like(held_ref)
    for k in range(spare // 3):
        two, mid_gain, ffn_gain = (gains_ref, *extra)[3 * k : 3 * k + 3]
        held_ref[4 * k : 4 * k + 1, :] = two[0:1, :]
        held_ref[4 * k + 1 : 4 * k + 2, :] = mid_gain[...]
        held_ref[4 * k + 2 : 4 * k + 3, :] = ffn_gain[...]
        held_ref[4 * k + 3 : 4 * k + 4, :] = two[1:2, :]
    normed = normed_ref[...]
    products(normed, dmixin_ref, mix_ref, width)
    products(normed, dmixin_ref, mix_ref, half, 2 * width, width)
    mix_ref[:, width + half :] = jnp.transpose(held_ref[...]).astype(BF16)
    pairs = export(me_ref, rels, "cell", mix_ref, 0, HALVES["cell"], keep_ref, send_ref, out_sem)
    load_wait(pairs, out_sem)


def back_two(plan, me, x, params, dafter, dgpre, dstates, states, kept, rate, cpre, first, sub, rsub, every, revery, weights, rels=None, extra=()):
    rows, width = x.shape
    half = width // 2
    size = 2 * width + half
    block = sds((2 ** len(STAGES), UNIT, HALVES["cell"]), BF16)
    scratch = [
        pltpu.VMEM((rows, width), F32),
        pltpu.VMEM((width // GROUP, rows, GROUP), F32),
        pltpu.VMEM((half // GROUP, rows, GROUP), F32),
        pltpu.VMEM((2, SUB, half), F32),
        pltpu.VMEM((width, mix_width(plan, width)), BF16),
        pltpu.SemaphoreType.DMA,
    ]
    if rels is None:
        first_out, specs, more = (sds((rows, size), BF16),), (VMEM,), []
    else:
        first_out, specs = (block, block), (ANY, ANY)
        scratch.insert(0, pltpu.VMEM((rows, size), BF16))
        more = [pltpu.VMEM((width, 2 * HALVES["cell"]), BF16), pltpu.VMEM((GROUP, width), F32), pltpu.SemaphoreType.DMA]
    return pl.pallas_call(
        functools.partial(back_two_kernel, plan, len(weights), rels, len(extra)),
        out_shape=first_out + (sds((rows, width)), sds((2, width))),
        in_specs=[SMEM] + [VMEM] * 14 + [ANY] * len(weights) + [VMEM] * len(extra),
        out_specs=specs + (VMEM, VMEM),
        scratch_shapes=scratch + more,
        compiler_params=pltpu.CompilerParams(vmem_limit_bytes=18 << 20),
        cost_estimate=COST,
        name="back_two",
    )(me, x, params, dafter, dgpre, dstates, states, kept, rate, cpre, first, sub, rsub, every, revery, *weights, *extra)


def row_product(left, right):
    return lax.dot_general(left, right, (((0,), (0,)), ((), ())), preferred_element_type=F32)


def export(info_ref, rels, name, grad, column, columns, keep_ref, send_ref, sem):
    chip, core = info_ref[1], info_ref[2]
    pairs = []
    for half, target in ((1 - core, send_ref), (core, keep_ref)):
        for b, (zero, one) in enumerate(zip(*rels)):
            block = chip ^ (zero + half * (one - zero))
            if name == "down":
                row, left = block * (2 * UNIT) + half * UNIT, 0
            else:
                row, left = block * UNIT, half * HALVES[name]
            pairs.append(
                (
                    grad.at[pl.ds(pl.multiple_of(row, UNIT), UNIT), pl.ds(pl.multiple_of(left, GROUP), columns)],
                    target.at[b, :, pl.ds(column, columns)],
                )
            )
    load_start(pairs, sem)
    return pairs


def products(left, right_ref, grad_ref, size, source=0, target=0):
    step = HALVES["out"]
    for k in range(0, size, step):
        right = right_ref[:, source + k : source + k + step]
        grad_ref[:, target + k : target + k + step] = row_product(left, right).astype(BF16)


def grad_od_kernel(
    rels, info_ref, gated_ref, dmid_ref, hidden_ref, dlow_ref, normed_ref, dgpre_ref, keep_ref, send_ref,
    out_ref, gate_ref, down_ref, sem,
):
    width = dlow_ref.shape[1]
    products(hidden_ref[...], dlow_ref, down_ref, width)
    at = HALVES["out"] + HALVES["gate"]
    pairs = export(info_ref, rels, "down", down_ref, at, width, keep_ref, send_ref, sem)
    products(gated_ref[...], dmid_ref, out_ref, width)
    pairs += export(info_ref, rels, "out", out_ref, 0, HALVES["out"], keep_ref, send_ref, sem)
    products(normed_ref[...], dgpre_ref, gate_ref, width)
    pairs += export(info_ref, rels, "gate", gate_ref, HALVES["out"], HALVES["gate"], keep_ref, send_ref, sem)
    load_wait(pairs, sem)


def grad_od(rels, info, gated, dmid, hidden, dlow, normed, dgpre):
    width = dlow.shape[1]
    shape = sds((len(rels[0]), UNIT, HALVES["out"] + HALVES["gate"] + width), BF16)
    return pl.pallas_call(
        functools.partial(grad_od_kernel, rels),
        out_shape=(shape, shape),
        in_specs=[SMEM] + [VMEM] * 6,
        out_specs=(ANY, ANY),
        scratch_shapes=[
            pltpu.VMEM((width, width), BF16),
            pltpu.VMEM((width, width), BF16),
            pltpu.VMEM((hidden.shape[1], width), BF16),
            pltpu.SemaphoreType.DMA,
        ],
        compiler_params=pltpu.CompilerParams(vmem_limit_bytes=11 << 20),
        cost_estimate=COST,
        name="grad_od",
    )(info, gated, dmid, hidden, dlow, normed, dgpre)


def table_kernel(plan, count, me_ref, *refs):
    sources, (table_ref, held_ref, sem) = refs[:count], refs[count:]
    pairs = pairs_of(plan, sources, me_ref, "small", held_ref)
    load_start(pairs, sem)
    load_wait(pairs, sem)
    depth = table_ref.shape[0]
    half = table_ref.shape[2] // 2
    table = jnp.transpose(held_ref[:, GROUP:].astype(F32))
    table_ref[...] = jnp.zeros_like(table_ref)
    for l in range(depth):
        chan = table[3 * depth + l : 3 * depth + l + 1]
        table_ref[l, 0:3, :] = table[3 * l : 3 * l + 3]
        table_ref[l, 3:4, :half] = chan[:, :half]
        table_ref[l, 3:4, half:] = jnp.cos(chan[:, half:])
        table_ref[l, 4:5, :half] = jnp.sin(chan[:, half:])


def table_of(plan, me, weights, depth, width):
    return pl.pallas_call(
        functools.partial(table_kernel, plan, len(weights)),
        out_shape=sds((depth, 8, width)),
        in_specs=[SMEM] + [ANY] * len(weights),
        out_specs=VMEM,
        scratch_shapes=[pltpu.VMEM((width, 2 * GROUP), BF16), pltpu.SemaphoreType.DMA],
        compiler_params=pltpu.CompilerParams(vmem_limit_bytes=6 << 20),
        cost_estimate=COST,
        name="table",
    )(me, *weights)


def swap(x, bits):
    count = lax.axis_size("dp") * lax.axis_size("seq")
    return lax.ppermute(x, ALL, [(i, i ^ bits[i % 2]) for i in range(count)])


class Order:
    def __init__(self):
        self.last = None

    def step(self, *values):
        if self.last is not None:
            values = lax.optimization_barrier(values + (self.last,))[: len(values)]
        self.last = values[0]
        return values

    def join(self, *moves, cores=()):
        values = [move.got for move in moves]
        for move in cores:
            values += [move.last_core, move.held_core]
        values = list(self.step(*values))
        for move in moves:
            move.got = values.pop(0)
        for move in cores:
            move.last_core, move.held_core = values.pop(0), values.pop(0)


    def pass_on(self, *moves):
        for move in moves:
            move.ready()
        for move, value in zip(moves, self.step(*(move.out for move in moves))):
            move.out = value
            move.send()


def rels_of(stages):
    rels = ([0], [0])
    for bits in stages:
        for core in range(2):
            rels[core].extend([rel ^ bits[core] for rel in rels[core]])
    return rels


class Spread:
    def __init__(self, unit, stages):
        self.held, self.stages, self.at = unit[None], stages, 0
        self.got = None

    def join(self):
        if self.got is not None:
            self.held = jnp.concatenate([self.held, self.got])

    def ready(self):
        self.join()
        self.out = self.held

    def send(self):
        self.held = self.out
        one, two = self.stages[self.at]
        self.at += 1
        self.got = swap(self.held, (2 * one, 2 * two))

    def end(self):
        self.near, self.last = self.held, self.got
        self.last_core = swap(self.last, (1, 1))

    def near_core(self):
        self.held_core = swap(self.held, (1, 1))

    def arrays(self):
        return (self.near, self.held_core, self.last, self.last_core)

    def sources(self):
        rels = rels_of(self.stages)
        half = len(rels[0]) // 2
        low = tuple(tuple(rel[:half]) for rel in rels)
        high = tuple(tuple(rel[half:]) for rel in rels)
        return ((0, low), (1, low), (0, high), (1, high))


class Reduce:
    def __init__(self, keep, send, stages):
        self.held, self.stages = keep, list(stages)
        self.got = swap(send, (1, 1))

    def add(self):
        half = self.held.shape[0] // 2
        if not half:
            return self.held[0].astype(F32) + self.got[0].astype(F32)

        def joined(part):
            return (self.held[part].astype(F32) + self.got[part].astype(F32)).astype(BF16)

        self.held, self.out = joined(slice(0, half)), joined(slice(half, None))
        self.got = None

    def ready(self):
        if self.got is not None:
            self.add()

    def send(self):
        one, two = self.stages.pop()
        self.got = swap(self.out, (2 * one, 2 * two))


def exchange(x, order=None):
    other = swap(x, (1, 1))
    if order is not None:
        (other,) = order.step(other)
    pair = jnp.stack([x, other])
    got = [swap(pair, (k, k)) for k in range(2, lax.axis_size("seq"), 2)]
    return jnp.concatenate([pair] + got)


def finish_kernel(info_ref, *refs):
    depth = (len(refs) - 5) // 3
    mine, other, downs = refs[:depth], refs[depth : 2 * depth], refs[2 * depth : 3 * depth]
    mix_ref, out_ref, up_ref, down_ref, tail_ref = refs[3 * depth :]
    width = down_ref.shape[2]
    size = HALVES["cell"]

    def place(first, second):
        for l in range(depth):
            rest = width - size
            mix_ref[l, :, :size] = first[l][:, :size]
            mix_ref[l, :, size:width] = second[l][:, :rest]
            mix_ref[l, :, 2 * width :] = second[l][:, rest : size - GROUP]
            at = size
            for name, ref, begin in (("out", out_ref, 0), ("gate", mix_ref, width), ("up", up_ref, 0)):
                step = HALVES[name]
                ref[l, :, begin : begin + step] = first[l][:, at : at + step]
                ref[l, :, begin + step : begin + 2 * step] = second[l][:, at : at + step]
                at += step
        tail_ref[...] = second[0][:, size - GROUP : size]

    @pl.when(info_ref[2] == 0)
    def _():
        place(mine, other)

    @pl.when(info_ref[2] == 1)
    def _():
        place(other, mine)

    for l in range(depth):
        down_ref[l] = downs[l][:, downs[l].shape[1] - width :]


def finish(info, mine, other, downs, shapes):
    share = mine[0].shape[0]
    return pl.pallas_call(
        finish_kernel,
        out_shape=tuple(sds(shape) for shape in shapes) + (sds((share, GROUP)),),
        in_specs=[SMEM] + [VMEM] * (3 * len(mine)),
        out_specs=(VMEM,) * 5,
        compiler_params=pltpu.CompilerParams(vmem_limit_bytes=8 << 20),
        cost_estimate=COST,
        name="finish",
    )(info, *mine, *other, *downs)


def layer_params(gains, chan):
    half = chan.shape[0] // 2
    angle = chan[half:]
    rows = [
        gains[0],
        gains[1],
        gains[2],
        jnp.concatenate([chan[:half], jnp.cos(angle)]),
        jnp.concatenate([jnp.sin(angle), jnp.zeros((half,), F32)]),
    ]
    return jnp.concatenate([jnp.stack(rows), jnp.zeros((3, 2 * half), F32)], axis=0)


STAGES = ((4, 8), (8, 4), (1, 2), (2, 1))
LATER = ((1, 2), (4, 8), (8, 4), (2, 1))
UPPER = (STAGES, LATER, STAGES)
LOWER = (LATER, STAGES, STAGES)


def small_of(gains, chan_params):
    depth, _, share = gains.shape
    return jnp.concatenate(
        [gains.reshape(depth * 3, share).T, chan_params.T, jnp.zeros((share, GROUP - 4 * depth), BF16)], axis=1
    )


def info_of(lengths, rows, turned):
    where = lax.axis_index("seq")
    base = where * rows
    ends = [lengths[0, 0]]
    for j in range(1, lengths.shape[1]):
        ends.append(ends[-1] + lengths[0, j])
    chip = (lax.axis_index("dp") * lax.axis_size("seq") + where) // 2
    values = [where, chip, where % 2, where if turned else jnp.zeros_like(where), ends[-1] - base]
    values += [end - lengths[0, j] - base for j, end in enumerate(ends)]
    return jnp.stack([value.astype(jnp.int32) for value in values])


def plain_body(stream, w_mix, w_out, w_up, w_down, gains, chan_params, lengths, cotangent):
    rows, width = stream.shape
    depth = w_mix.shape[0]
    info = info_of(lengths, rows, False)
    small = small_of(gains, chan_params)
    table = lax.all_gather(small, ALL, axis=0, tiled=True)[:, : 4 * depth].T.astype(F32)
    params = [layer_params(table[3 * l : 3 * l + 3], table[3 * depth + l]) for l in range(depth)]
    weights = [
        tuple(lax.all_gather(w[l], ALL, axis=0, tiled=True) for w in (w_mix, w_out, w_up, w_down))
        for l in range(depth)
    ]
    x = stream
    saved = []
    for l in range(depth):
        head = front(None, info, x, params[l], weights[l])
        every = lax.all_gather(head[-1], "seq")
        middle = mid(None, info, x, params[l], head[2], head[4], head[5], head[6], every, weights[l])
        tail = ffn(None, info, middle[5], middle[6], weights[l], F32)
        saved.append((x, every, head, middle, tail))
        x = tail[-1]
    mixed = x.astype(BF16)
    dx = cotangent
    sums = [None] * depth
    for l in reversed(range(depth)):
        x, every, (normed, cpre, gate, rate, kept, feed, sub, _), middle, (both, hidden, _) = saved[l]
        states, first, gn, rg, gated, after, lifted = middle
        dlow, dboth, dafter, dmid, ffn_gain = back_ffn(None, info, dx, params[l], both, after, weights[l])
        dgpre, dstates, mid_gain, rsub, rtotal = back_mid(
            None, info, dmid, params[l], gn, rg, gate, states, kept, sub, weights[l]
        )
        revery = lax.all_gather(rtotal, "seq")
        dmixin, dx, gains_b = back_two(
            None, info, x, params[l], dafter, dgpre, dstates, states, kept, rate, cpre, first, sub, rsub, every, revery,
            weights[l],
        )
        grads = [row_product(normed, dmixin), row_product(gated, dmid), row_product(lifted, dboth), row_product(hidden, dlow)]
        grads.append(jnp.stack([gains_b[0], mid_gain[0], ffn_gain[0], gains_b[1]], axis=1))
        sums[l] = [lax.psum_scatter(g.astype(BF16), ALL, scatter_dimension=0, tiled=True).astype(F32) for g in grads]
    outs = [jnp.stack([sums[l][k] for l in range(depth)]) for k in range(5)]
    tail = outs.pop()
    return (mixed, dx, *outs, jnp.swapaxes(tail[:, :, :3], 1, 2), tail[:, :, 3])


def fast_body(stream, w_mix, w_out, w_up, w_down, gains, chan_params, lengths, cotangent):
    rows, width = stream.shape
    depth, share, mix_cols = w_mix.shape
    info = info_of(lengths, rows, True)
    small = small_of(gains, chan_params)
    core = lax.axis_index("seq") % 2
    padding = jnp.zeros((share, 2 * HALVES["mix"] - mix_cols - GROUP), BF16)
    halves = ([], [])
    for l in range(depth):
        mix = jnp.concatenate([w_mix[l], padding, small if l == 0 else jnp.zeros_like(small)], axis=1)
        for h in range(2):
            for w, size in ((mix, HALVES["mix"]), (w_out[l], HALVES["out"]), (w_up[l], HALVES["up"])):
                halves[h].append(w[:, h * size : (h + 1) * size])
    halves = [jnp.concatenate(half, axis=1) for half in halves]
    mine = jnp.where(core == 0, halves[0], halves[1])
    other = swap(jnp.where(core == 0, halves[1], halves[0]), (1, 1))
    units = jnp.where(core == 0, jnp.concatenate([mine, other]), jnp.concatenate([other, mine]))
    joint = HALVES["mix"] + HALVES["out"]
    size = joint + HALVES["up"]
    mos, uds = [], []
    for l in range(depth):
        unit = units[:, l * size : (l + 1) * size]
        stages = LATER if l else STAGES
        mos.append(Spread(unit[:, :joint], stages))
        uds.append(Spread(jnp.concatenate([unit[:, joint:], w_down[l]], axis=1), stages))
    plan = {
        "mix": (0, HALVES["mix"]),
        "out": (HALVES["mix"], HALVES["out"]),
        "small": (HALVES["mix"] - GROUP, GROUP),
        "up": (0, HALVES["up"]),
        "down": (HALVES["up"], width),
    }
    plans = [dict(plan, sources=mo.sources()) for mo in mos]

    order = Order()
    mo, ud = mos[0], uds[0]
    later = [move for l in range(1, depth) for move in (mos[l], uds[l])]
    order.pass_on(ud, mo, *later)
    order.join(ud, mo, *later)
    order.pass_on(mo, ud, *later)
    order.join(mo, ud)
    order.pass_on(mo, ud)
    order.join(mo, *later[:1])
    order.pass_on(mo, *later[:1])
    mo.near_core()
    order.join(ud, *later[1:2])
    if later:
        order.pass_on(*later[1:2])
    order.join(mo, *later[:1])
    mo.end()
    order.pass_on(ud)
    ud.near_core()
    x = stream
    saved = []
    params = None
    for l in range(depth):
        mo, ud, plan = mos[l], uds[l], plans[l]
        more = l + 1 < depth
        order.join(cores=(mo,))
        if l == 0:
            params = table_of(plan, info, mo.arrays(), depth, width)
        (layer,) = order.step(params[l])
        head = front(plan, info, x, layer, mo.arrays())
        (total,) = order.step(head[-1])
        if more:
            order.join(ud, uds[l + 1])
        else:
            order.join(ud)
        ud.end()
        every = exchange(order.step(total)[0])
        (every,) = order.step(every)
        if more:
            order.pass_on(mos[l + 1])
            mos[l + 1].near_core()
        middle = mid(plan, info, x, layer, head[2], head[4], head[5], head[6], order.step(every)[0], mo.arrays())
        middle = (*middle[:-1], *order.step(middle[-1]))
        if more:
            order.join(mos[l + 1], cores=(ud,))
            mos[l + 1].end()
            order.pass_on(uds[l + 1])
            uds[l + 1].near_core()
        else:
            order.join(cores=(ud,))
        if more:
            tail = ffn(plan, info, middle[5], middle[6], ud.arrays(), F32)
            saved.append((x, every, head, middle, tail, layer))
            (x,) = order.step(tail[-1])
    later_stages = UPPER if depth > 1 else (STAGES,) * 3
    keep, send, mixed, hidden, dlow, dafter, dmid, ffn_gain = turn(
        plan, rels_of(later_stages[0]), info, cotangent, layer, middle[5], middle[6], ud.arrays()
    )
    saved.append((x, every, head, middle, (None, hidden, None), layer))
    above = None
    sums = [None] * depth
    extra = ()
    for l in reversed(range(depth)):
        x, every, (normed, cpre, gate, rate, kept, feed, sub, _), middle, (both, hidden, _), layer = saved[l]
        states, first, gn, rg, gated, after, lifted = middle
        plan = plans[l]
        u_stages, od_stages, c_stages = UPPER if l else LOWER
        if above:
            (dx,) = order.step(dx)
            keep, send, dlow, dafter, dmid, ffn_gain = back_ffn(
                plan, info, dx, layer, both, after, uds[l].arrays(), rels_of(u_stages), (lifted,)
            )
        (keep,) = order.step(keep)
        u = Reduce(keep, send, u_stages)
        if above:
            u_up, od_up, c_up = above
            order.join(od_up, c_up, u_up)
            od_up.ready()
            order.pass_on(c_up, u_up)
        (dmid,) = order.step(dmid)
        dgpre, dstates, mid_gain, rsub, rtotal = back_mid(
            plan, info, dmid, layer, gn, rg, gate, states, kept, sub, mos[l].arrays()
        )
        (rtotal,) = order.step(rtotal)
        order.join(u, *((c_up, u_up) if above else ()))
        revery = exchange(rtotal, order)
        waiting = [u] + ([od_up, c_up, u_up] if above else [])
        for move in waiting:
            move.ready()
        (dlow,) = order.step(dlow)
        od = Reduce(
            *grad_od(rels_of(od_stages), info, gated, dmid, hidden, dlow, normed, dgpre), od_stages
        )
        (od.held,) = order.step(od.held)
        (revery,) = order.step(revery)
        order.pass_on(*waiting)
        (dstates,) = order.step(dstates)
        more = (normed,)
        if l == 0:
            more = (normed, mid_gain, ffn_gain, *extra)
        keep, send, dx, gains_b = back_two(
            plan, info, x, layer, dafter, dgpre, dstates, states, kept, rate, cpre, first, sub, rsub, every, revery,
            mos[l].arrays(), rels_of(c_stages), more,
        )
        extra = (gains_b, mid_gain, ffn_gain) + extra
        (keep,) = order.step(keep)
        c = Reduce(keep, send, c_stages)
        order.join(*waiting, od)
        order.pass_on(od, u, *((od_up, c_up) if above else ()))
        above = sums[l] = (u, od, c)
    u, od, c = sums[0]
    others = ()
    if depth > 1:
        u_up, od_up, c_up = sums[1]
        others = (od_up, c_up)
    for moves in ((c,), (od, *others), (u,), (c,), (od,), (u,), (c,), (od,), (c,)):
        order.join(*moves)
        order.pass_on(*moves)
    mine, other, downs = [], [], []
    for u, od, c in reversed(sums):
        ready = od.add()
        line = jnp.concatenate([c.add(), ready[:, : HALVES["out"] + HALVES["gate"]], u.add()], axis=1)
        first, second = line[:share], line[share:]
        mine.insert(0, jnp.where(core == 0, first, second))
        other.insert(0, swap(jnp.where(core == 0, second, first), (1, 1)))
        downs.insert(0, ready)
    shapes = (w_mix.shape, w_out.shape, w_up.shape, w_down.shape)
    *grads, tail = finish(info, mine, other, downs, shapes)
    tail = tail[:, : 4 * depth].T.reshape(depth, 4, share)
    return (mixed, dx, *grads, tail[:, :3], tail[:, 3])


def body(stream, w_mix, *others):
    n_dp, n_seq = lax.axis_size("dp"), lax.axis_size("seq")
    fast = n_seq == 8 and n_dp == 4 and 2 * w_mix.shape[1] == UNIT and w_mix.shape[0] == 2
    return (fast_body if fast else plain_body)(stream, w_mix, *others)


def solution(mesh):
    placed = (
        P(ALL, None),
        P(None, ALL, None),
        P(None, ALL, None),
        P(None, ALL, None),
        P(None, ALL, None),
        P(None, None, ALL),
        P(None, ALL),
        P("dp", None),
        P(ALL, None),
    )
    return jax.shard_map(
        body,
        mesh=mesh,
        in_specs=placed,
        out_specs=(
            P(ALL, None),
            P(ALL, None),
            P(None, ALL, None),
            P(None, ALL, None),
            P(None, ALL, None),
            P(None, ALL, None),
            P(None, None, ALL),
            P(None, ALL),
        ),
        check_vma=False,
    )
```

```python
import functools

import jax
import jax.numpy as jnp
from jax import lax
from jax.experimental import pallas as pl
from jax.experimental.pallas import tpu as pltpu
from jax.sharding import PartitionSpec as P

GROUP = 128
EPS = 1e-06
SUB = 8
UNIT = 48
HALVES = {"mix": 1024, "out": 384, "up": 1536, "gate": 384, "cell": 640}
ROWS = 256
F32 = jnp.float32
BF16 = jnp.bfloat16
ALL = ("dp", "seq")
VMEM = pl.BlockSpec(memory_space=pltpu.VMEM)
SMEM = pl.BlockSpec(memory_space=pltpu.SMEM)
ANY = pl.BlockSpec(memory_space=pl.ANY)
COST = pl.CostEstimate(flops=1000, bytes_accessed=1000, transcendentals=0)


def sds(shape, dtype=F32):
    return jax.ShapeDtypeStruct(shape, dtype)


def over_rows(total, body):
    for i in range(total // ROWS):
        body(pl.ds(i * ROWS, ROWS))


def dot(left, right):
    return jnp.dot(left, right, preferred_element_type=F32)


def dot_t(left, right):
    return lax.dot_general(left, right, (((1,), (1,)), ((), ())), preferred_element_type=F32)


def cmul(ar, ai, br, bi):
    return ar * br - ai * bi, ar * bi + ai * br


def power(cos, sin, times):
    while times > 1:
        cos, sin = cos * cos - sin * sin, 2.0 * cos * sin
        times //= 2
    return cos, sin


def turns(p_ref, half):
    cos, sin = p_ref[3:4, half:], p_ref[4:5, :half]
    return tuple(
        [jnp.broadcast_to(part[:, t * GROUP : (t + 1) * GROUP], (SUB, GROUP)) for t in range(half // GROUP)]
        for part in (cos, sin)
    )


def parts(ref, k, tiles):
    return [ref[k, :, t * GROUP : (t + 1) * GROUP] for t in range(tiles)]


def mix_width(plan, width):
    return 2 * width + width // 2 if plan is None else 2 * HALVES["mix"]


def load_start(pairs, sem):
    for source, target in pairs:
        pltpu.make_async_copy(source, target, sem).start()


def load_wait(pairs, sem):
    for source, target in pairs:
        pltpu.make_async_copy(source, target, sem).wait()


def pairs_of(plan, sources, me_ref, name, target):
    if plan is None:
        return [(sources[{"mix": 0, "out": 1, "up": 2, "down": 3}[name]], target)]
    chip, core = me_ref[1], me_ref[2]
    column, columns = plan[name]
    pairs = []
    for source, (other_core, rels) in enumerate(plan["sources"]):
        half = core ^ other_core
        for b, (zero, one) in enumerate(zip(*rels)):
            block = chip ^ (zero + half * (one - zero))
            if name == "down":
                row, left = block * (2 * UNIT) + half * UNIT, 0
            elif name == "small":
                row, left = block * UNIT, half * GROUP
            else:
                row, left = block * UNIT, half * HALVES[name]
            to = target.at[pl.ds(pl.multiple_of(row, UNIT), UNIT), pl.ds(pl.multiple_of(left, GROUP), columns)]
            pairs.append((sources[source].at[b, :, pl.ds(column, columns)], to))
    return pairs


def front_kernel(
    plan, count, me_ref, x_ref, p_ref, *refs
):
    w_hbm, refs = refs[:count], refs[count:]
    (
    normed_ref, cpre_ref, gate_ref, rate_ref, kept_ref, feed_ref, sub_ref, total_ref,
    w_ref, sem,
    ) = refs
    rows, width = x_ref.shape
    half = width // 2
    block = rows // SUB
    pairs = pairs_of(plan, w_hbm, me_ref, "mix", w_ref)
    load_start(pairs, sem)

    def norm(r):
        x = x_ref[r, :].astype(F32)
        scale = lax.rsqrt(jnp.mean(x * x, axis=1, keepdims=True) + EPS)
        normed_ref[r, :] = (x * scale * p_ref[0:1, :]).astype(BF16)

    over_rows(rows, norm)
    load_wait(pairs, sem)
    normed = normed_ref[...]
    rate = jax.nn.sigmoid(dot(normed, w_ref[:, 2 * width : 2 * width + half]) + p_ref[3:4, :half])
    rate_ref[...] = rate
    at = lax.broadcasted_iota(jnp.int32, (rows, GROUP), 0)
    fresh = at == me_ref[5]
    for j in range(6, me_ref.shape[0]):
        fresh = jnp.logical_or(fresh, at == me_ref[j])
    tiles = half // GROUP
    for t in range(tiles):
        kept_ref[t] = jnp.where(fresh, 0.0, rate[:, t * GROUP : (t + 1) * GROUP])
    for k in range(2):
        cols = slice(k * half, (k + 1) * half)
        pre = dot(normed, w_ref[:, cols])
        cpre_ref[:, cols] = pre
        feed = (1.0 - rate_ref[...]) * (pre * jax.nn.sigmoid(pre))
        for t in range(tiles):
            feed_ref[k * tiles + t] = feed[:, t * GROUP : (t + 1) * GROUP]
    cos, sin = turns(p_ref, half)

    mag = [jnp.ones((SUB, GROUP), F32)] * tiles
    br = [jnp.zeros((SUB, GROUP), F32)] * tiles
    bi = [jnp.zeros((SUB, GROUP), F32)] * tiles
    for j in range(block):
        at = pl.ds(j, SUB, stride=block)
        for t in range(tiles):
            kept = kept_ref[t, at, :]
            tr, ti = cmul(cos[t], sin[t], br[t], bi[t])
            br[t] = kept * tr + feed_ref[t, at, :]
            bi[t] = kept * ti + feed_ref[tiles + t, at, :]
            mag[t] = mag[t] * kept
    mag, br, bi = (jnp.concatenate(part, axis=1) for part in (mag, br, bi))
    far_cos, far_sin = power(jnp.concatenate(cos, axis=1), jnp.concatenate(sin, axis=1), block)
    ar, ai = mag * far_cos, mag * far_sin
    sub_ref[0] = ar
    sub_ref[1] = ai
    sub_ref[2] = br
    sub_ref[3] = bi
    one_r, one_i, sum_r, sum_i = (part[0:1] for part in (ar, ai, br, bi))
    for k in range(1, SUB):
        kr, ki = ar[k : k + 1], ai[k : k + 1]
        one_r, one_i = cmul(kr, ki, one_r, one_i)
        sum_r, sum_i = cmul(kr, ki, sum_r, sum_i)
        sum_r = sum_r + br[k : k + 1]
        sum_i = sum_i + bi[k : k + 1]
    total_ref[0:1, :] = one_r
    total_ref[1:2, :] = one_i
    total_ref[2:3, :] = sum_r
    total_ref[3:4, :] = sum_i
    for k in range(2):
        cols = slice(width + k * half, width + (k + 1) * half)
        gate_ref[:, k * half : (k + 1) * half] = jax.nn.sigmoid(dot(normed, w_ref[:, cols]))


def front(plan, me, x, params, weights):
    rows, width = x.shape
    half = width // 2
    return pl.pallas_call(
        functools.partial(front_kernel, plan, len(weights)),
        out_shape=(
            sds((rows, width), BF16),
            sds((rows, width)),
            sds((rows, width)),
            sds((rows, half)),
            sds((half // GROUP, rows, GROUP)),
            sds((width // GROUP, rows, GROUP)),
            sds((4, SUB, half)),
            sds((4, half)),
        ),
        in_specs=[SMEM, VMEM, VMEM] + [ANY] * len(weights),
        out_specs=(VMEM,) * 8,
        scratch_shapes=[pltpu.VMEM((width, mix_width(plan, width)), BF16), pltpu.SemaphoreType.DMA],
        compiler_params=pltpu.CompilerParams(vmem_limit_bytes=12 << 20),
        cost_estimate=COST,
        name="front",
    )(me, x, params, *weights)


def mid_kernel(plan, count, me_ref, x_ref, p_ref, gate_ref, kept_ref, feed_ref, sub_ref, every_ref, *refs):
    w_hbm, refs = refs[:count], refs[count:]
    states_ref, first_ref, gn_ref, rg_ref, gated_ref, after_ref, lifted_ref, out_ref, sem = refs
    rows, width = x_ref.shape
    half = width // 2
    block = rows // SUB
    pairs = pairs_of(plan, w_hbm, me_ref, "out", out_ref)
    load_start(pairs, sem)

    sr = jnp.zeros((1, half), F32)
    si = jnp.zeros((1, half), F32)
    for k in range(every_ref.shape[0]):
        at = k ^ me_ref[3]
        nr, ni = cmul(every_ref[at, 0:1, :], every_ref[at, 1:2, :], sr, si)
        earlier = k < me_ref[0]
        sr = jnp.where(earlier, nr + every_ref[at, 2:3, :], sr)
        si = jnp.where(earlier, ni + every_ref[at, 3:4, :], si)
    for k in range(SUB):
        first_ref[0, k : k + 1, :] = sr
        first_ref[1, k : k + 1, :] = si
        nr, ni = cmul(sub_ref[0, k : k + 1, :], sub_ref[1, k : k + 1, :], sr, si)
        sr = nr + sub_ref[2, k : k + 1, :]
        si = ni + sub_ref[3, k : k + 1, :]
    cos, sin = turns(p_ref, half)
    tiles = half // GROUP
    sr = parts(first_ref, 0, tiles)
    si = parts(first_ref, 1, tiles)
    for j in range(block):
        at = pl.ds(j, SUB, stride=block)
        for t in range(tiles):
            kept = kept_ref[t, at, :]
            tr, ti = cmul(cos[t], sin[t], sr[t], si[t])
            sr[t] = kept * tr + feed_ref[t, at, :]
            si[t] = kept * ti + feed_ref[tiles + t, at, :]
            states_ref[t, at, :] = sr[t]
            states_ref[tiles + t, at, :] = si[t]

    lane = lax.broadcasted_iota(jnp.int32, (ROWS, GROUP), 1)

    def group_norm(r):
        held = jnp.zeros((ROWS, GROUP), F32)
        for g in range(width // GROUP):
            cols = slice(g * GROUP, (g + 1) * GROUP)
            v = gate_ref[r, cols] * states_ref[g, r, :]
            centre = v - jnp.mean(v, axis=1, keepdims=True)
            scale = lax.rsqrt(jnp.mean(centre * centre, axis=1, keepdims=True) + EPS)
            gn = centre * scale
            gn_ref[r, cols] = gn
            gated_ref[r, cols] = (gn * p_ref[1:2, cols]).astype(BF16)
            held = jnp.where(lane == g, scale, held)
        rg_ref[r, :] = held

    over_rows(rows, group_norm)
    load_wait(pairs, sem)
    after_ref[...] = x_ref[...].astype(F32) + dot(gated_ref[...], out_ref[...])

    def norm(r):
        after = after_ref[r, :]
        scale = lax.rsqrt(jnp.mean(after * after, axis=1, keepdims=True) + EPS)
        lifted_ref[r, :] = (after * scale * p_ref[2:3, :]).astype(BF16)

    over_rows(rows, norm)


def mid(plan, me, x, params, gate, kept, feed, sub, every, weights):
    rows, width = x.shape
    half = width // 2
    return pl.pallas_call(
        functools.partial(mid_kernel, plan, len(weights)),
        out_shape=(
            sds((width // GROUP, rows, GROUP)),
            sds((2, SUB, half)),
            sds((rows, width)),
            sds((rows, GROUP)),
            sds((rows, width), BF16),
            sds((rows, width)),
            sds((rows, width), BF16),
        ),
        in_specs=[SMEM] + [VMEM] * 7 + [ANY] * len(weights),
        out_specs=(VMEM,) * 7,
        scratch_shapes=[pltpu.VMEM((width, width), BF16), pltpu.SemaphoreType.DMA],
        compiler_params=pltpu.CompilerParams(vmem_limit_bytes=12 << 20),
        cost_estimate=COST,
        name="mid",
    )(me, x, params, gate, kept, feed, sub, every, *weights)


def ffn_kernel(plan, count, me_ref, after_ref, lifted_ref, *refs):
    w_hbm, refs = refs[:count], refs[count:]
    both_ref, hidden_ref, next_ref, up_ref, down_ref, sems = refs
    inner = hidden_ref.shape[1]
    up_pairs = pairs_of(plan, w_hbm, me_ref, "up", up_ref)
    down_pairs = pairs_of(plan, w_hbm, me_ref, "down", down_ref)
    load_start(up_pairs, sems.at[0])
    load_start(down_pairs, sems.at[1])
    load_wait(up_pairs, sems.at[0])
    lifted = lifted_ref[...]
    step = after_ref.shape[1] // 2
    for k in range(inner // step):
        cols = slice(k * step, (k + 1) * step)
        more = slice(inner + k * step, inner + (k + 1) * step)
        a = dot(lifted, up_ref[:, cols])
        b = dot(lifted, up_ref[:, more])
        both_ref[:, cols] = a
        both_ref[:, more] = b
        hidden_ref[:, cols] = (a * jax.nn.sigmoid(a) * b).astype(BF16)
    load_wait(down_pairs, sems.at[1])
    next_ref[...] = (after_ref[...] + dot(hidden_ref[...], down_ref[...])).astype(next_ref.dtype)


def ffn(plan, me, after, lifted, weights, dtype):
    rows, width = after.shape
    inner = 2 * width
    return pl.pallas_call(
        functools.partial(ffn_kernel, plan, len(weights)),
        out_shape=(sds((rows, 2 * inner)), sds((rows, inner), BF16), sds((rows, width), dtype)),
        in_specs=[SMEM] + [VMEM] * 2 + [ANY] * len(weights),
        out_specs=(VMEM,) * 3,
        scratch_shapes=[
            pltpu.VMEM((width, 2 * inner), BF16),
            pltpu.VMEM((inner, width), BF16),
            pltpu.SemaphoreType.DMA((2,)),
        ],
        compiler_params=pltpu.CompilerParams(vmem_limit_bytes=17 << 20),
        cost_estimate=COST,
        name="ffn",
    )(me, after, lifted, *weights)


def lower(me_ref, dx_ref, dlow_ref):
    rows, width = dx_ref.shape
    if dx_ref.dtype == BF16:
        at = lax.broadcasted_iota(jnp.int32, (rows, GROUP), 0)
        live = at < me_ref[4]
        for t in range(width // GROUP):
            cols = slice(t * GROUP, (t + 1) * GROUP)
            dlow_ref[:, cols] = jnp.where(live, dx_ref[:, cols].astype(F32), 0.0).astype(BF16)
        return dlow_ref
    dlow_ref[...] = dx_ref[...].astype(BF16)
    return dx_ref


def lift_back(grad_ref, p_ref, after_ref, work_ref, dafter_ref, dmid_ref, gain_ref):
    def norm_back(r):
        after = after_ref[r, :]
        scale = lax.rsqrt(jnp.mean(after * after, axis=1, keepdims=True) + EPS)
        normal = after * scale
        lift = work_ref[r, :]
        e = lift * p_ref[2:3, :]
        d = grad_ref[r, :].astype(F32) + scale * (e - normal * jnp.mean(e * normal, axis=1, keepdims=True))
        dafter_ref[r, :] = d
        dmid_ref[r, :] = d.astype(BF16)
        work_ref[r, :] = lift * normal

    over_rows(after_ref.shape[0], norm_back)
    gain_ref[...] = jnp.sum(work_ref[...], axis=0, keepdims=True)


def back_ffn_kernel(plan, count, rels, me_ref, dx_ref, p_ref, both_ref, after_ref, *refs):
    w_hbm, refs = refs[:count], refs[count:]
    if rels is not None:
        lifted_ref, keep_ref, send_ref, *refs, dboth_ref, grad_up_ref, out_sem = refs
        dlow_ref, *refs = refs
    else:
        dlow_ref, dboth_ref, *refs = refs
    dafter_ref, dmid_ref, gain_ref, work_ref, up_ref, down_ref, sems = refs
    rows, width = dx_ref.shape
    inner = down_ref.shape[0]
    up_pairs = pairs_of(plan, w_hbm, me_ref, "up", up_ref)
    down_pairs = pairs_of(plan, w_hbm, me_ref, "down", down_ref)
    load_start(down_pairs, sems.at[1])
    load_start(up_pairs, sems.at[0])
    grad_ref = lower(me_ref, dx_ref, dlow_ref)
    dlow = dlow_ref[...]
    load_wait(down_pairs, sems.at[1])
    step = width // 2
    for k in range(inner // step):
        cols = slice(k * step, (k + 1) * step)
        more = slice(inner + k * step, inner + (k + 1) * step)
        dh = dot_t(dlow, down_ref[cols, :])
        a = both_ref[:, cols]
        sig = jax.nn.sigmoid(a)
        dboth_ref[:, cols] = (dh * both_ref[:, more] * (sig * (1.0 + a * (1.0 - sig)))).astype(BF16)
        dboth_ref[:, more] = (dh * (a * sig)).astype(BF16)
    if rels is not None:
        products(lifted_ref[...], dboth_ref, grad_up_ref, grad_up_ref.shape[1])
        pairs = export(me_ref, rels, "up", grad_up_ref, 0, HALVES["up"], keep_ref, send_ref, out_sem)
    load_wait(up_pairs, sems.at[0])
    work_ref[...] = dot_t(dboth_ref[...], up_ref[...])

    lift_back(grad_ref, p_ref, after_ref, work_ref, dafter_ref, dmid_ref, gain_ref)
    if rels is not None:
        load_wait(pairs, out_sem)


def turn_kernel(plan, count, rels, me_ref, dx_ref, p_ref, after_ref, lifted_ref, *refs):
    w_hbm, refs = refs[:count], refs[count:]
    (
        keep_ref, send_ref, next_ref, hidden_ref, dlow_ref, dafter_ref, dmid_ref, gain_ref,
        dboth_ref, grad_up_ref, work_ref, up_ref, down_ref, sems, out_sem,
    ) = refs
    width = dx_ref.shape[1]
    inner = down_ref.shape[0]
    up_pairs = pairs_of(plan, w_hbm, me_ref, "up", up_ref)
    down_pairs = pairs_of(plan, w_hbm, me_ref, "down", down_ref)
    load_start(up_pairs, sems.at[0])
    load_start(down_pairs, sems.at[1])
    grad_ref = lower(me_ref, dx_ref, dlow_ref)
    dlow = dlow_ref[...]
    lifted = lifted_ref[...]
    load_wait(up_pairs, sems.at[0])
    load_wait(down_pairs, sems.at[1])
    step = width
    for k in range(inner // step):
        cols = slice(k * step, (k + 1) * step)
        more = slice(inner + k * step, inner + (k + 1) * step)
        a = dot(lifted, up_ref[:, cols])
        b = dot(lifted, up_ref[:, more])
        dh = dot_t(dlow, down_ref[cols, :])
        sig = jax.nn.sigmoid(a)
        gated = a * sig
        hidden_ref[:, cols] = (gated * b).astype(BF16)
        dboth_ref[:, cols] = (dh * b * (sig * (1.0 + a * (1.0 - sig)))).astype(BF16)
        dboth_ref[:, more] = (dh * gated).astype(BF16)
    products(lifted, dboth_ref, grad_up_ref, grad_up_ref.shape[1])
    pairs = export(me_ref, rels, "up", grad_up_ref, 0, HALVES["up"], keep_ref, send_ref, out_sem)
    work_ref[...] = dot_t(dboth_ref[...], up_ref[...])
    lift_back(grad_ref, p_ref, after_ref, work_ref, dafter_ref, dmid_ref, gain_ref)
    next_ref[...] = (after_ref[...] + dot(hidden_ref[...], down_ref[...])).astype(next_ref.dtype)
    load_wait(pairs, out_sem)


def turn(plan, rels, me, dx, params, after, lifted, weights):
    rows, width = dx.shape
    inner = 2 * width
    block = sds((2 ** len(STAGES), UNIT, HALVES["up"]), BF16)
    low = sds((rows, width), BF16)
    return pl.pallas_call(
        functools.partial(turn_kernel, plan, len(weights), rels),
        out_shape=(block, block, low, sds((rows, inner), BF16), low, sds((rows, width)), low, sds((1, width))),
        in_specs=[SMEM] + [VMEM] * 4 + [ANY] * len(weights),
        out_specs=(ANY, ANY) + (VMEM,) * 6,
        scratch_shapes=[
            pltpu.VMEM((rows, 2 * inner), BF16),
            pltpu.VMEM((width, 2 * inner), BF16),
            pltpu.VMEM((rows, width), F32),
            pltpu.VMEM((width, 2 * inner), BF16),
            pltpu.VMEM((inner, width), BF16),
            pltpu.SemaphoreType.DMA((2,)),
            pltpu.SemaphoreType.DMA,
        ],
        compiler_params=pltpu.CompilerParams(vmem_limit_bytes=22 << 20),
        cost_estimate=COST,
        name="turn",
    )(me, dx, params, after, lifted, *weights)


def back_ffn(plan, me, dx, params, both, after, weights, rels=None, lifted=()):
    rows, width = dx.shape
    inner = 2 * width
    block = sds((2 ** len(STAGES), UNIT, HALVES["up"]), BF16)
    dboth = (rows, 2 * inner)
    outs = (sds((rows, width), BF16), sds(dboth, BF16), sds((rows, width)), sds((rows, width), BF16), sds((1, width)))
    specs, more = (VMEM,) * 5, []
    if rels is not None:
        outs, specs = (block, block, outs[0], *outs[2:]), (ANY, ANY, *specs[1:])
        more = [pltpu.VMEM(dboth, BF16), pltpu.VMEM((width, 2 * inner), BF16), pltpu.SemaphoreType.DMA]
    return pl.pallas_call(
        functools.partial(back_ffn_kernel, plan, len(weights), rels),
        out_shape=outs,
        in_specs=[SMEM] + [VMEM] * 4 + [ANY] * len(weights) + [VMEM] * len(lifted),
        out_specs=specs,
        scratch_shapes=[
            pltpu.VMEM((rows, width), F32),
            pltpu.VMEM((width, 2 * inner), BF16),
            pltpu.VMEM((inner, width), BF16),
            pltpu.SemaphoreType.DMA((2,)),
        ]
        + more,
        compiler_params=pltpu.CompilerParams(vmem_limit_bytes=25 << 20),
        cost_estimate=COST,
        name="back_ffn",
    )(me, dx, params, both, after, *weights, *lifted)


def back_mid_kernel(
    plan, count, me_ref, dmid_ref, p_ref, gn_ref, rg_ref, gate_ref, states_ref, kept_ref, sub_ref, *refs
):
    w_hbm, refs = refs[:count], refs[count:]
    dgpre_ref, dstates_ref, gain_ref, rsub_ref, rtotal_ref, work_ref, out_ref, sem = refs
    rows, width = dmid_ref.shape
    half = width // 2
    block = rows // SUB
    pairs = pairs_of(plan, w_hbm, me_ref, "out", out_ref)
    load_start(pairs, sem)
    load_wait(pairs, sem)
    work_ref[...] = dot_t(dmid_ref[...], out_ref[...])

    def group_back(r):
        held = rg_ref[r, :]
        for g in range(width // GROUP):
            cols = slice(g * GROUP, (g + 1) * GROUP)
            gn = gn_ref[r, cols]
            dg = work_ref[r, cols]
            e = dg * p_ref[1:2, cols]
            dv = held[:, g : g + 1] * (
                e - jnp.mean(e, axis=1, keepdims=True) - gn * jnp.mean(e * gn, axis=1, keepdims=True)
            )
            gate = gate_ref[r, cols]
            dgpre_ref[r, cols] = (dv * states_ref[g, r, :] * gate * (1.0 - gate)).astype(BF16)
            dstates_ref[g, r, :] = dv * gate
            work_ref[r, cols] = dg * gn

    over_rows(rows, group_back)
    gain_ref[...] = jnp.sum(work_ref[...], axis=0, keepdims=True)

    cos, sin = turns(p_ref, half)
    tiles = half // GROUP
    zr = [jnp.zeros((SUB, GROUP), F32)] * tiles
    zi = [jnp.zeros((SUB, GROUP), F32)] * tiles
    for j in reversed(range(block)):
        at = pl.ds(j, SUB, stride=block)
        for t in range(tiles):
            kept = kept_ref[t, at, :]
            qr = dstates_ref[t, at, :] + zr[t]
            qi = dstates_ref[tiles + t, at, :] + zi[t]
            zr[t] = kept * (cos[t] * qr + sin[t] * qi)
            zi[t] = kept * (cos[t] * qi - sin[t] * qr)
    zr, zi = jnp.concatenate(zr, axis=1), jnp.concatenate(zi, axis=1)
    rsub_ref[0] = zr
    rsub_ref[1] = zi
    tr = jnp.zeros((1, half), F32)
    ti = jnp.zeros((1, half), F32)
    for k in reversed(range(SUB)):
        ar, ai = sub_ref[0, k : k + 1, :], sub_ref[1, k : k + 1, :]
        tr, ti = ar * tr + ai * ti + zr[k : k + 1], ar * ti - ai * tr + zi[k : k + 1]
    rtotal_ref[0:1, :] = tr
    rtotal_ref[1:2, :] = ti


def back_mid(plan, me, dmid, params, gn, rg, gate, states, kept, sub, weights):
    rows, width = dmid.shape
    half = width // 2
    return pl.pallas_call(
        functools.partial(back_mid_kernel, plan, len(weights)),
        out_shape=(
            sds((rows, width), BF16),
            sds((width // GROUP, rows, GROUP)),
            sds((1, width)),
            sds((2, SUB, half)),
            sds((2, half)),
        ),
        in_specs=[SMEM] + [VMEM] * 8 + [ANY] * len(weights),
        out_specs=(VMEM,) * 5,
        scratch_shapes=[
            pltpu.VMEM((rows, width), F32),
            pltpu.VMEM((width, width), BF16),
            pltpu.SemaphoreType.DMA,
        ],
        compiler_params=pltpu.CompilerParams(vmem_limit_bytes=11 << 20),
        cost_estimate=COST,
        name="back_mid",
    )(me, dmid, params, gn, rg, gate, states, kept, sub, *weights)


def back_two_kernel(
    plan, count, rels, spare, me_ref, x_ref, p_ref, dafter_ref, dgpre_ref, dstates_ref, states_ref, kept_ref, rate_ref, cpre_ref,
    first_ref, sub_ref, rsub_ref, every_ref, revery_ref, *refs
):
    w_hbm, extra, refs = refs[:count], refs[count : count + spare], refs[count + spare :]
    if rels is not None:
        normed_ref, *extra = extra
        keep_ref, send_ref, dx_ref, gains_ref, *refs, mix_ref, held_ref, out_sem = refs
        dmixin_ref, *refs = refs
    else:
        dmixin_ref, dx_ref, gains_ref, *refs = refs
    work_ref, q_ref, turn_ref, start_ref, w_ref, sem = refs
    rows, width = x_ref.shape
    half = width // 2
    block = rows // SUB
    pairs = pairs_of(plan, w_hbm, me_ref, "mix", w_ref)
    load_start(pairs, sem)
    zr = jnp.zeros((1, half), F32)
    zi = jnp.zeros((1, half), F32)
    for k in reversed(range(every_ref.shape[0])):
        at = k ^ me_ref[3]
        ar, ai = every_ref[at, 0:1, :], every_ref[at, 1:2, :]
        later = k > me_ref[0]
        nr = ar * zr + ai * zi + revery_ref[at, 0:1, :]
        ni = ar * zi - ai * zr + revery_ref[at, 1:2, :]
        zr = jnp.where(later, nr, zr)
        zi = jnp.where(later, ni, zi)
    for k in reversed(range(SUB)):
        start_ref[0, k : k + 1, :] = zr
        start_ref[1, k : k + 1, :] = zi
        ar, ai = sub_ref[0, k : k + 1, :], sub_ref[1, k : k + 1, :]
        zr, zi = (
            ar * zr + ai * zi + rsub_ref[0, k : k + 1, :],
            ar * zi - ai * zr + rsub_ref[1, k : k + 1, :],
        )
    cos, sin = turns(p_ref, half)
    tiles = half // GROUP
    zr = parts(start_ref, 0, tiles)
    zi = parts(start_ref, 1, tiles)
    angle = [jnp.zeros((SUB, GROUP), F32)] * tiles
    for j in reversed(range(block)):
        at = pl.ds(j, SUB, stride=block)
        before = pl.ds(max(j - 1, 0), SUB, stride=block)
        for t in range(tiles):
            kept = kept_ref[t, at, :]
            qr = dstates_ref[t, at, :] + zr[t]
            qi = dstates_ref[tiles + t, at, :] + zi[t]
            q_ref[t, at, :] = qr
            q_ref[tiles + t, at, :] = qi
            zr[t] = kept * (cos[t] * qr + sin[t] * qi)
            zi[t] = kept * (cos[t] * qi - sin[t] * qr)
            if j:
                sr, si = states_ref[t, before, :], states_ref[tiles + t, before, :]
            else:
                sr, si = (first_ref[k, :, t * GROUP : (t + 1) * GROUP] for k in range(2))
            turn_ref[t, at, :] = zr[t] * sr + zi[t] * si
            angle[t] = angle[t] + (zi[t] * sr - zr[t] * si)
    gains_ref[1:2, half:] = jnp.sum(jnp.concatenate(angle, axis=1), axis=0, keepdims=True)

    def activations(r):
        for t in range(tiles):
            rate = rate_ref[r, t * GROUP : (t + 1) * GROUP]
            left = 1.0 - rate
            meet = jnp.zeros_like(rate)
            for k in range(2):
                cols = slice((k * tiles + t) * GROUP, (k * tiles + t + 1) * GROUP)
                pre = cpre_ref[r, cols]
                sig = jax.nn.sigmoid(pre)
                q = q_ref[k * tiles + t, r, :]
                meet = meet + q * (pre * sig)
                dmixin_ref[r, cols] = (left * q * (sig * (1.0 + pre * (1.0 - sig)))).astype(BF16)
            dfpre = left * (turn_ref[t, r, :] - rate * meet)
            dmixin_ref[r, 2 * width + t * GROUP : 2 * width + (t + 1) * GROUP] = dfpre.astype(BF16)
            turn_ref[t, r, :] = dfpre
        dmixin_ref[r, width : 2 * width] = dgpre_ref[r, :]

    over_rows(rows, activations)
    for t in range(tiles):
        gains_ref[1:2, t * GROUP : (t + 1) * GROUP] = jnp.sum(turn_ref[t], axis=0, keepdims=True)
    load_wait(pairs, sem)
    work_ref[...] = dot_t(dmixin_ref[...], w_ref[:, : dmixin_ref.shape[1]])

    def norm_back(r):
        x = x_ref[r, :].astype(F32)
        scale = lax.rsqrt(jnp.mean(x * x, axis=1, keepdims=True) + EPS)
        normal = x * scale
        dn = work_ref[r, :]
        e = dn * p_ref[0:1, :]
        dx_ref[r, :] = dafter_ref[r, :] + scale * (e - normal * jnp.mean(e * normal, axis=1, keepdims=True))
        work_ref[r, :] = dn * normal

    over_rows(rows, norm_back)
    gains_ref[0:1, :] = jnp.sum(work_ref[...], axis=0, keepdims=True)

    if rels is None:
        return
    held_ref[...] = jnp.zeros_like(held_ref)
    for k in range(spare // 3):
        two, mid_gain, ffn_gain = (gains_ref, *extra)[3 * k : 3 * k + 3]
        held_ref[4 * k : 4 * k + 1, :] = two[0:1, :]
        held_ref[4 * k + 1 : 4 * k + 2, :] = mid_gain[...]
        held_ref[4 * k + 2 : 4 * k + 3, :] = ffn_gain[...]
        held_ref[4 * k + 3 : 4 * k + 4, :] = two[1:2, :]
    normed = normed_ref[...]
    products(normed, dmixin_ref, mix_ref, width)
    products(normed, dmixin_ref, mix_ref, half, 2 * width, width)
    mix_ref[:, width + half :] = jnp.transpose(held_ref[...]).astype(BF16)
    pairs = export(me_ref, rels, "cell", mix_ref, 0, HALVES["cell"], keep_ref, send_ref, out_sem)
    load_wait(pairs, out_sem)


def back_two(plan, me, x, params, dafter, dgpre, dstates, states, kept, rate, cpre, first, sub, rsub, every, revery, weights, rels=None, extra=()):
    rows, width = x.shape
    half = width // 2
    size = 2 * width + half
    block = sds((2 ** len(STAGES), UNIT, HALVES["cell"]), BF16)
    scratch = [
        pltpu.VMEM((rows, width), F32),
        pltpu.VMEM((width // GROUP, rows, GROUP), F32),
        pltpu.VMEM((half // GROUP, rows, GROUP), F32),
        pltpu.VMEM((2, SUB, half), F32),
        pltpu.VMEM((width, mix_width(plan, width)), BF16),
        pltpu.SemaphoreType.DMA,
    ]
    if rels is None:
        first_out, specs, more = (sds((rows, size), BF16),), (VMEM,), []
    else:
        first_out, specs = (block, block), (ANY, ANY)
        scratch.insert(0, pltpu.VMEM((rows, size), BF16))
        more = [pltpu.VMEM((width, 2 * HALVES["cell"]), BF16), pltpu.VMEM((GROUP, width), F32), pltpu.SemaphoreType.DMA]
    return pl.pallas_call(
        functools.partial(back_two_kernel, plan, len(weights), rels, len(extra)),
        out_shape=first_out + (sds((rows, width)), sds((2, width))),
        in_specs=[SMEM] + [VMEM] * 14 + [ANY] * len(weights) + [VMEM] * len(extra),
        out_specs=specs + (VMEM, VMEM),
        scratch_shapes=scratch + more,
        compiler_params=pltpu.CompilerParams(vmem_limit_bytes=18 << 20),
        cost_estimate=COST,
        name="back_two",
    )(me, x, params, dafter, dgpre, dstates, states, kept, rate, cpre, first, sub, rsub, every, revery, *weights, *extra)


def row_product(left, right):
    return lax.dot_general(left, right, (((0,), (0,)), ((), ())), preferred_element_type=F32)


def export(info_ref, rels, name, grad, column, columns, keep_ref, send_ref, sem):
    chip, core = info_ref[1], info_ref[2]
    pairs = []
    for half, target in ((1 - core, send_ref), (core, keep_ref)):
        for b, (zero, one) in enumerate(zip(*rels)):
            block = chip ^ (zero + half * (one - zero))
            if name == "down":
                row, left = block * (2 * UNIT) + half * UNIT, 0
            else:
                row, left = block * UNIT, half * HALVES[name]
            pairs.append(
                (
                    grad.at[pl.ds(pl.multiple_of(row, UNIT), UNIT), pl.ds(pl.multiple_of(left, GROUP), columns)],
                    target.at[b, :, pl.ds(column, columns)],
                )
            )
    load_start(pairs, sem)
    return pairs


def products(left, right_ref, grad_ref, size, source=0, target=0):
    step = min(size, 2 * HALVES["out"])
    for k in range(0, size, step):
        right = right_ref[:, source + k : source + k + step]
        grad_ref[:, target + k : target + k + step] = row_product(left, right).astype(BF16)


def grad_od_kernel(
    rels, info_ref, gated_ref, dmid_ref, hidden_ref, dlow_ref, normed_ref, dgpre_ref, keep_ref, send_ref,
    out_ref, gate_ref, down_ref, sem,
):
    width = dlow_ref.shape[1]
    products(hidden_ref[...], dlow_ref, down_ref, width)
    at = HALVES["out"] + HALVES["gate"]
    pairs = export(info_ref, rels, "down", down_ref, at, width, keep_ref, send_ref, sem)
    products(gated_ref[...], dmid_ref, out_ref, width)
    pairs += export(info_ref, rels, "out", out_ref, 0, HALVES["out"], keep_ref, send_ref, sem)
    products(normed_ref[...], dgpre_ref, gate_ref, width)
    pairs += export(info_ref, rels, "gate", gate_ref, HALVES["out"], HALVES["gate"], keep_ref, send_ref, sem)
    load_wait(pairs, sem)


def grad_od(rels, info, gated, dmid, hidden, dlow, normed, dgpre):
    width = dlow.shape[1]
    shape = sds((len(rels[0]), UNIT, HALVES["out"] + HALVES["gate"] + width), BF16)
    return pl.pallas_call(
        functools.partial(grad_od_kernel, rels),
        out_shape=(shape, shape),
        in_specs=[SMEM] + [VMEM] * 6,
        out_specs=(ANY, ANY),
        scratch_shapes=[
            pltpu.VMEM((width, width), BF16),
            pltpu.VMEM((width, width), BF16),
            pltpu.VMEM((hidden.shape[1], width), BF16),
            pltpu.SemaphoreType.DMA,
        ],
        compiler_params=pltpu.CompilerParams(vmem_limit_bytes=11 << 20),
        cost_estimate=COST,
        name="grad_od",
    )(info, gated, dmid, hidden, dlow, normed, dgpre)


def table_kernel(plan, count, me_ref, *refs):
    sources, (table_ref, held_ref, sem) = refs[:count], refs[count:]
    pairs = pairs_of(plan, sources, me_ref, "small", held_ref)
    load_start(pairs, sem)
    load_wait(pairs, sem)
    depth = table_ref.shape[0]
    half = table_ref.shape[2] // 2
    table = jnp.transpose(held_ref[:, GROUP:].astype(F32))
    table_ref[...] = jnp.zeros_like(table_ref)
    for l in range(depth):
        chan = table[3 * depth + l : 3 * depth + l + 1]
        table_ref[l, 0:3, :] = table[3 * l : 3 * l + 3]
        table_ref[l, 3:4, :half] = chan[:, :half]
        table_ref[l, 3:4, half:] = jnp.cos(chan[:, half:])
        table_ref[l, 4:5, :half] = jnp.sin(chan[:, half:])


def table_of(plan, me, weights, depth, width):
    return pl.pallas_call(
        functools.partial(table_kernel, plan, len(weights)),
        out_shape=sds((depth, 8, width)),
        in_specs=[SMEM] + [ANY] * len(weights),
        out_specs=VMEM,
        scratch_shapes=[pltpu.VMEM((width, 2 * GROUP), BF16), pltpu.SemaphoreType.DMA],
        compiler_params=pltpu.CompilerParams(vmem_limit_bytes=6 << 20),
        cost_estimate=COST,
        name="table",
    )(me, *weights)


def swap(x, bits):
    count = lax.axis_size("dp") * lax.axis_size("seq")
    return lax.ppermute(x, ALL, [(i, i ^ bits[i % 2]) for i in range(count)])


class Order:
    def __init__(self):
        self.last = None

    def step(self, *values):
        if self.last is not None:
            values = lax.optimization_barrier(values + (self.last,))[: len(values)]
        self.last = values[0]
        return values

    def join(self, *moves, cores=()):
        values = [move.got for move in moves]
        for move in cores:
            values += [move.last_core, move.held_core]
        values = list(self.step(*values))
        for move in moves:
            move.got = values.pop(0)
        for move in cores:
            move.last_core, move.held_core = values.pop(0), values.pop(0)


    def pass_on(self, *moves):
        for move in moves:
            move.ready()
        for move, value in zip(moves, self.step(*(move.out for move in moves))):
            move.out = value
            move.send()


def rels_of(stages):
    rels = ([0], [0])
    for bits in stages:
        for core in range(2):
            rels[core].extend([rel ^ bits[core] for rel in rels[core]])
    return rels


class Spread:
    def __init__(self, unit, stages):
        self.held, self.stages, self.at = unit[None], stages, 0
        self.got = None

    def join(self):
        if self.got is not None:
            self.held = jnp.concatenate([self.held, self.got])

    def ready(self):
        self.join()
        self.out = self.held

    def send(self):
        self.held = self.out
        one, two = self.stages[self.at]
        self.at += 1
        self.got = swap(self.held, (2 * one, 2 * two))

    def end(self):
        self.near, self.last = self.held, self.got
        self.last_core = swap(self.last, (1, 1))

    def near_core(self):
        self.held_core = swap(self.held, (1, 1))

    def arrays(self):
        return (self.near, self.held_core, self.last, self.last_core)

    def sources(self):
        rels = rels_of(self.stages)
        half = len(rels[0]) // 2
        low = tuple(tuple(rel[:half]) for rel in rels)
        high = tuple(tuple(rel[half:]) for rel in rels)
        return ((0, low), (1, low), (0, high), (1, high))


class Reduce:
    def __init__(self, keep, send, stages):
        self.held, self.stages = keep, list(stages)
        self.got = swap(send, (1, 1))

    def add(self):
        half = self.held.shape[0] // 2
        if not half:
            return self.held[0].astype(F32) + self.got[0].astype(F32)

        def joined(part):
            return (self.held[part].astype(F32) + self.got[part].astype(F32)).astype(BF16)

        self.held, self.out = joined(slice(0, half)), joined(slice(half, None))
        self.got = None

    def ready(self):
        if self.got is not None:
            self.add()

    def send(self):
        one, two = self.stages.pop()
        self.got = swap(self.out, (2 * one, 2 * two))


def exchange(x, order=None):
    other = swap(x, (1, 1))
    if order is not None:
        (other,) = order.step(other)
    pair = jnp.stack([x, other])
    got = [swap(pair, (k, k)) for k in range(2, lax.axis_size("seq"), 2)]
    return jnp.concatenate([pair] + got)


def finish_kernel(info_ref, *refs):
    depth = (len(refs) - 5) // 3
    mine, other, downs = refs[:depth], refs[depth : 2 * depth], refs[2 * depth : 3 * depth]
    mix_ref, out_ref, up_ref, down_ref, tail_ref = refs[3 * depth :]
    width = down_ref.shape[2]
    size = HALVES["cell"]

    def place(first, second):
        for l in range(depth):
            rest = width - size
            mix_ref[l, :, :size] = first[l][:, :size]
            mix_ref[l, :, size:width] = second[l][:, :rest]
            mix_ref[l, :, 2 * width :] = second[l][:, rest : size - GROUP]
            at = size
            for name, ref, begin in (("out", out_ref, 0), ("gate", mix_ref, width), ("up", up_ref, 0)):
                step = HALVES[name]
                ref[l, :, begin : begin + step] = first[l][:, at : at + step]
                ref[l, :, begin + step : begin + 2 * step] = second[l][:, at : at + step]
                at += step
        tail_ref[...] = second[0][:, size - GROUP : size]

    @pl.when(info_ref[2] == 0)
    def _():
        place(mine, other)

    @pl.when(info_ref[2] == 1)
    def _():
        place(other, mine)

    for l in range(depth):
        down_ref[l] = downs[l][:, downs[l].shape[1] - width :]


def finish(info, mine, other, downs, shapes):
    share = mine[0].shape[0]
    return pl.pallas_call(
        finish_kernel,
        out_shape=tuple(sds(shape) for shape in shapes) + (sds((share, GROUP)),),
        in_specs=[SMEM] + [VMEM] * (3 * len(mine)),
        out_specs=(VMEM,) * 5,
        compiler_params=pltpu.CompilerParams(vmem_limit_bytes=8 << 20),
        cost_estimate=COST,
        name="finish",
    )(info, *mine, *other, *downs)


def layer_params(gains, chan):
    half = chan.shape[0] // 2
    angle = chan[half:]
    rows = [
        gains[0],
        gains[1],
        gains[2],
        jnp.concatenate([chan[:half], jnp.cos(angle)]),
        jnp.concatenate([jnp.sin(angle), jnp.zeros((half,), F32)]),
    ]
    return jnp.concatenate([jnp.stack(rows), jnp.zeros((3, 2 * half), F32)], axis=0)


STAGES = ((4, 8), (8, 4), (1, 2), (2, 1))
LATER = ((1, 2), (4, 8), (8, 4), (2, 1))
UPPER = (STAGES, LATER, STAGES)
LOWER = (LATER, STAGES, STAGES)


def small_of(gains, chan_params):
    depth, _, share = gains.shape
    return jnp.concatenate(
        [gains.reshape(depth * 3, share).T, chan_params.T, jnp.zeros((share, GROUP - 4 * depth), BF16)], axis=1
    )


def info_of(lengths, rows, turned):
    where = lax.axis_index("seq")
    base = where * rows
    ends = [lengths[0, 0]]
    for j in range(1, lengths.shape[1]):
        ends.append(ends[-1] + lengths[0, j])
    chip = (lax.axis_index("dp") * lax.axis_size("seq") + where) // 2
    values = [where, chip, where % 2, where if turned else jnp.zeros_like(where), ends[-1] - base]
    values += [end - lengths[0, j] - base for j, end in enumerate(ends)]
    return jnp.stack([value.astype(jnp.int32) for value in values])


def plain_body(stream, w_mix, w_out, w_up, w_down, gains, chan_params, lengths, cotangent):
    rows, width = stream.shape
    depth = w_mix.shape[0]
    info = info_of(lengths, rows, False)
    small = small_of(gains, chan_params)
    table = lax.all_gather(small, ALL, axis=0, tiled=True)[:, : 4 * depth].T.astype(F32)
    params = [layer_params(table[3 * l : 3 * l + 3], table[3 * depth + l]) for l in range(depth)]
    weights = [
        tuple(lax.all_gather(w[l], ALL, axis=0, tiled=True) for w in (w_mix, w_out, w_up, w_down))
        for l in range(depth)
    ]
    x = stream
    saved = []
    for l in range(depth):
        head = front(None, info, x, params[l], weights[l])
        every = lax.all_gather(head[-1], "seq")
        middle = mid(None, info, x, params[l], head[2], head[4], head[5], head[6], every, weights[l])
        tail = ffn(None, info, middle[5], middle[6], weights[l], F32)
        saved.append((x, every, head, middle, tail))
        x = tail[-1]
    mixed = x.astype(BF16)
    dx = cotangent
    sums = [None] * depth
    for l in reversed(range(depth)):
        x, every, (normed, cpre, gate, rate, kept, feed, sub, _), middle, (both, hidden, _) = saved[l]
        states, first, gn, rg, gated, after, lifted = middle
        dlow, dboth, dafter, dmid, ffn_gain = back_ffn(None, info, dx, params[l], both, after, weights[l])
        dgpre, dstates, mid_gain, rsub, rtotal = back_mid(
            None, info, dmid, params[l], gn, rg, gate, states, kept, sub, weights[l]
        )
        revery = lax.all_gather(rtotal, "seq")
        dmixin, dx, gains_b = back_two(
            None, info, x, params[l], dafter, dgpre, dstates, states, kept, rate, cpre, first, sub, rsub, every, revery,
            weights[l],
        )
        grads = [row_product(normed, dmixin), row_product(gated, dmid), row_product(lifted, dboth), row_product(hidden, dlow)]
        grads.append(jnp.stack([gains_b[0], mid_gain[0], ffn_gain[0], gains_b[1]], axis=1))
        sums[l] = [lax.psum_scatter(g.astype(BF16), ALL, scatter_dimension=0, tiled=True).astype(F32) for g in grads]
    outs = [jnp.stack([sums[l][k] for l in range(depth)]) for k in range(5)]
    tail = outs.pop()
    return (mixed, dx, *outs, jnp.swapaxes(tail[:, :, :3], 1, 2), tail[:, :, 3])


def fast_body(stream, w_mix, w_out, w_up, w_down, gains, chan_params, lengths, cotangent):
    rows, width = stream.shape
    depth, share, mix_cols = w_mix.shape
    info = info_of(lengths, rows, True)
    small = small_of(gains, chan_params)
    core = lax.axis_index("seq") % 2
    padding = jnp.zeros((share, 2 * HALVES["mix"] - mix_cols - GROUP), BF16)
    halves = ([], [])
    for l in range(depth):
        mix = jnp.concatenate([w_mix[l], padding, small if l == 0 else jnp.zeros_like(small)], axis=1)
        for h in range(2):
            for w, size in ((mix, HALVES["mix"]), (w_out[l], HALVES["out"]), (w_up[l], HALVES["up"])):
                halves[h].append(w[:, h * size : (h + 1) * size])
    halves = [jnp.concatenate(half, axis=1) for half in halves]
    mine = jnp.where(core == 0, halves[0], halves[1])
    other = swap(jnp.where(core == 0, halves[1], halves[0]), (1, 1))
    units = jnp.where(core == 0, jnp.concatenate([mine, other]), jnp.concatenate([other, mine]))
    joint = HALVES["mix"] + HALVES["out"]
    size = joint + HALVES["up"]
    mos, uds = [], []
    for l in range(depth):
        unit = units[:, l * size : (l + 1) * size]
        stages = LATER if l else STAGES
        mos.append(Spread(unit[:, :joint], stages))
        uds.append(Spread(jnp.concatenate([unit[:, joint:], w_down[l]], axis=1), stages))
    plan = {
        "mix": (0, HALVES["mix"]),
        "out": (HALVES["mix"], HALVES["out"]),
        "small": (HALVES["mix"] - GROUP, GROUP),
        "up": (0, HALVES["up"]),
        "down": (HALVES["up"], width),
    }
    plans = [dict(plan, sources=mo.sources()) for mo in mos]

    order = Order()
    mo, ud = mos[0], uds[0]
    later = [move for l in range(1, depth) for move in (mos[l], uds[l])]
    order.pass_on(ud, mo, *later)
    order.join(ud, mo, *later)
    order.pass_on(mo, ud, *later)
    order.join(mo, ud)
    order.pass_on(mo, ud)
    order.join(mo, *later[:1])
    order.pass_on(mo, *later[:1])
    mo.near_core()
    order.join(ud, *later[1:2])
    if later:
        order.pass_on(*later[1:2])
    order.join(mo, *later[:1])
    mo.end()
    order.pass_on(ud)
    ud.near_core()
    x = stream
    saved = []
    params = None
    for l in range(depth):
        mo, ud, plan = mos[l], uds[l], plans[l]
        more = l + 1 < depth
        order.join(cores=(mo,))
        if l == 0:
            params = table_of(plan, info, mo.arrays(), depth, width)
        (layer,) = order.step(params[l])
        head = front(plan, info, x, layer, mo.arrays())
        (total,) = order.step(head[-1])
        if more:
            order.join(ud, uds[l + 1])
        else:
            order.join(ud)
        ud.end()
        every = exchange(order.step(total)[0])
        (every,) = order.step(every)
        if more:
            order.pass_on(mos[l + 1])
            mos[l + 1].near_core()
        middle = mid(plan, info, x, layer, head[2], head[4], head[5], head[6], order.step(every)[0], mo.arrays())
        middle = (*middle[:-1], *order.step(middle[-1]))
        if more:
            order.join(mos[l + 1], cores=(ud,))
            mos[l + 1].end()
            order.pass_on(uds[l + 1])
            uds[l + 1].near_core()
        else:
            order.join(cores=(ud,))
        if more:
            tail = ffn(plan, info, middle[5], middle[6], ud.arrays(), F32)
            saved.append((x, every, head, middle, tail, layer))
            (x,) = order.step(tail[-1])
    later_stages = UPPER if depth > 1 else (STAGES,) * 3
    keep, send, mixed, hidden, dlow, dafter, dmid, ffn_gain = turn(
        plan, rels_of(later_stages[0]), info, cotangent, layer, middle[5], middle[6], ud.arrays()
    )
    saved.append((x, every, head, middle, (None, hidden, None), layer))
    above = None
    sums = [None] * depth
    extra = ()
    for l in reversed(range(depth)):
        x, every, (normed, cpre, gate, rate, kept, feed, sub, _), middle, (both, hidden, _), layer = saved[l]
        states, first, gn, rg, gated, after, lifted = middle
        plan = plans[l]
        u_stages, od_stages, c_stages = UPPER if l else LOWER
        if above:
            (dx,) = order.step(dx)
            keep, send, dlow, dafter, dmid, ffn_gain = back_ffn(
                plan, info, dx, layer, both, after, uds[l].arrays(), rels_of(u_stages), (lifted,)
            )
        (keep,) = order.step(keep)
        u = Reduce(keep, send, u_stages)
        if above:
            u_up, od_up, c_up = above
            order.join(od_up, c_up, u_up)
            od_up.ready()
            order.pass_on(c_up, u_up)
        (dmid,) = order.step(dmid)
        dgpre, dstates, mid_gain, rsub, rtotal = back_mid(
            plan, info, dmid, layer, gn, rg, gate, states, kept, sub, mos[l].arrays()
        )
        (rtotal,) = order.step(rtotal)
        order.join(u, *((c_up, u_up) if above else ()))
        revery = exchange(rtotal, order)
        waiting = [u] + ([od_up, c_up, u_up] if above else [])
        for move in waiting:
            move.ready()
        (dlow,) = order.step(dlow)
        od = Reduce(
            *grad_od(rels_of(od_stages), info, gated, dmid, hidden, dlow, normed, dgpre), od_stages
        )
        (od.held,) = order.step(od.held)
        (revery,) = order.step(revery)
        order.pass_on(*waiting)
        (dstates,) = order.step(dstates)
        more = (normed,)
        if l == 0:
            more = (normed, mid_gain, ffn_gain, *extra)
        keep, send, dx, gains_b = back_two(
            plan, info, x, layer, dafter, dgpre, dstates, states, kept, rate, cpre, first, sub, rsub, every, revery,
            mos[l].arrays(), rels_of(c_stages), more,
        )
        extra = (gains_b, mid_gain, ffn_gain) + extra
        (keep,) = order.step(keep)
        c = Reduce(keep, send, c_stages)
        order.join(*waiting, od)
        order.pass_on(od, u, *((od_up, c_up) if above else ()))
        above = sums[l] = (u, od, c)
    u, od, c = sums[0]
    others = ()
    if depth > 1:
        u_up, od_up, c_up = sums[1]
        others = (od_up, c_up)
    for moves in ((c,), (od, *others), (u,), (c,), (od,), (u,), (c,), (od,), (c,)):
        order.join(*moves)
        order.pass_on(*moves)
    mine, other, downs = [], [], []
    for u, od, c in reversed(sums):
        ready = od.add()
        line = jnp.concatenate([c.add(), ready[:, : HALVES["out"] + HALVES["gate"]], u.add()], axis=1)
        first, second = line[:share], line[share:]
        mine.insert(0, jnp.where(core == 0, first, second))
        other.insert(0, swap(jnp.where(core == 0, second, first), (1, 1)))
        downs.insert(0, ready)
    shapes = (w_mix.shape, w_out.shape, w_up.shape, w_down.shape)
    *grads, tail = finish(info, mine, other, downs, shapes)
    tail = tail[:, : 4 * depth].T.reshape(depth, 4, share)
    return (mixed, dx, *grads, tail[:, :3], tail[:, 3])


def body(stream, w_mix, *others):
    n_dp, n_seq = lax.axis_size("dp"), lax.axis_size("seq")
    fast = n_seq == 8 and n_dp == 4 and 2 * w_mix.shape[1] == UNIT and w_mix.shape[0] == 2
    return (fast_body if fast else plain_body)(stream, w_mix, *others)


def solution(mesh):
    placed = (
        P(ALL, None),
        P(None, ALL, None),
        P(None, ALL, None),
        P(None, ALL, None),
        P(None, ALL, None),
        P(None, None, ALL),
        P(None, ALL),
        P("dp", None),
        P(ALL, None),
    )
    return jax.shard_map(
        body,
        mesh=mesh,
        in_specs=placed,
        out_specs=(
            P(ALL, None),
            P(ALL, None),
            P(None, ALL, None),
            P(None, ALL, None),
            P(None, ALL, None),
            P(None, ALL, None),
            P(None, None, ALL),
            P(None, ALL),
        ),
        check_vma=False,
    )
```
